32 devices in a mesh: rep: 4 (over x, core), shard: 8 (over z, y).
Axes of the slice: x: 2, y: 2, z: 4, core: 2. Of those that a mesh axis runs over, the one named last changes fastest.
Arguments:
- decoder_states: bfloat16 [32768, 1024], P(('rep', 'shard')), may hold values from -6 to 6
- encoder_states: bfloat16 [8192, 1024], P(('rep', 'shard')), may hold values from -6 to 6
- piece_starts: int32 [32, 2], P(('rep', 'shard')), may hold values from 0 to 768, as said below
- out_cotangent: bfloat16 [32768, 1024], P(('rep', 'shard')), may hold values from -6 to 6
- self_query: bfloat16 [1024, 1024], P('shard'), may hold values from -0.1875 to 0.1875
- self_key: bfloat16 [1024, 1024], P('shard'), may hold values from -0.1875 to 0.1875
- self_value: bfloat16 [1024, 1024], P('shard'), may hold values from -0.1875 to 0.1875
- self_out: bfloat16 [1024, 1024], P('shard'), may hold values from -1 to 1
- cross_query: bfloat16 [1024, 1024], P('shard'), may hold values from -0.1875 to 0.1875
- cross_key: bfloat16 [1024, 1024], P('shard'), may hold values from -0.1875 to 0.1875
- cross_value: bfloat16 [1024, 1024], P('shard'), may hold values from -0.1875 to 0.1875
- cross_out: bfloat16 [1024, 1024], P('shard'), may hold values from -1 to 1
- expand_weight: bfloat16 [1024, 4096], P('shard'), may hold values from -0.1875 to 0.1875
- contract_weight: bfloat16 [4096, 1024], P('shard'), may hold values from -0.125 to 0.125
- self_gain: bfloat16 [1024], P('shard'), may hold values from 0.25 to 1.75
- self_shift: bfloat16 [1024], P('shard'), may hold values from -1.5 to 1.5
- cross_gain: bfloat16 [1024], P('shard'), may hold values from 0.25 to 1.75
- cross_shift: bfloat16 [1024], P('shard'), may hold values from -1.5 to 1.5
- mlp_gain: bfloat16 [1024], P('shard'), may hold values from 0.25 to 1.75
- mlp_shift: bfloat16 [1024], P('shard'), may hold values from -1.5 to 1.5
Outputs:
- layer_out: bfloat16 [32768, 1024], P(('rep', 'shard'))
- grad_decoder: float32 [32768, 1024], P(('rep', 'shard'))
- grad_encoder: float32 [8192, 1024], P(('rep', 'shard'))
- grad_self_query: float32 [1024, 1024], P('shard')
- grad_self_key: float32 [1024, 1024], P('shard')
- grad_self_value: float32 [1024, 1024], P('shard')
- grad_self_out: float32 [1024, 1024], P('shard')
- grad_cross_query: float32 [1024, 1024], P('shard')
- grad_cross_key: float32 [1024, 1024], P('shard')
- grad_cross_value: float32 [1024, 1024], P('shard')
- grad_cross_out: float32 [1024, 1024], P('shard')
- grad_expand: float32 [1024, 4096], P('shard')
- grad_contract: float32 [4096, 1024], P('shard')
- grad_self_gain: float32 [1024], P('shard')
- grad_self_shift: float32 [1024], P('shard')
- grad_cross_gain: float32 [1024], P('shard')
- grad_cross_shift: float32 [1024], P('shard')
- grad_mlp_gain: float32 [1024], P('shard')
- grad_mlp_shift: float32 [1024], P('shard')
The draws below stay inside these ranges and needn't reach their ends.
Inputs may be any that keep to these rules, and one draw needn't show every extreme that they name: `piece_starts`: row s holds the first positions of the 2 picture pieces of sequence s in increasing order; piece p starts within positions p * (512) to (p + 1) * 512 - 256, so pieces lie inside the sequence and never intersect.
All inputs are finite; a program needn't handle non-finite values.
Results may differ from the reference program's by a relative error of at most 0.025.
Values may be sent and summed in bfloat16 or wider, within the bound.
A program may use at most 320 MiB of HBM per device.

```python
import jax
import jax.numpy as jnp
from jax import lax

D = 1024
HD = 64
FF = 4096
SEQ_LEN = 1024
NPIC = 2
PIC = 256
ENC = 256
SEQS = 32
TOKENS = 32768
ENC_ROWS = 8192


def draw_piece_starts(key, part):
    region = SEQ_LEN // NPIC
    offsets = jax.random.randint(key, (SEQS, NPIC), 0, region - PIC + 1)
    starts = jnp.arange(NPIC, dtype=jnp.int32)[None, :] * region + offsets
    chosen = jax.random.randint(jax.random.fold_in(key, 7), (), 0, SEQS)
    rows = jnp.arange(SEQS, dtype=jnp.int32)[:, None]
    columns = jnp.arange(NPIC, dtype=jnp.int32)[None, :]
    starts = jnp.where((rows == chosen) & (columns == 0), 0, starts)
    starts = jnp.where((rows == chosen) & (columns == NPIC - 1), SEQ_LEN - PIC, starts)
    return starts.astype(jnp.int32)


def raised(values, rng, source, target, parts, factor):
    owner, partner = [(jnp.arange(values.shape[dim]) // (values.shape[dim] // parts)).reshape([-1 if axis == dim else 1 for axis in range(values.ndim)]) for dim in (source, target)]
    chosen = jax.random.permutation(rng, parts)[partner]
    strong = (owner == chosen) | (owner == (partner + parts // 2) % parts)
    return jnp.where(strong, factor * values, values)


def level_of(own_key, extent, shards, least, largest):
    level = 1.0
    for dim, shards_of in shards:
        heights = jax.random.uniform(jax.random.fold_in(jax.random.fold_in(own_key, 6), dim), (shards_of,), jnp.float32, least / len(shards), largest / len(shards))
        level = level * jnp.repeat(jnp.exp(heights), extent[dim] // shards_of).reshape((-1,) + (1,) * (len(extent) - 1 - dim))
    return level


def bell_draw(stream_key, shape, scale, bound, shards=(), kind=jnp.bfloat16):
    values = scale * jax.random.normal(stream_key, shape, jnp.float32)
    if shards:
        values = values * level_of(stream_key, shape, shards, -0.22, 0.18)
    return jnp.clip(values, -bound, bound).astype(kind)


def heavy_noise(key, extent, scale, reach, shards, heavy, kind=jnp.bfloat16):
    values = scale * jax.random.normal(key, extent, jnp.float32)
    if shards:
        values = values * level_of(key, extent, shards, -0.22, 0.18)
    return jnp.clip(raised(values, jax.random.fold_in(key, 3), *heavy), -reach, reach).astype(kind)


def setup_inputs(seed: int = 0) -> dict:
    key_list = jax.random.split(jax.random.key(seed), 21)
    decoder_states = heavy_noise(key_list[0], (TOKENS, D), 1.0, 6.0, ((0, 32),), (0, 1, 32, 2.75))
    encoder_states = heavy_noise(key_list[1], (ENC_ROWS, D), 1.0, 6.0, ((0, 32),), (0, 1, 32, 2.75))
    piece_starts = draw_piece_starts(jax.random.fold_in(key_list[20], 71), 0)
    out_cotangent = bell_draw(key_list[3], (TOKENS, D), 1.0, 6.0, ((0, 32),))
    self_query = bell_draw(key_list[4], (D, D), D ** -0.5, 0.1875, ((0, 8),))
    self_key = bell_draw(key_list[5], (D, D), D ** -0.5, 0.1875, ((0, 8),))
    self_value = bell_draw(key_list[6], (D, D), D ** -0.5, 0.1875, ((0, 8),))
    self_out = bell_draw(key_list[7], (D, D), (D // 32) ** -0.5, 1.0, ((0, 8),))
    cross_query = bell_draw(key_list[8], (D, D), D ** -0.5, 0.1875, ((0, 8),))
    cross_key = bell_draw(key_list[9], (D, D), D ** -0.5, 0.1875, ((0, 8),))
    cross_value = bell_draw(key_list[10], (D, D), D ** -0.5, 0.1875, ((0, 8),))
    cross_out = bell_draw(key_list[11], (D, D), (D // 32) ** -0.5, 1.0, ((0, 8),))
    expand_weight = bell_draw(key_list[12], (D, FF), D ** -0.5, 0.1875, ((0, 8),))
    contract_weight = bell_draw(key_list[13], (FF, D), (FF // 2) ** -0.5, 0.125, ((0, 8),))
    self_gain = jnp.clip(1.0 + 0.15 * jax.random.normal(key_list[14], (D,), jnp.float32), 0.25, 1.75).astype(jnp.bfloat16)
    self_shift = bell_draw(key_list[15], (D,), 0.3, 1.5, ((0, 8),))
    cross_gain = jnp.clip(1.0 + 0.15 * jax.random.normal(key_list[16], (D,), jnp.float32), 0.25, 1.75).astype(jnp.bfloat16)
    cross_shift = bell_draw(key_list[17], (D,), 0.3, 1.5, ((0, 8),))
    mlp_gain = jnp.clip(1.0 + 0.15 * jax.random.normal(key_list[18], (D,), jnp.float32), 0.25, 1.75).astype(jnp.bfloat16)
    mlp_shift = bell_draw(key_list[19], (D,), 0.3, 1.5, ((0, 8),))
    return dict(decoder_states=decoder_states, encoder_states=encoder_states, piece_starts=piece_starts, out_cotangent=out_cotangent, self_query=self_query, self_key=self_key, self_value=self_value, self_out=self_out, cross_query=cross_query, cross_key=cross_key, cross_value=cross_value, cross_out=cross_out, expand_weight=expand_weight, contract_weight=contract_weight, self_gain=self_gain, self_shift=self_shift, cross_gain=cross_gain, cross_shift=cross_shift, mlp_gain=mlp_gain, mlp_shift=mlp_shift)


EPS = 1e-05
HIGH = lax.Precision.HIGHEST

@jax.custom_vjp
def low(v):
    return lax.optimization_barrier(v.astype(jnp.bfloat16)).astype(jnp.float32)

@jax.custom_vjp
def low_back(v):
    return v

def low_keep(v):
    return (low(v), None)

def low_pass(kept, grad):
    return (grad,)

def back_keep(v):
    return (v, None)

def back_low(kept, grad):
    return (low(grad),)
low.defvjp(low_keep, low_pass)
low_back.defvjp(back_keep, back_low)

def product(left, right):
    return jnp.dot(left, right, precision=HIGH)

def layer_norm(resid, gain, shift):
    mean = lax.optimization_barrier(jnp.mean(resid, -1, keepdims=True))
    centred = resid - mean
    variance = lax.optimization_barrier(jnp.mean(centred * centred, -1, keepdims=True))
    return centred * lax.rsqrt(variance + EPS) * gain + shift

def attention(queries, keys, values, allowed):
    rows = queries.shape[0]
    q_heads = queries.reshape(rows, -1, HD)
    k_heads = keys.reshape(keys.shape[0], -1, HD)
    v_heads = values.reshape(values.shape[0], -1, HD)
    scores = low_back(jnp.einsum('qhd,khd->hqk', q_heads, k_heads, precision=HIGH))
    scores = jnp.where(allowed[None], scores, -1e+30)
    probs = jax.nn.softmax(scores, axis=-1)
    mixed = jnp.einsum('hqk,khd->qhd', low(probs), v_heads, precision=HIGH)
    return mixed.reshape(rows, -1)

def forward(starts_row, states, encoded, w_sq, w_sk, w_sv, w_so, w_cq, w_ck, w_cv, w_co, w_up, w_down, gain_one, shift_one, gain_two, shift_two, gain_three, shift_three):
    rows = states.shape[0]
    scale = HD ** (-0.5)
    positions = jnp.arange(rows, dtype=jnp.int32)
    inside = ((positions[:, None] >= starts_row[None, :]) & (positions[:, None] < starts_row[None, :] + PIC)).astype(jnp.float32)
    same_piece = product(inside, inside.T) > 0.5
    allowed = (positions[None, :] <= positions[:, None]) | same_piece
    query_self = low_back(low(product(states, w_sq) * scale))
    key_self = low_back(low(product(states, w_sk)))
    value_self = low_back(low(product(states, w_sv)))
    mixed_self = low_back(low(attention(query_self, key_self, value_self, allowed)))
    resid_one = states + low_back(product(mixed_self, w_so))
    hidden_one = layer_norm(resid_one, gain_one, shift_one)
    hidden_one_low = low(hidden_one)
    query_cross = low_back(low(product(hidden_one_low, w_cq) * scale))
    key_cross = low_back(low(product(encoded, w_ck)))
    value_cross = low_back(low(product(encoded, w_cv)))
    everything = jnp.ones((rows, encoded.shape[0]), dtype=bool)
    mixed_cross = low_back(low(attention(query_cross, key_cross, value_cross, everything)))
    resid_two = hidden_one + low_back(product(mixed_cross, w_co))
    hidden_two = layer_norm(resid_two, gain_two, shift_two)
    hidden_two_low = low(hidden_two)
    pre_act = low_back(product(hidden_two_low, w_up))
    active = low(jax.nn.gelu(pre_act, approximate=False))
    resid_three = hidden_two + low_back(product(active, w_down))
    return layer_norm(resid_three, gain_three, shift_three)

def reference(decoder_states, encoder_states, piece_starts, out_cotangent, self_query, self_key, self_value, self_out, cross_query, cross_key, cross_value, cross_out, expand_weight, contract_weight, self_gain, self_shift, cross_gain, cross_shift, mlp_gain, mlp_shift):
    weights = (self_query, self_key, self_value, self_out, cross_query, cross_key, cross_value, cross_out, expand_weight, contract_weight, self_gain, self_shift, cross_gain, cross_shift, mlp_gain, mlp_shift)
    weights = tuple((w.astype(jnp.float32) for w in weights))
    states_all = decoder_states.astype(jnp.float32).reshape(SEQS, SEQ_LEN, D)
    encoded_all = encoder_states.astype(jnp.float32).reshape(SEQS, ENC, D)
    cotangents = out_cotangent.astype(jnp.float32).reshape(SEQS, SEQ_LEN, D)

    def step(totals, item):
        states, encoded, starts_row, cotangent = item

        def run(states_in, encoded_in, *params):
            return forward(starts_row, states_in, encoded_in, *params)
        result, pull = jax.vjp(run, states, encoded, *weights)
        grads = pull(cotangent)
        updated = tuple((t + g for t, g in zip(totals, grads[2:])))
        return (updated, (result.astype(jnp.bfloat16), grads[0], grads[1]))
    zeros = tuple((jnp.zeros_like(w) for w in weights))
    totals, (results, grad_states, grad_encoded) = lax.scan(step, zeros, (states_all, encoded_all, piece_starts, cotangents))
    return (results.reshape(TOKENS, D), grad_states.reshape(TOKENS, D), grad_encoded.reshape(ENC_ROWS, D), totals[0], totals[1], totals[2], totals[3], totals[4], totals[5], totals[6], totals[7], totals[8], totals[9], totals[10], totals[11], totals[12], totals[13], totals[14], totals[15])
```

```python
import functools

import jax
import jax.numpy as jnp
from jax import lax
from jax.experimental import pallas as pl
from jax.experimental.pallas import tpu as pltpu
from jax.sharding import PartitionSpec as P

HD = 64
PIC = 256
EPS = 1e-05
NEGATIVE = -1e30
INV_ROOT_TWO = 0.7071067811865476
INV_ROOT_TWO_PI = 0.3989422804014327
MESH = pl.DeviceIdType.MESH
MIB = 1 << 20
HBM = pl.BlockSpec(memory_space=pltpu.HBM)
bf16 = jnp.bfloat16
f32 = jnp.float32


def dot(a, b, ca=1, cb=0):
    return lax.dot_general(a, b, (((ca,), (cb,)), ((), ())), preferred_element_type=f32)


def place(n):
    half = n // 2

    def shard_at(pos):
        pos = lax.rem(pos + 2 * n, n)
        back = pos // half
        return (1 - back) * 2 * pos + back * (2 * (n - 1 - pos) + 1)

    s = lax.axis_index("shard")
    odd = s % 2
    pos = (1 - odd) * (s // 2) + odd * (n - 1 - s // 2)
    return pos, shard_at


def greet(partners):
    barrier = pltpu.get_barrier_semaphore()
    for who in partners:
        pl.semaphore_signal(barrier, inc=1, device_id=who, device_id_type=MESH)
    pl.semaphore_wait(barrier, len(partners))


def send(src, dst, ssem, rsem, who):
    copy = pltpu.make_async_remote_copy(
        src_ref=src, dst_ref=dst, send_sem=ssem, recv_sem=rsem, device_id=who, device_id_type=MESH
    )
    copy.start()
    return copy


def load(src, dst, sem):
    copy = pltpu.make_async_copy(src, dst, sem)
    copy.start()
    return copy


def gather_kernel(n, ne, ns, rows, stack, vec, full, vecs, local, rs, rr, cs, cr, xs, xr, fs, fr, vs, vr):
    rep, shard = lax.axis_index("rep"), lax.axis_index("shard")
    x, c = rep // 2, rep % 2
    pos, shard_at = place(n)
    ways = (((rep, shard_at(pos + 1)), 1), ((rep, shard_at(pos - 1)), -1))
    sibling, across = (x * 2 + 1 - c, shard), ((1 - x) * 2 + c, shard)
    width = stack.shape[-1] // 4
    ring = pl.ds(x * ne, ne + ns)
    mine = pl.ds(x * (ne + ns), ne)
    theirs = pl.ds((1 - x) * (ne + ns), ne)

    def spot(units, owner, d):
        cols = pl.multiple_of(c * 2 * width + d * width, width)
        return full.at[units, pl.ds(pl.multiple_of(owner * rows, rows), rows), pl.ds(cols, width)]

    own = load(stack, full.at[:, pl.ds(pl.multiple_of(shard * rows, rows), rows), :], local.at[0])
    own_vec = load(vec, vecs.at[shard], local.at[1])
    greet((ways[0][0], ways[1][0], sibling, across))
    own.wait()
    own_vec.wait()
    on_ring, crossing, beside, forwarded, vec_sent = {}, {}, {}, {}, {}

    def forward(k):
        for d, (_, sign) in enumerate(ways):
            here = spot(theirs, shard_at(pos - sign * k), d)
            crossing[d, k].wait_recv()
            forwarded[d, k] = send(here, here, fs.at[d, k - 1], fr.at[d, k - 1], sibling)

    for k in range(n):
        for d, (who, sign) in enumerate(ways):
            owner = shard_at(pos - sign * k)
            here = spot(ring, owner, d)
            if k:
                on_ring[d, k - 1].wait_recv()
            if k < n - 1:
                on_ring[d, k] = send(here, here, rs.at[d, k], rr.at[d, k], who)
            if k:
                part = spot(mine, owner, d)
                crossing[d, k] = send(part, part, xs.at[d, k - 1], xr.at[d, k - 1], across)
                beside[d, k] = send(here, here, cs.at[d, k - 1], cr.at[d, k - 1], sibling)
        if k:
            vec_sent[k - 1].wait_recv()
        if k < n - 1:
            owner = shard_at(pos - k)
            vec_sent[k] = send(vecs.at[owner], vecs.at[owner], vs.at[k], vr.at[k], ways[0][0])
        if k >= 2:
            forward(k - 1)
    forward(n - 1)
    for copy in beside.values():
        copy.wait_recv()
    for copy in forwarded.values():
        copy.wait_recv()
    for group in (on_ring, crossing, beside, forwarded, vec_sent):
        for copy in group.values():
            copy.wait_send()


def gather(stack, vec, n, ne, ns):
    units, rows, width = stack.shape
    hops = pltpu.SemaphoreType.DMA((2, n - 1))
    return pl.pallas_call(
        functools.partial(gather_kernel, n, ne, ns, rows),
        out_shape=(
            jax.ShapeDtypeStruct((units, n * rows, width), stack.dtype),
            jax.ShapeDtypeStruct((n,) + vec.shape, vec.dtype),
        ),
        in_specs=[HBM, HBM],
        out_specs=[HBM, HBM],
        scratch_shapes=[pltpu.SemaphoreType.DMA((2,))]
        + [hops] * 8
        + [pltpu.SemaphoreType.DMA((n - 1,))] * 2,
        compiler_params=pltpu.CompilerParams(collective_id=0, has_side_effects=True, vmem_limit_bytes=16 * MIB),
        name="gather_weights",
    )(stack, vec)


def scatter_kernel(
    n, ne, ns, rows, grads, out, near, beside, cross, ring, swap_s, swap_e,
    local, cs, cr, xs, xr, rs, rr, ss, sr, os, orr, done,
):
    rep, shard = lax.axis_index("rep"), lax.axis_index("shard")
    x, c = rep // 2, rep % 2
    pos, shard_at = place(n)
    ways = (((rep, shard_at(pos + 1)), 1), ((rep, shard_at(pos - 1)), -1))
    sibling, across = (x * 2 + 1 - c, shard), ((1 - x) * 2 + c, shard)
    units = grads.shape[0]
    width = grads.shape[-1] // 4
    on_ring = ne + ns
    owners = {(d, k): shard_at(pos - sign * (1 + k)) for d, (_, sign) in enumerate(ways) for k in range(n)}

    def rows_of(owner):
        return pl.ds(pl.multiple_of(owner * rows, rows), rows)

    def cols(d):
        return pl.ds(d * width, width)

    loads, sides, crossing, hops = {}, {}, {}, {}
    for k in range(n):
        for d in range(2):
            at = rows_of(owners[d, k])
            half = pl.multiple_of(c * 2 * width + d * width, width)
            loads[d, k] = load(grads.at[:, at, pl.ds(half, width)], near.at[:, at, cols(d)], local.at[d, k])
    greet((ways[0][0], ways[1][0], sibling, across))
    for k in range(n):
        for d in range(2):
            at = rows_of(owners[d, k])
            half = pl.multiple_of((1 - c) * 2 * width + d * width, width)
            sides[d, k] = send(
                grads.at[:, at, pl.ds(half, width)], beside.at[:, at, cols(d)], cs.at[d, k], cr.at[d, k], sibling
            )

    def pair(k):
        for d in range(2):
            at = rows_of(owners[d, k])
            loads[d, k].wait()
            sides[d, k].wait_recv()

            def add(u, _):
                near[u, at, cols(d)] = (
                    near[u, at, cols(d)].astype(f32) + beside[u, at, cols(d)].astype(f32)
                ).astype(bf16)
                return 0

            lax.fori_loop(0, units, add, 0)
            theirs = pl.ds((1 - x) * on_ring, ne)
            crossing[d, k] = send(
                near.at[theirs, at, cols(d)], cross.at[:, at, cols(d)], xs.at[d, k], xr.at[d, k], across
            )

    def hop(k):
        for d, (who, _) in enumerate(ways):
            at = rows_of(owners[d, k])
            if k:
                hops[d, k - 1].wait_recv()

            def add_shared(i, _):
                u = ne + i
                value = near[u, at, cols(d)].astype(f32) + ring[d, k - 1, (1 - x) * ne + i].astype(f32)
                near[u, at, cols(d)] = value.astype(bf16)
                return 0

            if k:
                lax.fori_loop(0, ns, add_shared, 0)
            crossing[d, k].wait_recv()

            def add_mine(i, _):
                u = x * on_ring + i
                value = near[u, at, cols(d)].astype(f32) + cross[i, at, cols(d)].astype(f32)
                if k:
                    value = value + ring[d, k - 1, x * ns + i].astype(f32)
                near[u, at, cols(d)] = value.astype(bf16)
                return 0

            lax.fori_loop(0, ne, add_mine, 0)
            if k < n - 1:
                hops[d, k] = send(near.at[pl.ds(x * ne, on_ring), at, cols(d)], ring.at[d, k], rs.at[d, k], rr.at[d, k], who)

    pair(0)
    pair(1)
    for k in range(n):
        if k + 2 < n:
            pair(k + 2)
        hop(k)
    at = rows_of(shard)
    shared = pl.ds(ne, ns)
    mine = pl.ds(x * on_ring, ne)
    theirs = pl.ds((1 - x) * on_ring, ne)
    half = pl.ds(pl.multiple_of(c * 2 * width, 2 * width), 2 * width)
    swap = send(near.at[shared, at, :], swap_s, ss.at[0], sr.at[0], across)
    give = send(near.at[mine, at, :], swap_e, ss.at[1], sr.at[1], across)
    final = [send(near.at[mine, at, :], out.at[mine, :, half], os.at[0], orr.at[0], sibling)]
    keep = [load(near.at[mine, at, :], out.at[mine, :, half], done.at[0])]
    swap.wait_recv()

    def join(i, _):
        swap_s[i] = (swap_s[i].astype(f32) + near[ne + i, at, :].astype(f32)).astype(bf16)
        return 0

    lax.fori_loop(0, ns, join, 0)
    final.append(send(swap_s, out.at[shared, :, half], os.at[1], orr.at[1], sibling))
    keep.append(load(swap_s, out.at[shared, :, half], done.at[1]))
    give.wait_recv()
    final.append(send(swap_e, out.at[theirs, :, half], os.at[2], orr.at[2], sibling))
    keep.append(load(swap_e, out.at[theirs, :, half], done.at[2]))
    for copy in keep:
        copy.wait()
    for copy in final:
        copy.wait_recv()
    for copy in [*sides.values(), *crossing.values(), *hops.values(), swap, give, *final]:
        copy.wait_send()


def scatter(grads, n, ne, ns, collective_id):
    units, total, width = grads.shape
    rows = total // n
    dma = pltpu.SemaphoreType.DMA
    return pl.pallas_call(
        functools.partial(scatter_kernel, n, ne, ns, rows),
        out_shape=jax.ShapeDtypeStruct((units, rows, width), bf16),
        in_specs=[HBM],
        out_specs=HBM,
        scratch_shapes=[
            pltpu.VMEM((units, total, width // 2), bf16),
            pltpu.VMEM((units, total, width // 2), bf16),
            pltpu.VMEM((ne, total, width // 2), bf16),
            pltpu.VMEM((2, n - 1, ne + ns, rows, width // 4), bf16),
            pltpu.VMEM((ns, rows, width // 2), bf16),
            pltpu.VMEM((ne, rows, width // 2), bf16),
            dma((2, n)), dma((2, n)), dma((2, n)), dma((2, n)), dma((2, n)),
            dma((2, n - 1)), dma((2, n - 1)), dma((2,)), dma((2,)), dma((3,)), dma((3,)), dma((3,)),
        ],
        compiler_params=pltpu.CompilerParams(
            collective_id=collective_id, has_side_effects=True, vmem_limit_bytes=56 * MIB
        ),
        name="scatter_grads",
    )(grads)


def first_lanes(shape):
    return lax.broadcasted_iota(jnp.int32, shape, len(shape) - 1) < HD


def region_bias(starts_ref, region, size, transposed):
    first = region * size
    one = first + lax.broadcasted_iota(jnp.int32, (size, size), 0)
    two = first + lax.broadcasted_iota(jnp.int32, (size, size), 1)
    q_at, k_at = (two, one) if transposed else (one, two)
    start = starts_ref[0, region]
    q_in = (q_at >= start) & (q_at < start + PIC)
    k_in = (k_at >= start) & (k_at < start + PIC)
    return jnp.where((k_at <= q_at) | (q_in & k_in), 0.0, NEGATIVE)


def attend_forward_kernel(regions, starts_ref, q_ref, k_ref, v_ref, o_ref, lse_ref, bias_ref):
    rows = q_ref.shape[0]
    size = rows // regions

    if starts_ref is not None:
        @pl.when(pl.program_id(0) == 0)
        def _():
            for r in range(regions):
                bias_ref[r] = region_bias(starts_ref, r, size, False)

    low = first_lanes((1, 2 * HD))
    outs, lses = [[], []], [[], []]
    for h in range(2):
        pick = low if h == 0 else ~low
        keys = jnp.where(pick, k_ref[...], jnp.zeros((), bf16))
        for r in range(regions):
            span = slice(r * size, (r + 1) * size)
            q = q_ref[span, :]
            scores = []
            if starts_ref is None:
                scores.append((dot(q, keys, 1, 1), v_ref[...]))
            else:
                if r:
                    scores.append((dot(q, keys[: r * size], 1, 1), v_ref[: r * size, :]))
                scores.append((dot(q, keys[span], 1, 1) + bias_ref[r], v_ref[span, :]))
            top = functools.reduce(jnp.maximum, [jnp.max(s, -1, keepdims=True) for s, _ in scores])
            total, mixed = 0.0, 0.0
            for s, v in scores:
                e = jnp.exp(s - top)
                total = total + jnp.sum(e, -1, keepdims=True)
                mixed = mixed + dot(e.astype(bf16), v)
            outs[h].append(mixed / total)
            lses[h].append(top + jnp.log(total))
    for r in range(regions):
        span = slice(r * size, (r + 1) * size)
        o_ref[span, :] = jnp.where(low, outs[0][r], outs[1][r]).astype(bf16)
        turned = jnp.where(low, lses[0][r], lses[1][r]).T
        lse_ref[0, 0:1, span] = turned[0:1]
        lse_ref[0, 1:2, span] = turned[HD : HD + 1]


def attend_forward(q, k, v, starts):
    rows, width = q.shape
    regions = 1 if starts is None else starts.shape[1]
    pairs = width // (2 * HD)
    tall = lambda a: pl.BlockSpec((a.shape[0], 2 * HD), lambda i: (0, i))
    specs = [tall(q), tall(k), tall(v)]
    args = [q, k, v]
    if starts is None:
        kernel = lambda *refs: attend_forward_kernel(2, None, *refs, None)
        scratch = []
    else:
        kernel = functools.partial(attend_forward_kernel, regions)
        specs = [pl.BlockSpec(memory_space=pltpu.SMEM)] + specs
        args = [starts] + args
        scratch = [pltpu.VMEM((regions, rows // regions, rows // regions), f32)]
    return pl.pallas_call(
        kernel,
        grid=(pairs,),
        out_shape=(jax.ShapeDtypeStruct((rows, width), bf16), jax.ShapeDtypeStruct((pairs, 8, rows), f32)),
        in_specs=specs,
        out_specs=[tall(q), pl.BlockSpec((1, 8, rows), lambda i: (i, 0, 0))],
        scratch_shapes=scratch,
        compiler_params=pltpu.CompilerParams(vmem_limit_bytes=48 * MIB),
        name="self_forward" if starts is not None else "cross_forward",
    )(*args)


def attend_backward_kernel(
    regions, starts_ref, q_ref, k_ref, v_ref, g_ref, o_ref, lse_ref, gq_ref, gk_ref, gv_ref, bias_ref
):
    rows = q_ref.shape[0]
    size = rows // regions

    if starts_ref is not None:
        @pl.when(pl.program_id(0) == 0)
        def _():
            for r in range(regions):
                bias_ref[r] = region_bias(starts_ref, r, size, True)

    low = first_lanes((1, 2 * HD))
    product = g_ref[...].astype(f32) * o_ref[...].astype(f32)
    chooser = lax.broadcasted_iota(jnp.int32, (8, 2 * HD), 0)
    chooser = ((chooser == 0) & first_lanes((8, 2 * HD))) | ((chooser == 1) & ~first_lanes((8, 2 * HD)))
    chooser = chooser.astype(f32).astype(bf16)
    upper = product.astype(bf16)
    lower = (product - upper.astype(f32)).astype(bf16)
    deltas = dot(chooser, upper, 1, 1) + dot(chooser, lower, 1, 1)
    gq, gk, gv = {}, {}, {}
    key_spans = [slice(0, k_ref.shape[0])]
    if starts_ref is not None:
        key_spans = [slice(r * size, (r + 1) * size) for r in range(regions)]
    for h in range(2):
        pick = low if h == 0 else ~low
        zero = jnp.zeros((), bf16)
        keys = jnp.where(pick, k_ref[...], zero)
        values = jnp.where(pick, v_ref[...], zero)
        for r in range(regions):
            span = slice(r * size, (r + 1) * size)
            q, g = q_ref[span, :], g_ref[span, :]
            lse = lse_ref[0, h : h + 1, span]
            delta = deltas[h : h + 1, span]
            for j, keyed in enumerate(key_spans):
                if starts_ref is not None and j > r:
                    continue
                scores = dot(keys[keyed], q, 1, 1)
                if starts_ref is not None and j == r:
                    scores = scores + bias_ref[r]
                probs = jnp.exp(scores - lse)
                grad_probs = dot(values[keyed], g, 1, 1)
                grad_scores = (probs * (grad_probs - delta)).astype(bf16)
                gv[h, j] = gv.get((h, j), 0.0) + dot(probs.astype(bf16), g)
                gk[h, j] = gk.get((h, j), 0.0) + dot(grad_scores, q)
                gq[h, r] = gq.get((h, r), 0.0) + dot(grad_scores, k_ref[keyed, :], 0, 0)
    for r in range(regions):
        span = slice(r * size, (r + 1) * size)
        gq_ref[span, :] = jnp.where(low, gq[0, r], gq[1, r]).astype(bf16)
    for j, keyed in enumerate(key_spans):
        gk_ref[keyed, :] = jnp.where(low, gk[0, j], gk[1, j]).astype(bf16)
        gv_ref[keyed, :] = jnp.where(low, gv[0, j], gv[1, j]).astype(bf16)


def attend_backward(q, k, v, g, o, lse, starts):
    rows, width = q.shape
    regions = 1 if starts is None else starts.shape[1]
    pairs = width // (2 * HD)
    tall = lambda a: pl.BlockSpec((a.shape[0], 2 * HD), lambda i: (0, i))
    specs = [tall(a) for a in (q, k, v, g, o)] + [pl.BlockSpec((1, 8, rows), lambda i: (i, 0, 0))]
    args = [q, k, v, g, o, lse]
    if starts is None:
        kernel = lambda *refs: attend_backward_kernel(2, None, *refs, None)
        scratch = []
    else:
        kernel = functools.partial(attend_backward_kernel, regions)
        specs = [pl.BlockSpec(memory_space=pltpu.SMEM)] + specs
        args = [starts] + args
        scratch = [pltpu.VMEM((regions, rows // regions, rows // regions), f32)]
    like = lambda a: jax.ShapeDtypeStruct(a.shape, bf16)
    return pl.pallas_call(
        kernel,
        grid=(pairs,),
        out_shape=(like(q), like(k), like(v)),
        in_specs=specs,
        out_specs=[tall(q), tall(k), tall(v)],
        scratch_shapes=scratch,
        compiler_params=pltpu.CompilerParams(vmem_limit_bytes=48 * MIB),
        name="self_backward" if starts is not None else "cross_backward",
    )(*args)


def norm_forward(resid, gain, shift):
    mean = jnp.mean(resid, -1, keepdims=True)
    centred = resid - mean
    variance = jnp.mean(centred * centred, -1, keepdims=True)
    inverse = lax.rsqrt(variance + EPS)
    normed = centred * inverse
    return (normed * gain + shift, normed, inverse)


def norm_backward(grad_out, normed, inverse, gain):
    grad_gain = jnp.sum(grad_out * normed, 0)
    grad_shift = jnp.sum(grad_out, 0)
    grad_normed = grad_out * gain
    centre_term = jnp.mean(grad_normed, -1, keepdims=True)
    slope_term = jnp.mean(grad_normed * normed, -1, keepdims=True)
    return (inverse * (grad_normed - centre_term - normed * slope_term), grad_gain, grad_shift)


def body(n, states, encoded, starts, cotangent, *weights):
    matrices, vectors = weights[:10], weights[10:]
    expand, contract = matrices[8], matrices[9]
    rows, width = matrices[0].shape
    blocks = contract.shape[0] // rows
    scale = HD ** (-0.5)
    small = n <= 16
    stack = jnp.concatenate(
        [
            jnp.stack(matrices[:8]),
            expand.reshape(rows, n, blocks, rows).transpose(2, 0, 1, 3).reshape(blocks, rows, width),
            contract.reshape(blocks, rows, width),
        ]
    )
    vec = jnp.zeros((16, max(rows, 128)), bf16).at[: len(vectors), :rows].set(jnp.stack(vectors))
    if small:
        full, vecs = gather(stack, vec, n, 5, 6)
    else:
        full = lax.all_gather(stack, "shard", axis=1, tiled=True)
        vecs = lax.all_gather(vec, "shard", axis=0)
    vecs = vecs[:, : len(vectors), :rows].transpose(1, 0, 2).reshape(len(vectors), width).astype(f32)
    w_sq, w_sk, w_sv, w_so, w_cq, w_ck, w_cv, w_co = [full[i] for i in range(8)]
    gain_one, shift_one, gain_two, shift_two, gain_three, shift_three = vecs

    wide = states.astype(f32)
    q_self = (dot(states, w_sq) * scale).astype(bf16)
    k_self = dot(states, w_sk).astype(bf16)
    v_self = dot(states, w_sv).astype(bf16)
    k_cross = dot(encoded, w_ck).astype(bf16)
    v_cross = dot(encoded, w_cv).astype(bf16)
    mixed_self, lse_self = attend_forward(q_self, k_self, v_self, starts)
    hidden_one, normed_one, inverse_one = norm_forward(wide + dot(mixed_self, w_so), gain_one, shift_one)
    one_low = hidden_one.astype(bf16)
    q_cross = (dot(one_low, w_cq) * scale).astype(bf16)
    mixed_cross, lse_cross = attend_forward(q_cross, k_cross, v_cross, None)
    hidden_two, normed_two, inverse_two = norm_forward(hidden_one + dot(mixed_cross, w_co), gain_two, shift_two)
    two_low = hidden_two.astype(bf16)
    active, slopes = [], []
    resid_three = hidden_two
    for j in range(blocks):
        pre = dot(two_low, full[8 + j])
        phi = 0.5 * (1.0 + lax.erf(pre * INV_ROOT_TWO))
        active.append((pre * phi).astype(bf16))
        slopes.append((phi + pre * jnp.exp(-0.5 * pre * pre) * INV_ROOT_TWO_PI).astype(bf16))
        resid_three = resid_three + dot(active[j], full[8 + blocks + j])
    final, normed_three, inverse_three = norm_forward(resid_three, gain_three, shift_three)

    grad_three, g_gain_three, g_shift_three = norm_backward(cotangent.astype(f32), normed_three, inverse_three, gain_three)
    branch_three = grad_three.astype(bf16)
    grad_two = grad_three
    g_expand, g_contract = [], []
    for j in range(blocks):
        g_contract.append(dot(active[j], branch_three, 0, 0).astype(bf16))
        g_pre = (dot(branch_three, full[8 + blocks + j], 1, 1) * slopes[j]).astype(bf16)
        g_expand.append(dot(two_low, g_pre, 0, 0).astype(bf16))
        grad_two = grad_two + dot(g_pre, full[8 + j], 1, 1)
    grad_resid_two, g_gain_two, g_shift_two = norm_backward(grad_two, normed_two, inverse_two, gain_two)
    branch_two = grad_resid_two.astype(bf16)
    g_cross_out = dot(mixed_cross, branch_two, 0, 0)
    grad_mixed = dot(branch_two, w_co, 1, 1).astype(bf16)
    g_q, g_k, g_v = attend_backward(q_cross, k_cross, v_cross, grad_mixed, mixed_cross, lse_cross, None)
    g_q = g_q * scale
    g_cross_query = dot(one_low, g_q, 0, 0)
    g_cross_key = dot(encoded, g_k, 0, 0)
    g_cross_value = dot(encoded, g_v, 0, 0)
    grad_encoded = dot(g_k, w_ck, 1, 1) + dot(g_v, w_cv, 1, 1)
    grad_one = grad_resid_two + dot(g_q, w_cq, 1, 1)
    grad_resid_one, g_gain_one, g_shift_one = norm_backward(grad_one, normed_one, inverse_one, gain_one)
    branch_one = grad_resid_one.astype(bf16)
    g_self_out = dot(mixed_self, branch_one, 0, 0)
    grad_mixed = dot(branch_one, w_so, 1, 1).astype(bf16)
    g_q, g_k, g_v = attend_backward(q_self, k_self, v_self, grad_mixed, mixed_self, lse_self, starts)
    g_q = g_q * scale
    g_self_query = dot(states, g_q, 0, 0)
    g_self_key = dot(states, g_k, 0, 0)
    g_self_value = dot(states, g_v, 0, 0)
    grad_states = grad_resid_one + dot(g_q, w_sq, 1, 1) + dot(g_k, w_sk, 1, 1) + dot(g_v, w_sv, 1, 1)

    grads_ff = jnp.stack(g_expand + g_contract)
    grads_at = jnp.stack(
        [
            g.astype(bf16)
            for g in (
                g_self_query, g_self_key, g_self_value, g_self_out,
                g_cross_query, g_cross_key, g_cross_value, g_cross_out,
            )
        ]
    )
    grads_vec = jnp.stack([g_gain_one, g_shift_one, g_gain_two, g_shift_two, g_gain_three, g_shift_three])
    if small:
        own_ff = scatter(grads_ff, n, 2, 4, 1)
        own_at = scatter(grads_at, n, 2, 4, 2)
    else:
        total = lambda g: lax.psum(lax.psum_scatter(g, "shard", scatter_dimension=1, tiled=True), "rep")
        own_ff, own_at = total(grads_ff), total(grads_at)
    grads_vec = lax.psum(grads_vec, ("rep", "shard"))
    own_vec = lax.dynamic_slice_in_dim(grads_vec, lax.axis_index("shard") * rows, rows, 1)
    own_at = own_at.astype(f32)
    own_expand = own_ff[:blocks].reshape(blocks, rows, n, rows).transpose(1, 2, 0, 3).reshape(rows, blocks * width)
    own_contract = own_ff[blocks:].reshape(blocks * rows, width)
    return (
        final.astype(bf16),
        grad_states,
        grad_encoded,
        *[own_at[i] for i in range(8)],
        own_expand.astype(f32),
        own_contract.astype(f32),
        *[own_vec[i] for i in range(6)],
    )


def solution(mesh):
    many, few = P(("rep", "shard"), None), P("shard", None)
    return jax.shard_map(
        functools.partial(body, mesh.shape["shard"]),
        mesh=mesh,
        in_specs=(many,) * 4 + (few,) * 10 + (P("shard"),) * 6,
        out_specs=(many,) * 3 + (few,) * 10 + (P("shard"),) * 6,
        check_vma=False,
    )
```

```python
import functools

import jax
import jax.numpy as jnp
from jax import lax
from jax.experimental import pallas as pl
from jax.experimental.pallas import tpu as pltpu
from jax.sharding import PartitionSpec as P

HD = 64
PIC = 256
EPS = 1e-05
NEGATIVE = -1e30
INV_ROOT_TWO = 0.7071067811865476
INV_ROOT_TWO_PI = 0.3989422804014327
MESH = pl.DeviceIdType.MESH
MIB = 1 << 20
HBM = pl.BlockSpec(memory_space=pltpu.HBM)
bf16 = jnp.bfloat16
f32 = jnp.float32


def dot(a, b, ca=1, cb=0):
    return lax.dot_general(a, b, (((ca,), (cb,)), ((), ())), preferred_element_type=f32)


def place(n):
    half = n // 2

    def shard_at(pos):
        pos = lax.rem(pos + 2 * n, n)
        back = pos // half
        return (1 - back) * 2 * pos + back * (2 * (n - 1 - pos) + 1)

    s = lax.axis_index("shard")
    odd = s % 2
    pos = (1 - odd) * (s // 2) + odd * (n - 1 - s // 2)
    return pos, shard_at


def greet(partners):
    barrier = pltpu.get_barrier_semaphore()
    for who in partners:
        pl.semaphore_signal(barrier, inc=1, device_id=who, device_id_type=MESH)
    pl.semaphore_wait(barrier, len(partners))


def send(src, dst, ssem, rsem, who):
    copy = pltpu.make_async_remote_copy(
        src_ref=src, dst_ref=dst, send_sem=ssem, recv_sem=rsem, device_id=who, device_id_type=MESH
    )
    copy.start()
    return copy


def load(src, dst, sem):
    copy = pltpu.make_async_copy(src, dst, sem)
    copy.start()
    return copy


def neighbours(n):
    rep, shard = lax.axis_index("rep"), lax.axis_index("shard")
    x, c = rep // 2, rep % 2
    pos, shard_at = place(n)
    ways = (((rep, shard_at(pos + 1)), 1), ((rep, shard_at(pos - 1)), -1))
    sibling, across, corner = (x * 2 + 1 - c, shard), ((1 - x) * 2 + c, shard), ((1 - x) * 2 + 1 - c, shard)
    return x, c, shard, pos, shard_at, ways, sibling, across, corner


def remote(src, dst, ssem, rsem, who):
    return pltpu.make_async_remote_copy(
        src_ref=src, dst_ref=dst, send_sem=ssem, recv_sem=rsem, device_id=who, device_id_type=MESH
    )


def block_of(index, size):
    return pl.ds(pl.multiple_of(index * size, size), size)


class Gather:
    def __init__(self, n, width, shards, units, alone, owner_first=False, vec=None):
        self.n, self.shards, self.owner_first, self.vec = n, shards, owner_first, vec
        self.units, self.ne, self.ns = units, alone, units - 2 * alone
        self.rows, self.width = sum(s.size for s in shards) // (units * width), width
        self.arrays = list(shards) + ([] if vec is None else [vec])
        shape = (n, units, self.rows, self.width) if owner_first else (units, n * self.rows, self.width)
        self.out_shapes = [jax.ShapeDtypeStruct(shape, bf16)]
        dma = pltpu.SemaphoreType.DMA
        self.scratch = [pltpu.VMEM((units, self.rows, width), bf16), dma((2,))] + [dma((2, n - 1))] * 12
        if vec is not None:
            self.out_shapes.append(jax.ShapeDtypeStruct((n,) + vec.shape, vec.dtype))
            self.scratch += [dma((1,)), dma((n - 1,)), dma((n - 1,))]

    def bind(self, ins, outs, scratch):
        self.ins, self.full = ins, outs[0]
        self.own, self.local, *self.sems = scratch[:14]
        if self.vec is not None:
            self.vec_in, self.vecs, self.vec_sems = ins[-1], outs[1], scratch[14:]
            self.ins = ins[:-1]
        (self.x, self.c, self.shard, self.pos, self.shard_at, self.ways, self.sibling, self.across, _) = neighbours(self.n)
        on_ring = self.ne + self.ns
        self.mine = pl.ds(self.x * on_ring, self.ne)
        self.sets = (self.mine, pl.ds(self.ne, self.ns))
        self.theirs = pl.ds((1 - self.x) * on_ring, self.ne)

    def at(self, units, owner):
        if self.owner_first:
            return self.full.at[owner, units]
        return self.full.at[units, block_of(owner, self.rows), :]

    def spot(self, units, d, k):
        owner = self.shard_at(self.pos - self.ways[d][1] * k)
        quarter = self.rows // 4
        if self.owner_first:
            return self.full.at[owner, units, block_of(self.c * 2 + d, quarter), :]
        return self.full.at[units, block_of(owner * 4 + self.c * 2 + d, quarter), :]

    def moved(self, kind, units, d, k, hop, who):
        here = self.spot(units, d, k)
        return remote(here, here, self.sems[2 * kind].at[d, hop], self.sems[2 * kind + 1].at[d, hop], who)

    def first(self, e, d):
        src = self.own.at[self.sets[e], block_of(self.c * 2 + d, self.rows // 4), :]
        sems = self.sems[2 * e : 2 * e + 2]
        return remote(src, self.spot(self.sets[e], d, 0), sems[0].at[d, 0], sems[1].at[d, 0], self.ways[d][0])

    def stored(self):
        return pltpu.make_async_copy(self.own, self.at(pl.ds(0, self.units), self.shard), self.local.at[1])

    def ring(self, e, d, k):
        return self.moved(e, self.sets[e], d, k, k, self.ways[d][0])

    def side(self, e, d, k):
        return self.moved(2 + e, self.sets[e], d, k + 1, k, self.sibling)

    def cross(self, d, k):
        return self.moved(4, self.mine, d, k + 1, k, self.across)

    def forward(self, d, k):
        return self.moved(5, self.theirs, d, k + 1, k, self.sibling)

    def vec_hop(self, k):
        here = self.vecs.at[self.shard_at(self.pos - k)]
        return remote(here, here, self.vec_sems[1].at[k], self.vec_sems[2].at[k], self.ways[0][0])

    def begin(self):
        per = self.units // len(self.ins)
        for i, ref in enumerate(self.ins):
            for j in range(per):
                if ref.shape[1] > self.width:
                    part = ref.at[:, pl.ds(j * self.width, self.width)]
                else:
                    part = ref.at[pl.ds(j * self.rows, self.rows), :]
                pltpu.make_async_copy(part, self.own.at[i * per + j], self.local.at[0]).start()
        if self.vec is not None:
            pltpu.make_async_copy(self.vec_in, self.vecs.at[self.shard], self.vec_sems[0].at[0]).start()
        greet((self.ways[0][0], self.ways[1][0], self.sibling, self.across))
        pltpu.make_async_copy(self.own, self.own, self.local.at[0]).wait()
        for e in range(2):
            for d in range(2):
                self.first(e, d).start()
        self.stored().start()
        if self.vec is not None:
            pltpu.make_async_copy(self.vec_in, self.vecs.at[self.shard], self.vec_sems[0].at[0]).wait()

    def step(self, i):
        n = self.n
        pl.when(i == 0)(self.begin)

        for e in range(2):
            for d in range(2):

                @pl.when((i > 0) & (i < n))
                def _():
                    self.ring(e, d, i - 1).wait_recv()

                    @pl.when(i < n - 1)
                    def _():
                        self.ring(e, d, i).start()

                    if e == 0:
                        self.cross(d, i - 1).start()
                    self.side(e, d, i - 1).start()

        @pl.when((i > 1) & (i <= n))
        def _():
            for d in range(2):
                self.cross(d, i - 2).wait_recv()
                self.forward(d, i - 2).start()

        if self.vec is not None:
            @pl.when((i > 0) & (i < n))
            def _():
                self.vec_hop(i - 1).wait_recv()

            @pl.when(i < n - 1)
            def _():
                self.vec_hop(i).start()

    def finish(self, steps):
        n = self.n
        if steps <= n:
            for d in range(2):
                self.cross(d, n - 2).wait_recv()
                self.forward(d, n - 2).start()

        def drain(k, _):
            for d in range(2):
                for e in range(2):
                    self.ring(e, d, k).wait_send()
                    self.side(e, d, k).wait()
                self.cross(d, k).wait_send()
                self.forward(d, k).wait()
            if self.vec is not None:
                self.vec_hop(k).wait_send()
            return 0

        lax.fori_loop(0, n - 1, drain, 0)
        self.stored().wait()


class Scatter:
    def __init__(self, n, sources, alone, vec=None):
        self.n, self.arrays = n, list(sources) + ([] if vec is None else [vec])
        self.vec = vec
        self.counts = [1 if s.ndim == 2 else s.shape[s.ndim - 3] for s in sources]
        self.kinds = [s.ndim for s in sources]
        units = self.units = sum(self.counts)
        self.ne, self.ns = alone, units - 2 * alone
        first = sources[0].shape
        rows = self.rows = first[-2] if len(first) == 4 else first[-2] // n
        width = self.width = sources[0].shape[-1]
        half, self.quarter = rows // 2, rows // 4
        self.out_shapes = [jax.ShapeDtypeStruct((units, rows, width), bf16)]
        dma = pltpu.SemaphoreType.DMA
        self.scratch = [
            pltpu.VMEM((units, n * half, width), bf16),
            pltpu.VMEM((units, n * half, width), bf16),
            pltpu.VMEM((alone, n * half, width), bf16),
            pltpu.VMEM((2, n - 1, alone, half // 2, width), bf16),
            pltpu.VMEM((2, n - 1, self.ns, half // 2, width), bf16),
            pltpu.VMEM((self.ns, half, width), bf16),
            pltpu.VMEM((alone, half, width), bf16),
            dma((2, n)), dma((2, n)), dma((2, n)), dma((2, n)), dma((2, n)),
            dma((2, n - 1)), dma((2, n - 1)), dma((2, n - 1)), dma((2, n - 1)),
            dma((2,)), dma((2,)), dma((3,)), dma((3,)), dma((3,)),
        ]
        if vec is not None:
            self.out_shapes.append(jax.ShapeDtypeStruct((8, rows), f32))
            self.scratch += [
                pltpu.VMEM((n, 8, rows), f32), pltpu.VMEM((n - 1, 8, rows), f32), pltpu.VMEM((4, 8, rows), f32),
                pltpu.VMEM((8, rows), f32), dma((2,)), dma((n - 1,)), dma((n - 1,)), dma((3,)), dma((3,)),
            ]

    def bind(self, ins, outs, scratch):
        self.ins, self.out = ins, outs[0]
        (self.near, self.beside, self.over, slots_e, slots_s, self.swap_s, self.swap_e, self.local, self.cs, self.cr,
         self.xs, self.xr, *ring_sems, self.ss, self.sr, self.os, self.orr, self.done) = scratch[:21]
        self.slots, self.ring_sems = (slots_e, slots_s), (ring_sems[:2], ring_sems[2:])
        if self.vec is not None:
            self.vec_in, self.vec_out, self.ins = ins[-1], outs[1], ins[:-1]
            (self.v_near, self.v_ring, self.v_all, self.v_sum, self.v_local, self.v_rs, self.v_rr,
             self.v_ss, self.v_sr) = scratch[21:]
        (self.x, self.c, self.shard, self.pos, self.shard_at, self.ways, self.sibling, self.across,
         self.corner) = neighbours(self.n)
        self.on_ring = self.ne + self.ns
        self.theirs = pl.ds((1 - self.x) * self.on_ring, self.ne)
        self.mine = pl.ds(self.x * self.on_ring, self.ne)
        self.shared = pl.ds(self.ne, self.ns)
        self.sets = (self.mine, self.shared)

    def owner(self, d, k):
        return self.shard_at(self.pos - self.ways[d][1] * (1 + k))

    def span(self, d, k):
        return block_of(self.owner(d, k) * 2 + d, self.quarter)

    def region(self, ref, d, k):
        return ref.at[:, self.span(d, k), :]

    def pieces(self, d, k, core, target):
        owner = self.owner(d, k)
        u = 0
        for ref, count, kind in zip(self.ins, self.counts, self.kinds):
            rows = block_of(owner * 4 + core * 2 + d, self.quarter)
            if kind == 4:
                src = ref.at[owner, :, block_of(core * 2 + d, self.quarter), :]
            else:
                src = ref.at[rows, :] if kind == 2 else ref.at[:, rows, :]
            units = u if kind == 2 else pl.ds(u, count)
            yield src, target.at[units, self.span(d, k), :]
            u += count

    def crossing(self, d, k):
        rows = self.span(d, k)
        return remote(
            self.near.at[self.theirs, rows, :], self.over.at[:, rows, :], self.xs.at[d, k], self.xr.at[d, k], self.across
        )

    def hop(self, e, d, k):
        src = self.near.at[self.sets[e], self.span(d, k), :]
        sent, got = self.ring_sems[e]
        return remote(src, self.slots[e].at[d, k], sent.at[d, k], got.at[d, k], self.ways[d][0])

    def vec_hop(self, k):
        return remote(self.v_near.at[self.owner(0, k)], self.v_ring.at[k], self.v_rs.at[k], self.v_rr.at[k], self.ways[0][0])

    def begin(self):
        n = self.n

        def loads(k, _):
            for d in range(2):
                for src, dst in self.pieces(d, k, self.c, self.near):
                    pltpu.make_async_copy(src, dst, self.local.at[d, k]).start()
            return 0

        lax.fori_loop(0, n, loads, 0)
        if self.vec is not None:
            for s in range(n):
                pltpu.make_async_copy(
                    self.vec_in.at[:, pl.ds(s * self.rows, self.rows)], self.v_near.at[s], self.v_local.at[0]
                ).start()
        greet((self.ways[0][0], self.ways[1][0], self.sibling, self.across) + (() if self.vec is None else (self.corner,)))

        def sends(k, _):
            for d in range(2):
                for src, dst in self.pieces(d, k, 1 - self.c, self.beside):
                    remote(src, dst, self.cs.at[d, k], self.cr.at[d, k], self.sibling).start()
            return 0

        lax.fori_loop(0, n, sends, 0)
        if self.vec is not None:
            pltpu.make_async_copy(self.v_near, self.v_near, self.v_local.at[0]).wait()
        self.pair(0)
        self.pair(1)

    def arrived(self, ref, ssem, rsem, d, k):
        here = self.region(ref, d, k)
        return remote(here, here, ssem.at[d, k], rsem.at[d, k], self.sibling)

    def pair(self, k):
        for d in range(2):
            rows = self.span(d, k)
            here = self.region(self.near, d, k)
            pltpu.make_async_copy(here, here, self.local.at[d, k]).wait()
            self.arrived(self.beside, self.cs, self.cr, d, k).wait_recv()

            def add(u, _):
                self.near[u, rows, :] = self.near[u, rows, :] + self.beside[u, rows, :]
                return 0

            lax.fori_loop(0, self.units, add, 0)
            self.crossing(d, k).start()

    def combine(self, k, later):
        for e in (1, 0):
            for d in range(2):
                rows = self.span(d, k)
                if later:
                    self.hop(e, d, k - 1).wait_recv()
                if e == 0:
                    self.crossing(d, k).wait_recv()

                def add_shared(i, _):
                    u = self.ne + i
                    self.near[u, rows, :] = self.near[u, rows, :] + self.slots[1][d, k - 1, i]
                    return 0

                def add_mine(i, _):
                    u = self.x * self.on_ring + i
                    value = self.near[u, rows, :].astype(f32) + self.over[i, rows, :].astype(f32)
                    if later:
                        value = value + self.slots[0][d, k - 1, i].astype(f32)
                    self.near[u, rows, :] = value.astype(bf16)
                    return 0

                if e == 0:
                    lax.fori_loop(0, self.ne, add_mine, 0)
                elif later:
                    lax.fori_loop(0, self.ns, add_shared, 0)

                @pl.when(k < self.n - 1)
                def _():
                    self.hop(e, d, k).start()

        if self.vec is not None:
            if later:
                self.vec_hop(k - 1).wait_recv()
                self.v_near[self.owner(0, k)] = self.v_near[self.owner(0, k)] + self.v_ring[k - 1]

            @pl.when(k < self.n - 1)
            def _():
                self.vec_hop(k).start()

    def step(self, i):
        pl.when(i == 0)(self.begin)

        @pl.when(i == 0)
        def _():
            self.combine(i, False)

        @pl.when((i > 0) & (i < self.n))
        def _():
            self.combine(i, True)

        @pl.when(i + 2 < self.n)
        def _():
            self.pair(i + 2)

    def finish(self, steps):
        n = self.n
        at = block_of(self.shard, self.rows // 2)
        half = block_of(self.c, self.rows // 2)
        near, out = self.near, self.out
        swap = send(near.at[self.shared, at, :], self.swap_s, self.ss.at[0], self.sr.at[0], self.across)
        give = send(near.at[self.mine, at, :], self.swap_e, self.ss.at[1], self.sr.at[1], self.across)
        final = [send(near.at[self.mine, at, :], out.at[self.mine, half, :], self.os.at[0], self.orr.at[0], self.sibling)]
        keep = [load(near.at[self.mine, at, :], out.at[self.mine, half, :], self.done.at[0])]
        if self.vec is not None:
            sums = self.v_near.at[self.shard]
            rep = self.x * 2 + self.c
            shares = [
                send(sums, self.v_all.at[rep], self.v_ss.at[j], self.v_sr.at[j], who)
                for j, who in enumerate((self.sibling, self.across, self.corner))
            ]
            self.v_all[rep] = sums[...]
        swap.wait_recv()

        def join(i, _):
            self.swap_s[i] = (self.swap_s[i].astype(f32) + near[self.ne + i, at, :].astype(f32)).astype(bf16)
            return 0

        lax.fori_loop(0, self.ns, join, 0)
        final.append(send(self.swap_s, out.at[self.shared, half, :], self.os.at[1], self.orr.at[1], self.sibling))
        keep.append(load(self.swap_s, out.at[self.shared, half, :], self.done.at[1]))
        give.wait_recv()
        final.append(send(self.swap_e, out.at[self.theirs, half, :], self.os.at[2], self.orr.at[2], self.sibling))
        keep.append(load(self.swap_e, out.at[self.theirs, half, :], self.done.at[2]))
        if self.vec is not None:
            for copy in shares:
                copy.wait()
            self.v_sum[...] = (self.v_all[0] + self.v_all[1]) + (self.v_all[2] + self.v_all[3])
            keep.append(load(self.v_sum, self.vec_out, self.v_local.at[1]))
        for copy in keep:
            copy.wait()
        for copy in final:
            copy.wait()
        swap.wait_send()
        give.wait_send()

        def drain(k, _):
            for d in range(2):
                self.arrived(self.beside, self.cs, self.cr, d, k).wait_send()
                self.crossing(d, k).wait_send()
            return 0

        lax.fori_loop(0, n, drain, 0)

        def drain_ring(k, _):
            for d in range(2):
                self.hop(0, d, k).wait_send()
                self.hop(1, d, k).wait_send()
            if self.vec is not None:
                self.vec_hop(k).wait_send()
            return 0

        lax.fori_loop(0, n - 1, drain_ring, 0)


def hosted(kernel, steps, args, in_specs, out_shapes, out_specs, scratch, name, carry=None, collective_id=None, done_by=None, vmem=58):
    counts = [len(args), len(out_shapes), len(scratch)]
    extra = [0, 0, 0]
    params = dict(vmem_limit_bytes=vmem * MIB)
    if carry is not None:
        extra = [len(carry.arrays), len(carry.out_shapes), len(carry.scratch)]
        params.update(collective_id=collective_id, has_side_effects=True)

    def whole(*refs):
        main, other, first = [], [], 0
        for count, more in zip(counts, extra):
            main += refs[first : first + count]
            other.append(refs[first + count : first + count + more])
            first += count + more
        i = pl.program_id(0)
        if carry is not None:
            carry.bind(*other)
            carry.step(i)
            if done_by is not None:
                pl.when(i == done_by)(lambda: carry.finish(done_by + 1))
        if kernel is not None:
            kernel(*main)
        if carry is not None and done_by is None:
            pl.when(i == steps - 1)(lambda: carry.finish(steps))

    return pl.pallas_call(
        whole,
        grid=(steps,),
        out_shape=list(out_shapes) + (carry.out_shapes if carry else []),
        in_specs=list(in_specs) + [HBM] * extra[0],
        out_specs=list(out_specs) + [HBM] * extra[1],
        scratch_shapes=list(scratch) + (carry.scratch if carry else []),
        compiler_params=pltpu.CompilerParams(**params),
        name=name,
    )(*args, *(carry.arrays if carry else []))


def first_lanes(shape):
    return lax.broadcasted_iota(jnp.int32, shape, len(shape) - 1) < HD


def region_bias(starts_ref, region, size, transposed):
    first = region * size
    one = first + lax.broadcasted_iota(jnp.int32, (size, size), 0)
    two = first + lax.broadcasted_iota(jnp.int32, (size, size), 1)
    q_at, k_at = (two, one) if transposed else (one, two)
    start = starts_ref[0, region]
    q_in = (q_at >= start) & (q_at < start + PIC)
    k_in = (k_at >= start) & (k_at < start + PIC)
    return jnp.where((k_at <= q_at) | (q_in & k_in), 0.0, NEGATIVE)


def attend_forward_kernel(regions, starts_ref, q_ref, k_ref, v_ref, o_ref, lse_ref, bias_ref):
    rows = q_ref.shape[0]
    size = rows // regions

    if starts_ref is not None:
        @pl.when(pl.program_id(0) == 0)
        def _():
            for r in range(regions):
                bias_ref[r] = region_bias(starts_ref, r, size, False)

    low = first_lanes((1, 2 * HD))
    outs, lses = [[], []], [[], []]
    for h in range(2):
        pick = low if h == 0 else ~low
        keys = jnp.where(pick, k_ref[...], jnp.zeros((), bf16))
        for r in range(regions):
            span = slice(r * size, (r + 1) * size)
            q = q_ref[span, :]
            scores = []
            if starts_ref is None:
                scores.append((dot(q, keys, 1, 1), v_ref[...]))
            else:
                if r:
                    scores.append((dot(q, keys[: r * size], 1, 1), v_ref[: r * size, :]))
                scores.append((dot(q, keys[span], 1, 1) + bias_ref[r], v_ref[span, :]))
            top = functools.reduce(jnp.maximum, [jnp.max(s, -1, keepdims=True) for s, _ in scores])
            total, mixed = 0.0, 0.0
            for s, v in scores:
                e = jnp.exp(s - top)
                total = total + jnp.sum(e, -1, keepdims=True)
                mixed = mixed + dot(e.astype(bf16), v)
            outs[h].append(mixed / total)
            lses[h].append(top + jnp.log(total))
    for r in range(regions):
        span = slice(r * size, (r + 1) * size)
        o_ref[span, :] = jnp.where(low, outs[0][r], outs[1][r]).astype(bf16)
        turned = jnp.where(low, lses[0][r], lses[1][r]).T
        lse_ref[0, 0:1, span] = turned[0:1]
        lse_ref[0, 1:2, span] = turned[HD : HD + 1]


def attend_parts(kernel, regions_of, starts, arrays, rows):
    tall = [pl.BlockSpec((a.shape[0], 2 * HD), lambda i: (0, i)) if a.ndim == 2 else pl.BlockSpec((1, 8, rows), lambda i: (i, 0, 0)) for a in arrays]
    if starts is None:
        return lambda *refs: kernel(regions_of, None, *refs, None), list(arrays), tall, []
    size = rows // regions_of
    scratch = [pltpu.VMEM((regions_of, size, size), f32)]
    return functools.partial(kernel, regions_of), [starts, *arrays], [pl.BlockSpec(memory_space=pltpu.SMEM), *tall], scratch


def attend_forward(q, k, v, starts, carry, collective_id):
    rows, width = q.shape
    pairs = width // (2 * HD)
    kernel, args, specs, scratch = attend_parts(
        attend_forward_kernel, 2 if starts is None else starts.shape[1], starts, (q, k, v), rows
    )
    return hosted(
        kernel, pairs, args, specs,
        [jax.ShapeDtypeStruct((rows, width), bf16), jax.ShapeDtypeStruct((pairs, 8, rows), f32)],
        [pl.BlockSpec((rows, 2 * HD), lambda i: (0, i)), pl.BlockSpec((1, 8, rows), lambda i: (i, 0, 0))],
        scratch, "self_forward" if starts is not None else "cross_forward", carry, collective_id,
    )


def attend_backward_kernel(
    regions, starts_ref, q_ref, k_ref, v_ref, g_ref, o_ref, lse_ref, gq_ref, gk_ref, gv_ref, bias_ref
):
    rows = q_ref.shape[0]
    size = rows // regions

    if starts_ref is not None:
        @pl.when(pl.program_id(0) == 0)
        def _():
            for r in range(regions):
                bias_ref[r] = region_bias(starts_ref, r, size, True)

    low = first_lanes((1, 2 * HD))
    product = g_ref[...].astype(f32) * o_ref[...].astype(f32)
    chooser = lax.broadcasted_iota(jnp.int32, (8, 2 * HD), 0)
    chooser = ((chooser == 0) & first_lanes((8, 2 * HD))) | ((chooser == 1) & ~first_lanes((8, 2 * HD)))
    chooser = chooser.astype(f32).astype(bf16)
    upper = product.astype(bf16)
    lower = (product - upper.astype(f32)).astype(bf16)
    deltas = dot(chooser, upper, 1, 1) + dot(chooser, lower, 1, 1)
    gq, gk, gv = {}, {}, {}
    key_spans = [slice(0, k_ref.shape[0])]
    if starts_ref is not None:
        key_spans = [slice(r * size, (r + 1) * size) for r in range(regions)]
    for h in range(2):
        pick = low if h == 0 else ~low
        zero = jnp.zeros((), bf16)
        keys = jnp.where(pick, k_ref[...], zero)
        values = jnp.where(pick, v_ref[...], zero)
        for r in range(regions):
            span = slice(r * size, (r + 1) * size)
            q, g = q_ref[span, :], g_ref[span, :]
            lse = lse_ref[0, h : h + 1, span]
            delta = deltas[h : h + 1, span]
            for j, keyed in enumerate(key_spans):
                if starts_ref is not None and j > r:
                    continue
                scores = dot(keys[keyed], q, 1, 1)
                if starts_ref is not None and j == r:
                    scores = scores + bias_ref[r]
                probs = jnp.exp(scores - lse)
                grad_probs = dot(values[keyed], g, 1, 1)
                grad_scores = (probs * (grad_probs - delta)).astype(bf16)
                gv[h, j] = gv.get((h, j), 0.0) + dot(probs.astype(bf16), g)
                gk[h, j] = gk.get((h, j), 0.0) + dot(grad_scores, q)
                gq[h, r] = gq.get((h, r), 0.0) + dot(grad_scores, k_ref[keyed, :], 0, 0)
    for r in range(regions):
        span = slice(r * size, (r + 1) * size)
        gq_ref[span, :] = jnp.where(low, gq[0, r], gq[1, r]).astype(bf16)
    for j, keyed in enumerate(key_spans):
        gk_ref[keyed, :] = jnp.where(low, gk[0, j], gk[1, j]).astype(bf16)
        gv_ref[keyed, :] = jnp.where(low, gv[0, j], gv[1, j]).astype(bf16)


def attend_backward(q, k, v, g, o, lse, starts, carry, collective_id):
    rows, width = q.shape
    kernel, args, specs, scratch = attend_parts(
        attend_backward_kernel, 2 if starts is None else starts.shape[1], starts, (q, k, v, g, o, lse), rows
    )
    return hosted(
        kernel, width // (2 * HD), args, specs,
        [jax.ShapeDtypeStruct(a.shape, bf16) for a in (q, k, v)],
        [pl.BlockSpec((a.shape[0], 2 * HD), lambda i: (0, i)) for a in (q, k, v)],
        scratch, "self_backward" if starts is not None else "cross_backward", carry, collective_id,
    )


def norm_forward(resid, gain, shift):
    mean = jnp.mean(resid, -1, keepdims=True)
    centred = resid - mean
    variance = jnp.mean(centred * centred, -1, keepdims=True)
    inverse = lax.rsqrt(variance + EPS)
    normed = centred * inverse
    return (normed * gain + shift, normed, inverse)


def norm_backward(grad_out, normed, inverse, gain):
    grad_gain = jnp.sum(grad_out * normed, 0, keepdims=True)
    grad_shift = jnp.sum(grad_out, 0, keepdims=True)
    grad_normed = grad_out * gain
    centre_term = jnp.mean(grad_normed, -1, keepdims=True)
    slope_term = jnp.mean(grad_normed * normed, -1, keepdims=True)
    return (inverse * (grad_normed - centre_term - normed * slope_term), grad_gain, grad_shift)


def fixed(a):
    zeros = (0,) * a.ndim
    return pl.BlockSpec(a.shape, lambda i: zeros, pipeline_mode=pl.Buffered(1))


def slices(rows, count):
    size = rows // count
    return [slice(j * size, (j + 1) * size) for j in range(count)]


def ffn_forward_kernel(blocks, carry, low_ref, two_ref, cot_ref, vec_ref, w1_ref, *refs):
    refs = list(refs)
    w2_ref = refs.pop(0) if carry is None else carry.full
    final_ref, branch_ref, grad_ref, act_ref, slope_ref, sums_ref, acts, acc, w2_buf, sems = refs
    i = pl.program_id(0)
    spans = slices(low_ref.shape[0], 4)

    @pl.when(i < blocks)
    def _():
        for span in spans:
            pre = dot(low_ref[span, :], w1_ref[0])
            phi = 0.5 * (1.0 + lax.erf(pre * INV_ROOT_TWO))
            act = (pre * phi).astype(bf16)
            acts[i, span, :] = act
            act_ref[span, :] = act
            slope_ref[span, :] = (phi + pre * jnp.exp(-0.5 * pre * pre) * INV_ROOT_TWO_PI).astype(bf16)

    j = i - blocks

    def fetch(block, slot):
        return pltpu.make_async_copy(w2_ref.at[block], w2_buf.at[slot], sems.at[slot])

    @pl.when(j == 0)
    def _():
        fetch(0, 0).start()
        acc[...] = two_ref[...]

    @pl.when(j >= 0)
    def _():
        slot = lax.rem(j + blocks * 2, 2)

        @pl.when(j + 1 < blocks)
        def _():
            fetch(j + 1, 1 - slot).start()

        fetch(j, slot).wait()
        w2 = w2_buf[slot].reshape(-1, w2_buf.shape[-1])
        for span in spans:
            acc[span, :] += dot(acts[j, span, :], w2)

    @pl.when(j == blocks - 1)
    def _():
        gain, shift = vec_ref[4:5, :], vec_ref[5:6, :]
        sums = [0.0, 0.0]
        for span in slices(low_ref.shape[0], 8):
            final, normed, inverse = norm_forward(acc[span, :], gain, shift)
            final_ref[span, :] = final.astype(bf16)
            grad, *parts = norm_backward(cot_ref[span, :].astype(f32), normed, inverse, gain)
            grad_ref[span, :] = grad
            branch_ref[span, :] = grad.astype(bf16)
            sums = [a + b for a, b in zip(sums, parts)]
        sums_ref[...] = jnp.zeros_like(sums_ref)
        sums_ref[0:1, :] = sums[0]
        sums_ref[1:2, :] = sums[1]


def ffn_forward(low, two, cotangent, vecs, w1, w2, carry, collective_id):
    rows, width = low.shape
    if carry is not None:
        blocks, size = carry.n, carry.units * carry.rows
    else:
        blocks, size = w2.shape[0], w2.shape[1] * w2.shape[2]
    per = width // size
    last = blocks - 1
    args = [low, two, cotangent, vecs, w1]
    specs = [fixed(a) for a in args[:4]]
    specs.append(pl.BlockSpec((1, width, size), lambda i: (jnp.minimum(i, last) // per, 0, lax.rem(jnp.minimum(i, last), per))))
    if carry is None:
        args.append(w2)
        specs.append(HBM)
    tall = jax.ShapeDtypeStruct((rows, blocks * size), bf16)
    outs = [low, low, two, tall, tall, jax.ShapeDtypeStruct((8, width), f32)]
    out_specs = [fixed(a) for a in outs[:3]]
    out_specs += [pl.BlockSpec((rows, size), lambda i: (0, jnp.minimum(i, last)))] * 2 + [fixed(outs[5])]
    part = (width // 256, size // (width // 256), width) if carry is None else (carry.units, carry.rows, width)
    return hosted(
        functools.partial(ffn_forward_kernel, blocks, carry), 2 * blocks, args, specs,
        [jax.ShapeDtypeStruct(a.shape, a.dtype) for a in outs], out_specs,
        [
            pltpu.VMEM((blocks, rows, size), bf16), pltpu.VMEM((rows, width), f32),
            pltpu.VMEM((2,) + part, bf16), pltpu.SemaphoreType.DMA((2,)),
        ],
        "ffn_forward", carry, collective_id, done_by=blocks if carry else None, vmem=60,
    )


def ffn_backward_kernel(
    low_ref, branch_ref, g_ref, normed_ref, inverse_ref, vec_ref, w1_ref, w2_ref, act_ref, slope_ref,
    g_expand_ref, g_contract_ref, grad_ref, branch_two_ref, sums_ref, turned, acc,
):
    i = pl.program_id(0)
    rows = low_ref.shape[0]
    spans = slices(rows, 4)

    @pl.when(i == 0)
    def _():
        turned[...] = low_ref[...].T
        acc[...] = g_ref[...]

    w2 = w2_ref[0].reshape(-1, w2_ref.shape[-1])
    g_contract_ref[0] = dot(act_ref[...], branch_ref[...], 0, 0).astype(bf16).reshape(g_contract_ref.shape[1:])
    expand = 0.0
    for span in spans:
        g_pre = (dot(branch_ref[span, :], w2, 1, 1) * slope_ref[span, :].astype(f32)).astype(bf16)
        expand = expand + dot(turned[:, span], g_pre)
        acc[span, :] += dot(g_pre, w1_ref[0], 1, 1)
    g_expand_ref[0] = expand.astype(bf16)

    @pl.when(i == pl.num_programs(0) - 1)
    def _():
        gain = vec_ref[2:3, :]
        sums = [0.0, 0.0]
        for span in slices(rows, 8):
            grad, *parts = norm_backward(acc[span, :], normed_ref[span, :], inverse_ref[span, :], gain)
            grad_ref[span, :] = grad
            branch_two_ref[span, :] = grad.astype(bf16)
            sums = [a + b for a, b in zip(sums, parts)]
        sums_ref[...] = jnp.zeros_like(sums_ref)
        sums_ref[0:1, :] = sums[0]
        sums_ref[1:2, :] = sums[1]


def ffn_backward(low, branch, grad, normed, inverse, vecs, w1, w2, act, slope):
    rows, width = low.shape
    blocks, size = w2.shape[0], w2.shape[1] * w2.shape[2]
    per = width // size
    wide = pl.BlockSpec((1, width, size), lambda i: (i // per, 0, lax.rem(i, per)))
    deep = pl.BlockSpec((1,) + w2.shape[1:], lambda i: (i, 0, 0, 0))
    column = pl.BlockSpec((rows, size), lambda i: (0, i))
    args = [low, branch, grad, normed, inverse, vecs, w1, w2, act, slope]
    outs = [w1, w2, grad, low, jax.ShapeDtypeStruct((8, width), f32)]
    return hosted(
        ffn_backward_kernel, blocks, args, [fixed(a) for a in args[:6]] + [wide, deep, column, column],
        [jax.ShapeDtypeStruct(a.shape, a.dtype) for a in outs], [wide, deep] + [fixed(a) for a in outs[2:]],
        [pltpu.VMEM((width, rows), bf16), pltpu.VMEM((rows, width), f32)], "ffn_backward", vmem=60,
    )


def body(n, states, encoded, starts, cotangent, *weights):
    matrices, vectors = weights[:10], weights[10:]
    expand, contract = matrices[8], matrices[9]
    rows, width = matrices[0].shape
    blocks = contract.shape[0] // rows
    scale = HD ** (-0.5)
    small = n <= 16
    vec = jnp.zeros((16, max(rows, 128)), bf16).at[: len(vectors), :rows].set(jnp.stack(vectors))
    take = lambda shards, units, alone, **more: Gather(n, width, shards, units, alone, **more) if small else None
    if small:
        first, vecs = hosted(None, n, [], [], [], [], [], "gather_first", take(matrices[:3], 3, 1, vec=vec), 0)
    else:
        first = lax.all_gather(jnp.stack(matrices[:3]), "shard", axis=1, tiled=True)
        vecs = lax.all_gather(vec, "shard", axis=0)
    vecs = vecs[:, : len(vectors), :rows].transpose(1, 0, 2).reshape(len(vectors), width).astype(f32)
    vecs = jnp.concatenate([vecs, jnp.zeros((2, width), f32)])
    gain_one, shift_one, gain_two, shift_two = [vecs[i] for i in range(4)]
    w_sq, w_sk, w_sv = [first[i] for i in range(3)]

    wide = states.astype(f32)
    q_self = (dot(states, w_sq) * scale).astype(bf16)
    k_self = dot(states, w_sk).astype(bf16)
    v_self = dot(states, w_sv).astype(bf16)
    mixed_self, lse_self, *second = attend_forward(q_self, k_self, v_self, starts, take(matrices[3:8], 5, 2), 1)
    if not small:
        second = [lax.all_gather(jnp.stack(matrices[3:8]), "shard", axis=1, tiled=True)]
    w_so, w_cq, w_ck, w_cv, w_co = [second[0][i] for i in range(5)]
    hidden_one, normed_one, inverse_one = norm_forward(wide + dot(mixed_self, w_so), gain_one, shift_one)
    one_low = hidden_one.astype(bf16)
    q_cross = (dot(one_low, w_cq) * scale).astype(bf16)
    k_cross = dot(encoded, w_ck).astype(bf16)
    v_cross = dot(encoded, w_cv).astype(bf16)
    mixed_cross, lse_cross, *third = attend_forward(q_cross, k_cross, v_cross, None, take([expand], blocks, 1), 2)
    if not small:
        third = [lax.all_gather(expand.reshape(rows, blocks, width).transpose(1, 0, 2), "shard", axis=1, tiled=True)]
    w1 = third[0]
    hidden_two, normed_two, inverse_two = norm_forward(hidden_one + dot(mixed_cross, w_co), gain_two, shift_two)
    two_low = hidden_two.astype(bf16)
    w2 = None
    if not small:
        w2 = lax.all_gather(contract, "shard", axis=0, tiled=True).reshape(8, 4, -1, width)
    final, branch_three, grad_three, act, slope, sums_three, *fourth = ffn_forward(
        two_low, hidden_two, cotangent, vecs, w1, w2, take([contract], blocks, 1, owner_first=True), 3
    )
    if small:
        w2 = fourth[0]

    give = lambda sources, alone, **more: Scatter(n, sources, alone, **more) if small else None
    g_expand, g_contract, grad_resid_two, branch_two, sums_two = ffn_backward(
        two_low, branch_three, grad_three, normed_two, inverse_two, vecs, w1, w2, act, slope
    )
    g_cross_out = dot(mixed_cross, branch_two, 0, 0).astype(bf16)
    grad_mixed = dot(branch_two, w_co, 1, 1).astype(bf16)
    g_q, g_k, g_v, *own_contract = attend_backward(
        q_cross, k_cross, v_cross, grad_mixed, mixed_cross, lse_cross, None, give([g_contract], 1), 4
    )
    g_q = g_q * scale
    g_cross = [
        dot(one_low, g_q, 0, 0).astype(bf16), dot(encoded, g_k, 0, 0).astype(bf16), dot(encoded, g_v, 0, 0).astype(bf16),
        g_cross_out,
    ]
    grad_encoded = dot(g_k, w_ck, 1, 1) + dot(g_v, w_cv, 1, 1)
    grad_one = grad_resid_two + dot(g_q, w_cq, 1, 1)
    grad_resid_one, *sums_one = norm_backward(grad_one, normed_one, inverse_one, gain_one)
    branch_one = grad_resid_one.astype(bf16)
    g_self_out = dot(mixed_self, branch_one, 0, 0).astype(bf16)
    grad_mixed = dot(branch_one, w_so, 1, 1).astype(bf16)
    g_q, g_k, g_v, *own_middle = attend_backward(
        q_self, k_self, v_self, grad_mixed, mixed_self, lse_self, starts, give([g_expand, *g_cross], 2), 5
    )
    g_q = g_q * scale
    g_self = [dot(states, g, 0, 0).astype(bf16) for g in (g_q, g_k, g_v)] + [g_self_out]
    grad_states = grad_resid_one + dot(g_q, w_sq, 1, 1) + dot(g_k, w_sk, 1, 1) + dot(g_v, w_sv, 1, 1)
    grads_vec = jnp.concatenate([*sums_one, sums_two[:2], sums_three[:2], jnp.zeros((2, width), f32)])
    if small:
        own_self, own_vec = hosted(None, n, [], [], [], [], [], "scatter_last", give(g_self, 1, vec=grads_vec), 6)
        own_contract, own_middle = own_contract[0], own_middle[0]
    else:
        total = lambda g: lax.psum(lax.psum_scatter(g, "shard", scatter_dimension=1, tiled=True), "rep")
        own_self = total(jnp.stack(g_self))
        own_middle = total(jnp.concatenate([g_expand, jnp.stack(g_cross)]))
        own_contract = total(g_contract.reshape(1, -1, width))
        own_vec = lax.dynamic_slice_in_dim(
            lax.psum(grads_vec, ("rep", "shard")), lax.axis_index("shard") * rows, rows, 1
        )
    own_contract = own_contract.reshape(blocks * rows, width).astype(f32)
    own_expand = jnp.concatenate([own_middle[j] for j in range(blocks)], 1).astype(f32)
    attention = [own_self[j] for j in range(4)] + [own_middle[blocks + j] for j in range(4)]
    return (
        final,
        grad_states,
        grad_encoded,
        *[g.astype(f32) for g in attention],
        own_expand,
        own_contract,
        *[own_vec[i] for i in range(6)],
    )


def solution(mesh):
    many, few = P(("rep", "shard"), None), P("shard", None)
    return jax.shard_map(
        functools.partial(body, mesh.shape["shard"]),
        mesh=mesh,
        in_specs=(many,) * 4 + (few,) * 10 + (P("shard"),) * 6,
        out_specs=(many,) * 3 + (few,) * 10 + (P("shard"),) * 6,
        check_vma=False,
    )
```

```python
import functools

import jax
import jax.numpy as jnp
from jax import lax
from jax.experimental import pallas as pl
from jax.experimental.pallas import tpu as pltpu
from jax.sharding import PartitionSpec as P

HD = 64
PIC = 256
EPS = 1e-05
NEGATIVE = -1e30
INV_ROOT_TWO = 0.7071067811865476
INV_ROOT_TWO_PI = 0.3989422804014327
MESH = pl.DeviceIdType.MESH
MIB = 1 << 20
HBM = pl.BlockSpec(memory_space=pltpu.HBM)
bf16 = jnp.bfloat16
f32 = jnp.float32


def dot(a, b, ca=1, cb=0):
    return lax.dot_general(a, b, (((ca,), (cb,)), ((), ())), preferred_element_type=f32)


def place(n):
    half = n // 2

    def shard_at(pos):
        pos = lax.rem(pos + 2 * n, n)
        back = pos // half
        return (1 - back) * 2 * pos + back * (2 * (n - 1 - pos) + 1)

    s = lax.axis_index("shard")
    odd = s % 2
    pos = (1 - odd) * (s // 2) + odd * (n - 1 - s // 2)
    return pos, shard_at


def greet(partners):
    barrier = pltpu.get_barrier_semaphore()
    for who in partners:
        pl.semaphore_signal(barrier, inc=1, device_id=who, device_id_type=MESH)
    pl.semaphore_wait(barrier, len(partners))


def send(src, dst, ssem, rsem, who):
    copy = pltpu.make_async_remote_copy(
        src_ref=src, dst_ref=dst, send_sem=ssem, recv_sem=rsem, device_id=who, device_id_type=MESH
    )
    copy.start()
    return copy


def load(src, dst, sem):
    copy = pltpu.make_async_copy(src, dst, sem)
    copy.start()
    return copy


def neighbours(n):
    rep, shard = lax.axis_index("rep"), lax.axis_index("shard")
    x, c = rep // 2, rep % 2
    pos, shard_at = place(n)
    ways = (((rep, shard_at(pos + 1)), 1), ((rep, shard_at(pos - 1)), -1))
    sibling, across, corner = (x * 2 + 1 - c, shard), ((1 - x) * 2 + c, shard), ((1 - x) * 2 + 1 - c, shard)
    return x, c, shard, pos, shard_at, ways, sibling, across, corner


def remote(src, dst, ssem, rsem, who):
    return pltpu.make_async_remote_copy(
        src_ref=src, dst_ref=dst, send_sem=ssem, recv_sem=rsem, device_id=who, device_id_type=MESH
    )


def block_of(index, size):
    return pl.ds(pl.multiple_of(index * size, size), size)


class Gather:
    def __init__(self, n, width, shards, units, alone, owner_first=False, vec=None):
        self.n, self.shards, self.owner_first, self.vec, self.follows = n, shards, owner_first, vec, False
        self.units, self.ne, self.ns = units, alone, units - 2 * alone
        self.rows, self.width = sum(s.size for s in shards) // (units * width), width
        self.arrays = list(shards) + ([] if vec is None else [vec])
        shape = (n, units, self.rows, self.width) if owner_first else (units, n * self.rows, self.width)
        self.out_shapes = [jax.ShapeDtypeStruct(shape, bf16)]
        dma = pltpu.SemaphoreType.DMA
        self.scratch = [pltpu.VMEM((units, self.rows, width), bf16), dma((2,))] + [dma((2, n - 1))] * 12
        if vec is not None:
            self.out_shapes.append(jax.ShapeDtypeStruct((n,) + vec.shape, vec.dtype))
            self.scratch += [dma((1,)), dma((n - 1,)), dma((n - 1,))]

    def bind(self, ins, outs, scratch):
        self.ins, self.full = ins, outs[0]
        self.own, self.local, *self.sems = scratch[:14]
        if self.vec is not None:
            self.vec_in, self.vecs, self.vec_sems = ins[-1], outs[1], scratch[14:]
            self.ins = ins[:-1]
        (self.x, self.c, self.shard, self.pos, self.shard_at, self.ways, self.sibling, self.across, _) = neighbours(self.n)
        on_ring = self.ne + self.ns
        self.mine = pl.ds(self.x * on_ring, self.ne)
        self.sets = (self.mine, pl.ds(self.ne, self.ns))
        self.theirs = pl.ds((1 - self.x) * on_ring, self.ne)

    def at(self, units, owner):
        if self.owner_first:
            return self.full.at[owner, units]
        return self.full.at[units, block_of(owner, self.rows), :]

    def spot(self, units, d, k):
        owner = self.shard_at(self.pos - self.ways[d][1] * k)
        quarter = self.rows // 4
        if self.owner_first:
            return self.full.at[owner, units, block_of(self.c * 2 + d, quarter), :]
        return self.full.at[units, block_of(owner * 4 + self.c * 2 + d, quarter), :]

    def moved(self, kind, units, d, k, hop, who):
        here = self.spot(units, d, k)
        return remote(here, here, self.sems[2 * kind].at[d, hop], self.sems[2 * kind + 1].at[d, hop], who)

    def first(self, e, d):
        src = self.own.at[self.sets[e], block_of(self.c * 2 + d, self.rows // 4), :]
        sems = self.sems[2 * e : 2 * e + 2]
        return remote(src, self.spot(self.sets[e], d, 0), sems[0].at[d, 0], sems[1].at[d, 0], self.ways[d][0])

    def stored(self):
        return pltpu.make_async_copy(self.own, self.at(pl.ds(0, self.units), self.shard), self.local.at[1])

    def ring(self, e, d, k):
        return self.moved(e, self.sets[e], d, k, k, self.ways[d][0])

    def side(self, e, d, k):
        return self.moved(2 + e, self.sets[e], d, k + 1, k, self.sibling)

    def cross(self, d, k):
        return self.moved(4, self.mine, d, k + 1, k, self.across)

    def forward(self, d, k):
        return self.moved(5, self.theirs, d, k + 1, k, self.sibling)

    def vec_hop(self, k):
        here = self.vecs.at[self.shard_at(self.pos - k)]
        return remote(here, here, self.vec_sems[1].at[k], self.vec_sems[2].at[k], self.ways[0][0])

    def begin(self):
        per = self.units // len(self.ins)
        for i, ref in enumerate(self.ins):
            for j in range(per):
                if ref.shape[1] > self.width:
                    part = ref.at[:, pl.ds(j * self.width, self.width)]
                else:
                    part = ref.at[pl.ds(j * self.rows, self.rows), :]
                pltpu.make_async_copy(part, self.own.at[i * per + j], self.local.at[0]).start()
        if self.vec is not None:
            pltpu.make_async_copy(self.vec_in, self.vecs.at[self.shard], self.vec_sems[0].at[0]).start()
        if not self.follows:
            greet((self.ways[0][0], self.ways[1][0], self.sibling, self.across))
        pltpu.make_async_copy(self.own, self.own, self.local.at[0]).wait()
        for e in range(2):
            for d in range(2):
                self.first(e, d).start()
        self.stored().start()
        if self.vec is not None:
            pltpu.make_async_copy(self.vec_in, self.vecs.at[self.shard], self.vec_sems[0].at[0]).wait()

    def step(self, i):
        n = self.n
        pl.when(i == 0)(self.begin)

        for e in range(2):
            for d in range(2):

                @pl.when((i > 0) & (i < n))
                def _():
                    self.ring(e, d, i - 1).wait_recv()

                    @pl.when(i < n - 1)
                    def _():
                        self.ring(e, d, i).start()

                    if e == 0:
                        self.cross(d, i - 1).start()
                    self.side(e, d, i - 1).start()

        @pl.when((i > 1) & (i <= n))
        def _():
            for d in range(2):
                self.cross(d, i - 2).wait_recv()
                self.forward(d, i - 2).start()

        if self.vec is not None:
            @pl.when((i > 0) & (i < n))
            def _():
                self.vec_hop(i - 1).wait_recv()

            @pl.when(i < n - 1)
            def _():
                self.vec_hop(i).start()

    def finish(self, steps):
        n = self.n
        if steps <= n:
            for d in range(2):
                self.cross(d, n - 2).wait_recv()
                self.forward(d, n - 2).start()

        def drain(k, _):
            for d in range(2):
                for e in range(2):
                    self.ring(e, d, k).wait_send()
                    self.side(e, d, k).wait()
                self.cross(d, k).wait_send()
                self.forward(d, k).wait()
            if self.vec is not None:
                self.vec_hop(k).wait_send()
            return 0

        lax.fori_loop(0, n - 1, drain, 0)
        self.stored().wait()


class Chain:
    def __init__(self, first, second):
        self.first, self.second, self.n = first, second, first.n
        second.follows = True
        self.arrays = first.arrays + second.arrays
        self.out_shapes = first.out_shapes + second.out_shapes
        self.scratch = first.scratch + second.scratch

    def bind(self, ins, outs, scratch):
        a, b, c = len(self.first.arrays), len(self.first.out_shapes), len(self.first.scratch)
        self.first.bind(ins[:a], outs[:b], scratch[:c])
        self.second.bind(ins[a:], outs[b:], scratch[c:])

    def step(self, t):
        self.first.step(t)
        pl.when(t == self.n)(lambda: self.first.finish(self.n + 1))
        self.second.step(t - (self.n - 2))

    def finish(self, ticks):
        self.second.finish(ticks - (self.n - 2))


class Scatter:
    def __init__(self, n, sources, alone, vec=None, start=1, every=1):
        self.n, self.arrays = n, list(sources) + ([] if vec is None else [vec])
        self.vec, self.start, self.every = vec, start, every
        self.counts = [1 if s.ndim == 2 else s.shape[s.ndim - 3] for s in sources]
        self.kinds = [s.ndim for s in sources]
        units = self.units = sum(self.counts)
        self.ne, self.ns = alone, units - 2 * alone
        first = sources[0].shape
        rows = self.rows = first[-2] if len(first) == 4 else first[-2] // n
        width = self.width = sources[0].shape[-1]
        half, self.quarter = rows // 2, rows // 4
        self.out_shapes = [jax.ShapeDtypeStruct((units, rows, width), bf16)]
        dma = pltpu.SemaphoreType.DMA
        self.scratch = [
            pltpu.VMEM((units, n * half, width), bf16),
            pltpu.VMEM((units, n * half, width), bf16),
            pltpu.VMEM((alone, n * half, width), bf16),
            pltpu.VMEM((2, n - 1, alone, half // 2, width), bf16),
            pltpu.VMEM((2, n - 1, self.ns, half // 2, width), bf16),
            pltpu.VMEM((self.ns, half, width), bf16),
            pltpu.VMEM((alone, half, width), bf16),
            dma((2, n)), dma((2, n)), dma((2, n)), dma((2, n)), dma((2, n)),
            dma((2, n - 1)), dma((2, n - 1)), dma((2, n - 1)), dma((2, n - 1)),
            dma((2,)), dma((2,)), dma((3,)), dma((3,)), dma((3,)),
        ]
        if vec is not None:
            self.out_shapes.append(jax.ShapeDtypeStruct((8, rows), f32))
            self.scratch += [
                pltpu.VMEM((n, 8, rows), f32), pltpu.VMEM((n - 1, 8, rows), f32), pltpu.VMEM((4, 8, rows), f32),
                pltpu.VMEM((8, rows), f32), dma((2,)), dma((n - 1,)), dma((n - 1,)), dma((3,)), dma((3,)),
            ]

    def bind(self, ins, outs, scratch):
        self.ins, self.out = ins, outs[0]
        (self.near, self.beside, self.over, slots_e, slots_s, self.swap_s, self.swap_e, self.local, self.cs, self.cr,
         self.xs, self.xr, *ring_sems, self.ss, self.sr, self.os, self.orr, self.done) = scratch[:21]
        self.slots, self.ring_sems = (slots_e, slots_s), (ring_sems[:2], ring_sems[2:])
        if self.vec is not None:
            self.vec_in, self.vec_out, self.ins = ins[-1], outs[1], ins[:-1]
            (self.v_near, self.v_ring, self.v_all, self.v_sum, self.v_local, self.v_rs, self.v_rr,
             self.v_ss, self.v_sr) = scratch[21:]
        (self.x, self.c, self.shard, self.pos, self.shard_at, self.ways, self.sibling, self.across,
         self.corner) = neighbours(self.n)
        self.on_ring = self.ne + self.ns
        self.theirs = pl.ds((1 - self.x) * self.on_ring, self.ne)
        self.mine = pl.ds(self.x * self.on_ring, self.ne)
        self.shared = pl.ds(self.ne, self.ns)
        self.sets = (self.mine, self.shared)

    def owner(self, d, k):
        return self.shard_at(self.pos - self.ways[d][1] * (1 + k))

    def span(self, d, k):
        return block_of(self.owner(d, k) * 2 + d, self.quarter)

    def region(self, ref, d, k):
        return ref.at[:, self.span(d, k), :]

    def pieces(self, d, k, core, target):
        owner = self.owner(d, k)
        u = 0
        for ref, count, kind in zip(self.ins, self.counts, self.kinds):
            rows = block_of(owner * 4 + core * 2 + d, self.quarter)
            if kind == 4:
                src = ref.at[owner, :, block_of(core * 2 + d, self.quarter), :]
            else:
                src = ref.at[rows, :] if kind == 2 else ref.at[:, rows, :]
            units = u if kind == 2 else pl.ds(u, count)
            yield src, target.at[units, self.span(d, k), :]
            u += count

    def crossing(self, d, k):
        rows = self.span(d, k)
        return remote(
            self.near.at[self.theirs, rows, :], self.over.at[:, rows, :], self.xs.at[d, k], self.xr.at[d, k], self.across
        )

    def hop(self, e, d, k):
        src = self.near.at[self.sets[e], self.span(d, k), :]
        sent, got = self.ring_sems[e]
        return remote(src, self.slots[e].at[d, k], sent.at[d, k], got.at[d, k], self.ways[d][0])

    def vec_hop(self, k):
        return remote(self.v_near.at[self.owner(0, k)], self.v_ring.at[k], self.v_rs.at[k], self.v_rr.at[k], self.ways[0][0])

    def begin(self):
        n = self.n

        def loads(k, _):
            for d in range(2):
                for src, dst in self.pieces(d, k, self.c, self.near):
                    pltpu.make_async_copy(src, dst, self.local.at[d, k]).start()
            return 0

        lax.fori_loop(0, n, loads, 0)
        if self.vec is not None:
            for s in range(n):
                pltpu.make_async_copy(
                    self.vec_in.at[:, pl.ds(s * self.rows, self.rows)], self.v_near.at[s], self.v_local.at[0]
                ).start()
        greet((self.ways[0][0], self.ways[1][0], self.sibling, self.across) + (() if self.vec is None else (self.corner,)))

        def sends(k, _):
            for d in range(2):
                for src, dst in self.pieces(d, k, 1 - self.c, self.beside):
                    remote(src, dst, self.cs.at[d, k], self.cr.at[d, k], self.sibling).start()
            return 0

        lax.fori_loop(0, n, sends, 0)
        if self.vec is not None:
            pltpu.make_async_copy(self.v_near, self.v_near, self.v_local.at[0]).wait()

    def arrived(self, ref, ssem, rsem, d, k):
        here = self.region(ref, d, k)
        return remote(here, here, ssem.at[d, k], rsem.at[d, k], self.sibling)

    def pair(self, k):
        for d in range(2):
            rows = self.span(d, k)
            here = self.region(self.near, d, k)
            pltpu.make_async_copy(here, here, self.local.at[d, k]).wait()
            self.arrived(self.beside, self.cs, self.cr, d, k).wait_recv()

            def add(u, _):
                self.near[u, rows, :] = self.near[u, rows, :] + self.beside[u, rows, :]
                return 0

            lax.fori_loop(0, self.units, add, 0)
            self.crossing(d, k).start()

    def combine(self, k, later):
        for e in (1, 0):
            for d in range(2):
                rows = self.span(d, k)
                if later:
                    self.hop(e, d, k - 1).wait_recv()
                if e == 0:
                    self.crossing(d, k).wait_recv()

                def add_shared(i, _):
                    u = self.ne + i
                    self.near[u, rows, :] = self.near[u, rows, :] + self.slots[1][d, k - 1, i]
                    return 0

                def add_mine(i, _):
                    u = self.x * self.on_ring + i
                    value = self.near[u, rows, :].astype(f32) + self.over[i, rows, :].astype(f32)
                    if later:
                        value = value + self.slots[0][d, k - 1, i].astype(f32)
                    self.near[u, rows, :] = value.astype(bf16)
                    return 0

                if e == 0:
                    lax.fori_loop(0, self.ne, add_mine, 0)
                elif later:
                    lax.fori_loop(0, self.ns, add_shared, 0)

                @pl.when(k < self.n - 1)
                def _():
                    self.hop(e, d, k).start()

        if self.vec is not None:
            if later:
                self.vec_hop(k - 1).wait_recv()
                self.v_near[self.owner(0, k)] = self.v_near[self.owner(0, k)] + self.v_ring[k - 1]

            @pl.when(k < self.n - 1)
            def _():
                self.vec_hop(k).start()

    def step(self, t):
        n = self.n
        pl.when(t == 0)(self.begin)
        since = t - self.start
        if self.every > 1:
            k, on = (since + n * self.every) // self.every - n, lax.rem(since + n * self.every, self.every) == 0
        else:
            k, on = since, since >= 0

        @pl.when(since == 0)
        def _():
            self.pair(0)
            self.pair(1)
            self.combine(0, False)

        @pl.when(on & (k > 0) & (k < n))
        def _():
            self.combine(k, True)

        @pl.when(on & (k >= 0) & (k + 2 < n))
        def _():
            self.pair(k + 2)

        pl.when(since == (n - 1) * self.every)(self.exchange)
        pl.when(since == (n - 1) * self.every + max(2, self.every))(self.join)

    def swap(self, e):
        src = self.near.at[self.sets[e], block_of(self.shard, self.rows // 2), :]
        return remote(src, (self.swap_e, self.swap_s)[e], self.ss.at[e], self.sr.at[e], self.across)

    def result(self, j, away):
        half = block_of(self.c, self.rows // 2)
        src = (self.near.at[self.mine, block_of(self.shard, self.rows // 2), :], self.swap_s, self.swap_e)[j]
        dst = self.out.at[(self.mine, self.shared, self.theirs)[j], half, :]
        if away:
            return remote(src, dst, self.os.at[j], self.orr.at[j], self.sibling)
        return pltpu.make_async_copy(src, dst, self.done.at[j])

    def shares(self):
        sums, rep = self.v_near.at[self.shard], self.x * 2 + self.c
        return [
            remote(sums, self.v_all.at[rep], self.v_ss.at[j], self.v_sr.at[j], who)
            for j, who in enumerate((self.sibling, self.across, self.corner))
        ]

    def put(self, j):
        self.result(j, True).start()
        self.result(j, False).start()

    def exchange(self):
        self.swap(1).start()
        self.swap(0).start()
        self.put(0)
        if self.vec is not None:
            for copy in self.shares():
                copy.start()
            self.v_all[self.x * 2 + self.c] = self.v_near[self.shard]

    def join(self):
        at = block_of(self.shard, self.rows // 2)
        self.swap(1).wait_recv()

        def add(i, _):
            self.swap_s[i] = self.swap_s[i] + self.near[self.ne + i, at, :]
            return 0

        lax.fori_loop(0, self.ns, add, 0)
        self.put(1)
        self.swap(0).wait_recv()
        self.put(2)

    def finish(self, ticks):
        n = self.n
        last = self.start + (n - 1) * self.every
        assert ticks > last - self.every
        if ticks <= last:
            self.combine(n - 1, True)
            self.exchange()
        if ticks <= last + max(2, self.every):
            self.join()
        if self.vec is not None:
            for copy in self.shares():
                copy.wait()
            self.v_sum[...] = (self.v_all[0] + self.v_all[1]) + (self.v_all[2] + self.v_all[3])
            load(self.v_sum, self.vec_out, self.v_local.at[1]).wait()
        for j in range(3):
            self.result(j, False).wait()
            self.result(j, True).wait()
        for e in range(2):
            self.swap(e).wait_send()

        def drain(k, _):
            for d in range(2):
                self.arrived(self.beside, self.cs, self.cr, d, k).wait_send()
                self.crossing(d, k).wait_send()
            return 0

        lax.fori_loop(0, n, drain, 0)

        def drain_ring(k, _):
            for d in range(2):
                self.hop(0, d, k).wait_send()
                self.hop(1, d, k).wait_send()
            if self.vec is not None:
                self.vec_hop(k).wait_send()
            return 0

        lax.fori_loop(0, n - 1, drain_ring, 0)


def hosted(
    kernel, steps, args, in_specs, out_shapes, out_specs, scratch, name, carry=None, collective_id=None, done_by=None, ticks=1, vmem=58
):
    counts = [len(args), len(out_shapes), len(scratch)]
    extra = [0, 0, 0]
    params = dict(vmem_limit_bytes=vmem * MIB)
    if carry is not None:
        extra = [len(carry.arrays), len(carry.out_shapes), len(carry.scratch)]
        params.update(collective_id=collective_id, has_side_effects=True)

    def whole(*refs):
        main, other, first = [], [], 0
        for count, more in zip(counts, extra):
            main += refs[first : first + count]
            other.append(refs[first + count : first + count + more])
            first += count + more
        i = pl.program_id(0)

        def tick(j):
            if carry is not None:
                carry.step(i * ticks + j)

        if carry is not None:
            carry.bind(*other)
        if ticks == 1:
            tick(0)
            if done_by is not None:
                pl.when(i == done_by)(lambda: carry.finish(done_by + 1))
            if kernel is not None:
                kernel(*main)
        else:
            kernel(tick, *main)
        if carry is not None and done_by is None:
            pl.when(i == steps - 1)(lambda: carry.finish(steps * ticks))

    return pl.pallas_call(
        whole,
        grid=(steps,),
        out_shape=list(out_shapes) + (carry.out_shapes if carry else []),
        in_specs=list(in_specs) + [HBM] * extra[0],
        out_specs=list(out_specs) + [HBM] * extra[1],
        scratch_shapes=list(scratch) + (carry.scratch if carry else []),
        compiler_params=pltpu.CompilerParams(**params),
        name=name,
    )(*args, *(carry.arrays if carry else []))


def norm_forward(resid, gain, shift):
    mean = jnp.mean(resid, -1, keepdims=True)
    centred = resid - mean
    variance = jnp.mean(centred * centred, -1, keepdims=True)
    inverse = lax.rsqrt(variance + EPS)
    normed = centred * inverse
    return (normed * gain + shift, normed, inverse)


def norm_backward(grad_out, normed, inverse, gain):
    grad_gain = jnp.sum(grad_out * normed, 0, keepdims=True)
    grad_shift = jnp.sum(grad_out, 0, keepdims=True)
    grad_normed = grad_out * gain
    centre_term = jnp.mean(grad_normed, -1, keepdims=True)
    slope_term = jnp.mean(grad_normed * normed, -1, keepdims=True)
    return (inverse * (grad_normed - centre_term - normed * slope_term), grad_gain, grad_shift)


def fixed(a):
    zeros = (0,) * a.ndim
    return pl.BlockSpec(a.shape, lambda i: zeros, pipeline_mode=pl.Buffered(1))


def slices(rows, count):
    size = rows // count
    return [slice(j * size, (j + 1) * size) for j in range(count)]


def first_lanes(shape):
    return lax.broadcasted_iota(jnp.int32, shape, len(shape) - 1) < HD


def region_bias(starts_ref, region, size, transposed):
    first = region * size
    one = first + lax.broadcasted_iota(jnp.int32, (size, size), 0)
    two = first + lax.broadcasted_iota(jnp.int32, (size, size), 1)
    q_at, k_at = (two, one) if transposed else (one, two)
    start = starts_ref[0, region]
    q_in = (q_at >= start) & (q_at < start + PIC)
    k_in = (k_at >= start) & (k_at < start + PIC)
    return jnp.where((k_at <= q_at) | (q_in & k_in), 0.0, NEGATIVE)


def self_forward_kernel(regions, lead, scale, carry, starts_ref, x_ref, *refs):
    refs = list(refs)
    w_ref = refs.pop(0) if carry is None else carry.first.full
    q_ref, k_ref, v_ref, o_ref, lse_ref, bias_ref, w_buf, sems = refs
    rows, size = x_ref.shape[0], x_ref.shape[0] // regions
    i = pl.program_id(0)
    j = i - lead
    pairs = pl.num_programs(0) - lead

    @pl.when(i == 0)
    def _():
        for r in range(regions):
            bias_ref[r] = region_bias(starts_ref, r, size, False)

    def fetch(pair, slot):
        return pltpu.make_async_copy(w_ref.at[:, :, block_of(pair, 2 * HD)], w_buf.at[slot], sems.at[slot])

    @pl.when(j == 0)
    def _():
        fetch(0, 0).start()

    @pl.when(j >= 0)
    def _():
        slot = lax.rem(i - lead + 2, 2)

        @pl.when(j + 1 < pairs)
        def _():
            fetch(j + 1, 1 - slot).start()

        fetch(j, slot).wait()
        made = dot(x_ref[...], jnp.concatenate([w_buf[slot, u] for u in range(3)], 1))
        q_ref[...] = (made[:, : 2 * HD] * scale).astype(bf16)
        k_ref[...] = made[:, 2 * HD : 4 * HD].astype(bf16)
        v_ref[...] = made[:, 4 * HD :].astype(bf16)
        low = first_lanes((1, 2 * HD))
        outs, lses = [[], []], [[], []]
        for h in range(2):
            keys = jnp.where(low if h == 0 else ~low, k_ref[...], jnp.zeros((), bf16))
            for r in range(regions):
                span = slice(r * size, (r + 1) * size)
                q = q_ref[span, :]
                scores = []
                if r:
                    scores.append((dot(q, keys[: r * size], 1, 1), v_ref[: r * size, :]))
                scores.append((dot(q, keys[span], 1, 1) + bias_ref[r], v_ref[span, :]))
                top = functools.reduce(jnp.maximum, [jnp.max(s, -1, keepdims=True) for s, _ in scores])
                total, mixed = 0.0, 0.0
                for s, v in scores:
                    e = jnp.exp(s - top)
                    total = total + jnp.sum(e, -1, keepdims=True)
                    mixed = mixed + dot(e.astype(bf16), v)
                outs[h].append(mixed / total)
                lses[h].append(top + jnp.log(total))
        for r in range(regions):
            span = slice(r * size, (r + 1) * size)
            o_ref[span, :] = jnp.where(low, outs[0][r], outs[1][r]).astype(bf16)
            turned = jnp.where(low, lses[0][r], lses[1][r]).T
            lse_ref[0, 0:1, span] = turned[0:1]
            lse_ref[0, 1:2, span] = turned[HD : HD + 1]


def self_forward(states, weights, starts, scale, carry, collective_id):
    rows, width = states.shape
    regions = starts.shape[1]
    size = rows // regions
    pairs = width // (2 * HD)
    lead = 0 if carry is None else carry.n
    args, specs = [starts, states], [pl.BlockSpec(memory_space=pltpu.SMEM), fixed(states)]
    if carry is None:
        args.append(weights)
        specs.append(HBM)
    column = pl.BlockSpec((rows, 2 * HD), lambda i: (0, jnp.maximum(i - lead, 0)))
    return hosted(
        functools.partial(self_forward_kernel, regions, lead, scale, carry), lead + pairs, args, specs,
        [jax.ShapeDtypeStruct((rows, width), bf16)] * 4 + [jax.ShapeDtypeStruct((pairs, 8, rows), f32)],
        [column] * 4 + [pl.BlockSpec((1, 8, rows), lambda i: (jnp.maximum(i - lead, 0), 0, 0))],
        [pltpu.VMEM((regions, size, size), f32), pltpu.VMEM((2, 3, width, 2 * HD), bf16), pltpu.SemaphoreType.DMA((2,))],
        "self_forward", carry, collective_id,
    )


def self_backward_kernel(
    regions, scale, pairs, starts_ref, q_ref, k_ref, v_ref, g_ref, o_ref, lse_ref, x_ref, w_ref, resid_ref,
    g_query_ref, g_key_ref, g_value_ref, grad_ref, bias_ref, grads,
):
    rows, width = x_ref.shape
    size = rows // regions
    i = pl.program_id(0)
    spans = slices(rows, regions)
    low = first_lanes((1, 2 * HD))

    @pl.when(i == 0)
    def _():
        for r in range(regions):
            bias_ref[r] = region_bias(starts_ref, r, size, True)

    @pl.when(i < pairs)
    def _():
        product = g_ref[...].astype(f32) * o_ref[...].astype(f32)
        chooser = lax.broadcasted_iota(jnp.int32, (8, 2 * HD), 0)
        chooser = ((chooser == 0) & first_lanes((8, 2 * HD))) | ((chooser == 1) & ~first_lanes((8, 2 * HD)))
        chooser = chooser.astype(f32).astype(bf16)
        upper = product.astype(bf16)
        lower = (product - upper.astype(f32)).astype(bf16)
        deltas = dot(chooser, upper, 1, 1) + dot(chooser, lower, 1, 1)
        gq, gk, gv = {}, {}, {}
        for h in range(2):
            pick = low if h == 0 else ~low
            zero = jnp.zeros((), bf16)
            keys = jnp.where(pick, k_ref[...], zero)
            values = jnp.where(pick, v_ref[...], zero)
            for r, span in enumerate(spans):
                q, g = q_ref[span, :], g_ref[span, :]
                lse = lse_ref[0, h : h + 1, span]
                delta = deltas[h : h + 1, span]
                for j, keyed in enumerate(spans[: r + 1]):
                    scores = dot(keys[keyed], q, 1, 1)
                    if j == r:
                        scores = scores + bias_ref[r]
                    probs = jnp.exp(scores - lse)
                    grad_probs = dot(values[keyed], g, 1, 1)
                    grad_scores = (probs * (grad_probs - delta)).astype(bf16)
                    gv[h, j] = gv.get((h, j), 0.0) + dot(probs.astype(bf16), g)
                    gk[h, j] = gk.get((h, j), 0.0) + dot(grad_scores, q)
                    gq[h, r] = gq.get((h, r), 0.0) + dot(grad_scores, k_ref[keyed, :], 0, 0)
        cols = block_of(i, 2 * HD)
        for r, span in enumerate(spans):
            grads[0, span, cols] = jnp.where(low, gq[0, r], gq[1, r]).astype(bf16) * scale
            grads[1, span, cols] = jnp.where(low, gk[0, r], gk[1, r]).astype(bf16)
            grads[2, span, cols] = jnp.where(low, gv[0, r], gv[1, r]).astype(bf16)

    for u, out in enumerate((g_query_ref, g_key_ref, g_value_ref)):

        @pl.when(i == pairs + u)
        def _():
            for span in slices(width, 4):
                out[span, :] = dot(x_ref[:, span], grads[u], 0, 0).astype(bf16)

    @pl.when(i >= pairs + 3)
    def _():
        at = block_of(i - pairs - 3, grad_ref.shape[0])
        total = resid_ref[...]
        for u in range(3):
            total = total + dot(grads[u, at, :], w_ref[u], 1, 1)
        grad_ref[...] = total


def self_backward(q, k, v, g, o, lse, starts, states, weights, resid, scale, carry, collective_id):
    rows, width = q.shape
    regions = starts.shape[1]
    size = rows // regions
    pairs, parts = width // (2 * HD), 4
    last = pairs - 1
    column = pl.BlockSpec((rows, 2 * HD), lambda i: (0, jnp.minimum(i, last)))
    some = pl.BlockSpec((rows // parts, width), lambda i: (jnp.maximum(i - pairs - 3, 0), 0))
    square = jax.ShapeDtypeStruct((width, width), bf16)
    return hosted(
        functools.partial(self_backward_kernel, regions, scale, pairs), pairs + 3 + parts,
        [starts, q, k, v, g, o, lse, states, weights, resid],
        [pl.BlockSpec(memory_space=pltpu.SMEM)] + [column] * 5
        + [pl.BlockSpec((1, 8, rows), lambda i: (jnp.minimum(i, last), 0, 0)), fixed(states), fixed(weights), some],
        [square] * 3 + [jax.ShapeDtypeStruct((rows, width), f32)], [fixed(square)] * 3 + [some],
        [pltpu.VMEM((regions, size, size), f32), pltpu.VMEM((3, rows, width), bf16)],
        "self_backward", carry, collective_id, vmem=60,
    )


def cross_forward_kernel(
    scale, tick, x_ref, mixed_in, enc_ref, w_ref, vec_ref, low_ref, n1_ref, i1_ref, q_ref, k_ref, v_ref, mixed_ref,
    lse_ref, two_ref, n2_ref, i2_ref, low_two_ref,
):
    tick(0)

    @pl.when(pl.program_id(0) == 0)
    def _():
        k_ref[...] = dot(enc_ref[...], w_ref[2]).astype(bf16)
        v_ref[...] = dot(enc_ref[...], w_ref[3]).astype(bf16)

    one, n1_ref[...], i1_ref[...] = norm_forward(
        x_ref[...].astype(f32) + dot(mixed_in[...], w_ref[0]), vec_ref[0:1, :], vec_ref[1:2, :]
    )
    low_ref[...] = one.astype(bf16)
    q_ref[...] = (dot(low_ref[...], w_ref[1]) * scale).astype(bf16)
    rows, width = x_ref.shape
    low = first_lanes((1, 2 * HD))
    lane = lax.broadcasted_iota(jnp.int32, (1, 2 * HD), 1)
    lses = jnp.zeros((rows, 2 * HD), f32)
    for pair in range(width // (2 * HD)):
        if pair == 2:
            tick(1)
        cols = slice(pair * 2 * HD, (pair + 1) * 2 * HD)
        parts = []
        for h in range(2):
            keys = jnp.where(low if h == 0 else ~low, k_ref[:, cols], jnp.zeros((), bf16))
            scores = dot(q_ref[:, cols], keys, 1, 1)
            top = jnp.max(scores, -1, keepdims=True)
            e = jnp.exp(scores - top)
            total = jnp.sum(e, -1, keepdims=True)
            parts.append(dot(e.astype(bf16), v_ref[:, cols]) / total)
            lses = jnp.where(lane == 8 * pair + h, top + jnp.log(total), lses)
        mixed_ref[:, cols] = jnp.where(low, *parts).astype(bf16)
    lse_ref[...] = lses.T[: lse_ref.shape[0]]
    two, n2_ref[...], i2_ref[...] = norm_forward(one + dot(mixed_ref[...], w_ref[4]), vec_ref[2:3, :], vec_ref[3:4, :])
    two_ref[...] = two
    low_two_ref[...] = two.astype(bf16)


def cross_forward(states, mixed, encoded, weights, vecs, scale, carry, collective_id):
    rows, width = states.shape
    steps = 4
    block = pl.BlockSpec((rows // steps, width), lambda i: (i, 0))
    thin = pl.BlockSpec((rows // steps, 1), lambda i: (i, 0))
    heads = width // HD * 4
    tall = lambda kind: jax.ShapeDtypeStruct((rows, width), kind)
    column = jax.ShapeDtypeStruct((rows, 1), f32)
    outs = [
        (tall(bf16), block), (tall(f32), block), (column, thin), (tall(bf16), block), (encoded, fixed(encoded)),
        (encoded, fixed(encoded)), (tall(bf16), block),
        (jax.ShapeDtypeStruct((heads, rows), f32), pl.BlockSpec((heads, rows // steps), lambda i: (0, i))),
        (tall(f32), block), (tall(f32), block), (column, thin), (tall(bf16), block),
    ]
    return hosted(
        functools.partial(cross_forward_kernel, scale), steps, [states, mixed, encoded, weights, vecs],
        [block, block, fixed(encoded), fixed(weights), fixed(vecs)],
        [jax.ShapeDtypeStruct(o.shape, o.dtype) for o, _ in outs], [spec for _, spec in outs], [],
        "cross_forward", carry, collective_id, ticks=2,
    )


def cross_backward_kernel(
    scale, pairs, parts, b2_ref, mixed_ref, low_ref, mixed_one_ref, q_ref, lse_ref, k_ref, v_ref, w_ref, vec_ref, g2_ref,
    n1_ref, i1_ref, g_out_ref, g_query_ref, g_self_out_ref, gk_ref, gv_ref, g1_ref, gm_ref, sums_ref,
    g_mixed, gq_all, b1_all,
):
    i = pl.program_id(0)
    rows, width = b2_ref.shape

    @pl.when(i == 0)
    def _():
        for span in slices(rows, 4):
            g_mixed[span, :] = dot(b2_ref[span, :], w_ref[4], 1, 1).astype(bf16)
        sums_ref[...] = jnp.zeros_like(sums_ref)

    j = i - 1

    @pl.when((j >= 0) & (j < pairs))
    def _():
        cols = block_of(j, 2 * HD)
        low = first_lanes((1, 2 * HD))
        chooser = lax.broadcasted_iota(jnp.int32, (8, 2 * HD), 0)
        chooser = ((chooser == 0) & first_lanes((8, 2 * HD))) | ((chooser == 1) & ~first_lanes((8, 2 * HD)))
        chooser = chooser.astype(f32).astype(bf16)
        gks, gvs = [0.0, 0.0], [0.0, 0.0]
        for span in slices(rows, 2):
            g, q = g_mixed[span, cols], q_ref[span, :]
            product = g.astype(f32) * mixed_ref[span, cols].astype(f32)
            upper = product.astype(bf16)
            lower = (product - upper.astype(f32)).astype(bf16)
            deltas = dot(chooser, upper, 1, 1) + dot(chooser, lower, 1, 1)
            gqs = []
            for h in range(2):
                pick = low if h == 0 else ~low
                keys = jnp.where(pick, k_ref[...], jnp.zeros((), bf16))
                values = jnp.where(pick, v_ref[...], jnp.zeros((), bf16))
                probs = jnp.exp(dot(keys, q, 1, 1) - lse_ref[h : h + 1, span])
                grad_scores = (probs * (dot(values, g, 1, 1) - deltas[h : h + 1, :])).astype(bf16)
                gvs[h] = gvs[h] + dot(probs.astype(bf16), g)
                gks[h] = gks[h] + dot(grad_scores, q)
                gqs.append(dot(grad_scores, k_ref[...], 0, 0))
            gq_all[span, cols] = jnp.where(low, *gqs).astype(bf16) * scale
        gk_ref[...] = jnp.where(low, *gks).astype(bf16)
        gv_ref[...] = jnp.where(low, *gvs).astype(bf16)

    m = j - pairs

    @pl.when((m >= 0) & (m < parts))
    def _():
        at = block_of(m, rows // parts)
        grad_one = g2_ref[...] + dot(gq_all[at, :], w_ref[1], 1, 1)
        grad, g_gain, g_shift = norm_backward(grad_one, n1_ref[...], i1_ref[...], vec_ref[0:1, :])
        sums_ref[0:1, :] += g_gain
        sums_ref[1:2, :] += g_shift
        g1_ref[...] = grad
        b1_all[at, :] = grad.astype(bf16)
        gm_ref[...] = dot(b1_all[at, :], w_ref[0], 1, 1).astype(bf16)

    for u, (left, right, out) in enumerate(
        ((mixed_ref, b2_ref, g_out_ref), (low_ref, gq_all, g_query_ref), (mixed_one_ref, b1_all, g_self_out_ref))
    ):

        @pl.when(m == parts + u)
        def _():
            for span in slices(width, 4):
                out[span, :] = dot(left[:, span], right[...], 0, 0).astype(bf16)


def cross_backward(
    branch, mixed, low, mixed_one, grad, normed, inverse, q, lse, k, v, weights, vecs, scale, carry, collective_id
):
    rows, width = q.shape
    pairs, parts = width // (2 * HD), 4
    column = lambda a: pl.BlockSpec((a.shape[0], 2 * HD), lambda i: (0, jnp.clip(i - 1, 0, pairs - 1)))
    some = lambda cols: pl.BlockSpec((rows // parts, cols), lambda i: (jnp.clip(i - 1 - pairs, 0, parts - 1), 0))
    square = jax.ShapeDtypeStruct((width, width), bf16)
    outs = [
        (square, fixed(square)), (square, fixed(square)), (square, fixed(square)), (k, column(k)), (v, column(v)),
        (grad, some(width)), (q, some(width)), (vecs, fixed(vecs)),
    ]
    args = [branch, mixed, low, mixed_one, q, lse, k, v, weights, vecs, grad, normed, inverse]
    lse_spec = pl.BlockSpec((8, rows), lambda i: (jnp.clip(i - 1, 0, pairs - 1), 0))
    return hosted(
        functools.partial(cross_backward_kernel, scale, pairs, parts), 1 + pairs + parts + 3, args,
        [fixed(a) for a in args[:4]] + [column(q), lse_spec, column(k), column(v), fixed(weights), fixed(vecs)]
        + [some(width), some(width), some(1)],
        [jax.ShapeDtypeStruct(o.shape, o.dtype) for o, _ in outs], [spec for _, spec in outs],
        [pltpu.VMEM((rows, width), bf16)] * 3, "cross_backward", carry, collective_id, vmem=60,
    )


def ffn_forward_kernel(blocks, carry, low_ref, two_ref, cot_ref, vec_ref, w1_ref, *refs):
    refs = list(refs)
    w2_ref = refs.pop(0) if carry is None else carry.full
    final_ref, branch_ref, grad_ref, slope_ref, g_contract_ref, sums_ref, acts, acc, w2_buf, sems = refs
    i = pl.program_id(0)
    spans = slices(low_ref.shape[0], 4)

    @pl.when(i < blocks)
    def _():
        for span in spans:
            pre = dot(low_ref[span, :], w1_ref[0])
            phi = 0.5 * (1.0 + lax.erf(pre * INV_ROOT_TWO))
            acts[i, span, :] = (pre * phi).astype(bf16)
            slope_ref[span, :] = (phi + pre * jnp.exp(-0.5 * pre * pre) * INV_ROOT_TWO_PI).astype(bf16)

    j = i - blocks

    def fetch(block, slot):
        return pltpu.make_async_copy(w2_ref.at[block], w2_buf.at[slot], sems.at[slot])

    @pl.when(j == 0)
    def _():
        fetch(0, 0).start()
        acc[...] = two_ref[...]

    @pl.when((j >= 0) & (j < blocks))
    def _():
        slot = lax.rem(j + blocks * 2, 2)

        @pl.when(j + 1 < blocks)
        def _():
            fetch(j + 1, 1 - slot).start()

        fetch(j, slot).wait()
        w2 = w2_buf[slot].reshape(-1, w2_buf.shape[-1])
        for span in spans:
            acc[span, :] += dot(acts[j, span, :], w2)

    @pl.when(j == blocks - 1)
    def _():
        gain, shift = vec_ref[4:5, :], vec_ref[5:6, :]
        sums = [0.0, 0.0]
        for span in slices(low_ref.shape[0], 8):
            final, normed, inverse = norm_forward(acc[span, :], gain, shift)
            final_ref[span, :] = final.astype(bf16)
            grad, *parts = norm_backward(cot_ref[span, :].astype(f32), normed, inverse, gain)
            grad_ref[span, :] = grad
            branch_ref[span, :] = grad.astype(bf16)
            sums = [a + b for a, b in zip(sums, parts)]
        sums_ref[...] = jnp.zeros_like(sums_ref)
        sums_ref[0:1, :] = sums[0]
        sums_ref[1:2, :] = sums[1]

    @pl.when(j >= blocks)
    def _():
        made = dot(acts[j - blocks], branch_ref[...], 0, 0).astype(bf16)
        g_contract_ref[0] = made.reshape(g_contract_ref.shape[1:])


def ffn_forward(low, two, cotangent, vecs, w1, w2, carry, collective_id):
    rows, width = low.shape
    if carry is not None:
        blocks, size = carry.n, carry.units * carry.rows
    else:
        blocks, size = w2.shape[0], w2.shape[1] * w2.shape[2]
    per = width // size
    last = blocks - 1
    args = [low, two, cotangent, vecs, w1]
    specs = [fixed(a) for a in args[:4]]
    specs.append(pl.BlockSpec((1, width, size), lambda i: (jnp.minimum(i, last) // per, 0, lax.rem(jnp.minimum(i, last), per))))
    if carry is None:
        args.append(w2)
        specs.append(HBM)
    tall = jax.ShapeDtypeStruct((rows, blocks * size), bf16)
    part = w2.shape[1:] if carry is None else (carry.units, carry.rows, width)
    outs = [low, low, two, tall, jax.ShapeDtypeStruct((blocks,) + part, bf16), jax.ShapeDtypeStruct((8, width), f32)]
    out_specs = [fixed(a) for a in outs[:3]]
    out_specs.append(pl.BlockSpec((rows, size), lambda i: (0, jnp.minimum(i, last))))
    out_specs.append(pl.BlockSpec((1,) + part, lambda i: (jnp.maximum(i - 2 * blocks, 0), 0, 0, 0)))
    out_specs.append(fixed(outs[5]))
    return hosted(
        functools.partial(ffn_forward_kernel, blocks, carry), 3 * blocks, args, specs,
        [jax.ShapeDtypeStruct(a.shape, a.dtype) for a in outs], out_specs,
        [
            pltpu.VMEM((blocks, rows, size), bf16), pltpu.VMEM((rows, width), f32),
            pltpu.VMEM((2,) + part, bf16), pltpu.SemaphoreType.DMA((2,)),
        ],
        "ffn_forward", carry, collective_id, done_by=blocks if carry else None, vmem=60,
    )


def ffn_backward_kernel(
    blocks, low_ref, branch_ref, vec_ref, w1_ref, w2_ref, slope_ref, normed_ref, inverse_ref, g_ref,
    g_expand_ref, grad_ref, branch_two_ref, sums_ref, turned, acc, g_pre, sem,
):
    i = pl.program_id(0)
    rows = low_ref.shape[0]
    spans = slices(rows, 4)
    start = pltpu.make_async_copy(g_ref, acc, sem.at[0])

    @pl.when(i == 0)
    def _():
        start.start()
        turned[...] = low_ref[...].T
        sums_ref[...] = jnp.zeros_like(sums_ref)

    @pl.when(i < blocks)
    def _():
        w2 = w2_ref[0].reshape(-1, w2_ref.shape[-1])
        for span in spans:
            g_pre[span, :] = (dot(branch_ref[span, :], w2, 1, 1) * slope_ref[span, :].astype(f32)).astype(bf16)
        for span in slices(turned.shape[0], 4):
            g_expand_ref[0, span, :] = dot(turned[span, :], g_pre[...]).astype(bf16)
        pl.when(i == 0)(start.wait)
        for span in spans:
            acc[span, :] += dot(g_pre[span, :], w1_ref[0], 1, 1)

    @pl.when(i >= blocks)
    def _():
        at = block_of(i - blocks, grad_ref.shape[0])
        grad, g_gain, g_shift = norm_backward(acc[at, :], normed_ref[...], inverse_ref[...], vec_ref[2:3, :])
        grad_ref[...] = grad
        branch_two_ref[...] = grad.astype(bf16)
        sums_ref[0:1, :] += g_gain
        sums_ref[1:2, :] += g_shift


def ffn_backward(low, branch, grad, normed, inverse, vecs, w1, w2, slope, carry, collective_id):
    rows, width = low.shape
    blocks, size = w2.shape[0], w2.shape[1] * w2.shape[2]
    per, last, parts = width // size, w2.shape[0] - 1, 4
    wide = pl.BlockSpec((1, width, size), lambda i: (jnp.minimum(i, last) // per, 0, lax.rem(jnp.minimum(i, last), per)))
    deep = pl.BlockSpec((1,) + w2.shape[1:], lambda i: (jnp.minimum(i, last), 0, 0, 0))
    column = pl.BlockSpec((rows, size), lambda i: (0, jnp.minimum(i, last)))
    some = lambda cols: pl.BlockSpec((rows // parts, cols), lambda i: (jnp.maximum(i - blocks, 0), 0))
    args = [low, branch, vecs, w1, w2, slope, normed, inverse, grad]
    outs = [w1, grad, low, vecs]
    return hosted(
        functools.partial(ffn_backward_kernel, blocks), blocks + parts, args,
        [fixed(a) for a in args[:3]] + [wide, deep, column, some(width), some(1), HBM],
        [jax.ShapeDtypeStruct(a.shape, a.dtype) for a in outs], [wide, some(width), some(width), fixed(vecs)],
        [
            pltpu.VMEM((width, rows), bf16), pltpu.VMEM((rows, width), f32), pltpu.VMEM((rows, size), bf16),
            pltpu.SemaphoreType.DMA((1,)),
        ],
        "ffn_backward", carry, collective_id, vmem=60,
    )


def body(n, states, encoded, starts, cotangent, *weights):
    matrices, vectors = weights[:10], weights[10:]
    expand, contract = matrices[8], matrices[9]
    rows, width = matrices[0].shape
    blocks = contract.shape[0] // rows
    scale = HD ** (-0.5)
    small = n <= 16
    vec = jnp.zeros((16, max(rows, 128)), bf16).at[: len(vectors), :rows].set(jnp.stack(vectors))
    take = lambda shards, units, alone, **more: Gather(n, width, shards, units, alone, **more) if small else None
    if small:
        chain = Chain(take(matrices[:3], 3, 1, vec=vec), take(matrices[3:8], 5, 2))
        q_self, k_self, v_self, mixed_self, lse_self, first, vecs, second = self_forward(states, None, starts, scale, chain, 0)
    else:
        first = lax.all_gather(jnp.stack(matrices[:3]), "shard", axis=1, tiled=True)
        vecs = lax.all_gather(vec, "shard", axis=0)
        second = lax.all_gather(jnp.stack(matrices[3:8]), "shard", axis=1, tiled=True)
        q_self, k_self, v_self, mixed_self, lse_self = self_forward(states, first, starts, scale, None, None)
    vecs = vecs[:, : len(vectors), :rows].transpose(1, 0, 2).reshape(len(vectors), width).astype(f32)
    vecs = jnp.concatenate([vecs, jnp.zeros((2, width), f32)])
    (one_low, normed_one, inverse_one, q_cross, k_cross, v_cross, mixed_cross, lse_cross, hidden_two, normed_two, inverse_two,
     two_low, *third) = cross_forward(states, mixed_self, encoded, second, vecs, scale, take([expand], blocks, 1), 2)
    if not small:
        third = [lax.all_gather(expand.reshape(rows, blocks, width).transpose(1, 0, 2), "shard", axis=1, tiled=True)]
    w1 = third[0]
    w2 = None
    if not small:
        w2 = lax.all_gather(contract, "shard", axis=0, tiled=True).reshape(8, 4, -1, width)
    final, branch_three, grad_three, slope, g_contract, sums_three, *fourth = ffn_forward(
        two_low, hidden_two, cotangent, vecs, w1, w2, take([contract], blocks, 1, owner_first=True), 3
    )
    if small:
        w2 = fourth[0]

    give = lambda sources, alone, **more: Scatter(n, sources, alone, **more) if small else None
    g_expand, grad_resid_two, branch_two, sums_two, *own_contract = ffn_backward(
        two_low, branch_three, grad_three, normed_two, inverse_two, vecs, w1, w2, slope, give([g_contract], 1), 4
    )
    g_cross_out, g_cross_query, g_self_out, g_k, g_v, grad_resid_one, grad_mixed, sums_one, *own_expand = cross_backward(
        branch_two, mixed_cross, one_low, mixed_self, grad_resid_two, normed_one, inverse_one, q_cross, lse_cross, k_cross,
        v_cross, second, vecs, scale, give([g_expand], 1, start=1, every=2), 5
    )
    g_cross = [g_cross_query, dot(encoded, g_k, 0, 0).astype(bf16), dot(encoded, g_v, 0, 0).astype(bf16), g_cross_out]
    grad_encoded = dot(g_k, second[2], 1, 1) + dot(g_v, second[3], 1, 1)
    g_query, g_key, g_value, grad_states, *own_middle = self_backward(
        q_self, k_self, v_self, grad_mixed, mixed_self, lse_self, starts, states, first, grad_resid_one, scale,
        give([*g_cross, g_self_out], 1), 6
    )
    g_self = [g_query, g_key, g_value]
    grads_vec = jnp.concatenate([sums_one[:2], sums_two[:2], sums_three[:2], jnp.zeros((2, width), f32)])
    if small:
        own_self, own_vec = hosted(None, n + 3, [], [], [], [], [], "scatter_last", give(g_self, 1, vec=grads_vec), 7)
        own_contract, own_expand, own_middle = own_contract[0], own_expand[0], own_middle[0]
    else:
        total = lambda g: lax.psum(lax.psum_scatter(g, "shard", scatter_dimension=1, tiled=True), "rep")
        own_self = total(jnp.stack(g_self))
        own_middle = total(jnp.stack([*g_cross, g_self_out]))
        own_expand = total(g_expand)
        own_contract = total(g_contract.reshape(1, -1, width))
        own_vec = lax.dynamic_slice_in_dim(
            lax.psum(grads_vec, ("rep", "shard")), lax.axis_index("shard") * rows, rows, 1
        )
    own_contract = own_contract.reshape(blocks * rows, width).astype(f32)
    own_expand = jnp.concatenate([own_expand[j] for j in range(blocks)], 1).astype(f32)
    attention = [own_self[0], own_self[1], own_self[2], own_middle[4]] + [own_middle[j] for j in range(4)]
    return (
        final,
        grad_states,
        grad_encoded,
        *[g.astype(f32) for g in attention],
        own_expand,
        own_contract,
        *[own_vec[i] for i in range(6)],
    )


def solution(mesh):
    many, few = P(("rep", "shard"), None), P("shard", None)
    return jax.shard_map(
        functools.partial(body, mesh.shape["shard"]),
        mesh=mesh,
        in_specs=(many,) * 4 + (few,) * 10 + (P("shard"),) * 6,
        out_specs=(many,) * 3 + (few,) * 10 + (P("shard"),) * 6,
        check_vma=False,
    )
```

```python
import functools

import jax
import jax.numpy as jnp
from jax import lax
from jax.experimental import pallas as pl
from jax.experimental.pallas import tpu as pltpu
from jax.sharding import PartitionSpec as P

HD = 64
PIC = 256
EPS = 1e-05
NEGATIVE = -1e30
INV_ROOT_TWO = 0.7071067811865476
INV_ROOT_TWO_PI = 0.3989422804014327
MESH = pl.DeviceIdType.MESH
MIB = 1 << 20
HBM = pl.BlockSpec(memory_space=pltpu.HBM)
bf16 = jnp.bfloat16
f32 = jnp.float32


def dot(a, b, ca=1, cb=0):
    return lax.dot_general(a, b, (((ca,), (cb,)), ((), ())), preferred_element_type=f32)


def place(n):
    half = n // 2

    def shard_at(pos):
        pos = lax.rem(pos + 2 * n, n)
        back = pos // half
        return (1 - back) * 2 * pos + back * (2 * (n - 1 - pos) + 1)

    s = lax.axis_index("shard")
    odd = s % 2
    pos = (1 - odd) * (s // 2) + odd * (n - 1 - s // 2)
    return pos, shard_at


def greet(partners):
    barrier = pltpu.get_barrier_semaphore()
    for who in partners:
        pl.semaphore_signal(barrier, inc=1, device_id=who, device_id_type=MESH)
    pl.semaphore_wait(barrier, len(partners))


def send(src, dst, ssem, rsem, who):
    copy = pltpu.make_async_remote_copy(
        src_ref=src, dst_ref=dst, send_sem=ssem, recv_sem=rsem, device_id=who, device_id_type=MESH
    )
    copy.start()
    return copy


def load(src, dst, sem):
    copy = pltpu.make_async_copy(src, dst, sem)
    copy.start()
    return copy


def neighbours(n):
    rep, shard = lax.axis_index("rep"), lax.axis_index("shard")
    x, c = rep // 2, rep % 2
    pos, shard_at = place(n)
    ways = (((rep, shard_at(pos + 1)), 1), ((rep, shard_at(pos - 1)), -1))
    sibling, across, corner = (x * 2 + 1 - c, shard), ((1 - x) * 2 + c, shard), ((1 - x) * 2 + 1 - c, shard)
    return x, c, shard, pos, shard_at, ways, sibling, across, corner


def remote(src, dst, ssem, rsem, who):
    return pltpu.make_async_remote_copy(
        src_ref=src, dst_ref=dst, send_sem=ssem, recv_sem=rsem, device_id=who, device_id_type=MESH
    )


def block_of(index, size):
    return pl.ds(pl.multiple_of(index * size, size), size)


class Gather:
    def __init__(self, n, width, shards, units, alone, owner_first=False, vec=None):
        self.n, self.shards, self.owner_first, self.vec, self.follows = n, shards, owner_first, vec, False
        self.units, self.ne, self.ns = units, alone, units - 2 * alone
        self.rows, self.width = sum(s.size for s in shards) // (units * width), width
        self.arrays = list(shards) + ([] if vec is None else [vec])
        shape = (n, units, self.rows, self.width) if owner_first else (units, n * self.rows, self.width)
        self.out_shapes = [jax.ShapeDtypeStruct(shape, bf16)]
        dma = pltpu.SemaphoreType.DMA
        self.scratch = [pltpu.VMEM((units, self.rows, width), bf16), dma((2,)), dma((6, 2)), dma((3, 2))]
        self.scratch += [dma((2, n - 1))] * 3
        if vec is not None:
            self.out_shapes.append(jax.ShapeDtypeStruct((n,) + vec.shape, vec.dtype))
            self.scratch += [dma((1,)), dma((n - 1,)), dma((n - 1,))]

    def bind(self, ins, outs, scratch):
        self.ins, self.full = ins, outs[0]
        self.own, self.local, self.sent, self.got, *self.came = scratch[:7]
        if self.vec is not None:
            self.vec_in, self.vecs, self.vec_sems = ins[-1], outs[1], scratch[7:]
            self.ins = ins[:-1]
        (self.x, self.c, self.shard, self.pos, self.shard_at, self.ways, self.sibling, self.across, _) = neighbours(self.n)
        on_ring = self.ne + self.ns
        self.mine = pl.ds(self.x * on_ring, self.ne)
        self.sets = (self.mine, pl.ds(self.ne, self.ns))
        self.theirs = pl.ds((1 - self.x) * on_ring, self.ne)

    def at(self, units, owner):
        if self.owner_first:
            return self.full.at[owner, units]
        return self.full.at[units, block_of(owner, self.rows), :]

    def spot(self, units, d, k):
        owner = self.shard_at(self.pos - self.ways[d][1] * k)
        quarter = self.rows // 4
        if self.owner_first:
            return self.full.at[owner, units, block_of(self.c * 2 + d, quarter), :]
        return self.full.at[units, block_of(owner * 4 + self.c * 2 + d, quarter), :]

    def moved(self, kind, units, d, k, hop, who):
        here = self.spot(units, d, k)
        came = self.came[kind].at[d, hop] if kind < 3 else self.got.at[kind - 3, d]
        return remote(here, here, self.sent.at[kind, d], came, who)

    def every(self, units, sem):
        size = self.rows // 4
        if self.owner_first:
            hops = self.full.at[pl.ds(0, self.n - 1), units, pl.ds(0, size), :]
        else:
            hops = self.full.at[units, pl.ds(0, (self.n - 1) * size), :]
        pltpu.make_async_copy(hops, hops, sem).wait()

    def first(self, e, d):
        src = self.own.at[self.sets[e], block_of(self.c * 2 + d, self.rows // 4), :]
        return remote(src, self.spot(self.sets[e], d, 0), self.sent.at[e, d], self.came[e].at[d, 0], self.ways[d][0])

    def stored(self):
        return pltpu.make_async_copy(self.own, self.at(pl.ds(0, self.units), self.shard), self.local.at[1])

    def ring(self, e, d, k):
        return self.moved(e, self.sets[e], d, k, k, self.ways[d][0])

    def side(self, e, d, k):
        return self.moved(3 + e, self.sets[e], d, k + 1, k, self.sibling)

    def cross(self, d, k):
        return self.moved(2, self.mine, d, k + 1, k, self.across)

    def forward(self, d, k):
        return self.moved(5, self.theirs, d, k + 1, k, self.sibling)

    def vec_hop(self, k):
        here = self.vecs.at[self.shard_at(self.pos - k)]
        return remote(here, here, self.vec_sems[1].at[k], self.vec_sems[2].at[k], self.ways[0][0])

    def begin(self):
        per = self.units // len(self.ins)
        for i, ref in enumerate(self.ins):
            for j in range(per):
                if ref.shape[1] > self.width:
                    part = ref.at[:, pl.ds(j * self.width, self.width)]
                else:
                    part = ref.at[pl.ds(j * self.rows, self.rows), :]
                pltpu.make_async_copy(part, self.own.at[i * per + j], self.local.at[0]).start()
        if self.vec is not None:
            pltpu.make_async_copy(self.vec_in, self.vecs.at[self.shard], self.vec_sems[0].at[0]).start()
        if not self.follows:
            greet((self.ways[0][0], self.ways[1][0], self.sibling, self.across))
        pltpu.make_async_copy(self.own, self.own, self.local.at[0]).wait()
        for e in range(2):
            for d in range(2):
                self.first(e, d).start()
        self.stored().start()
        if self.vec is not None:
            pltpu.make_async_copy(self.vec_in, self.vecs.at[self.shard], self.vec_sems[0].at[0]).wait()

    def step(self, i):
        n = self.n
        pl.when(i == 0)(self.begin)

        for e in range(2):
            for d in range(2):

                @pl.when((i > 0) & (i < n))
                def _():
                    self.ring(e, d, i - 1).wait_recv()

                    @pl.when(i < n - 1)
                    def _():
                        self.ring(e, d, i).start()

                    if e == 0:
                        self.cross(d, i - 1).start()
                    self.side(e, d, i - 1).start()

        @pl.when((i > 1) & (i <= n))
        def _():
            for d in range(2):
                self.cross(d, i - 2).wait_recv()
                self.forward(d, i - 2).start()

        if self.vec is not None:
            @pl.when((i > 0) & (i < n))
            def _():
                self.vec_hop(i - 1).wait_recv()

            @pl.when(i < n - 1)
            def _():
                self.vec_hop(i).start()

    def finish(self, steps):
        n = self.n
        if steps <= n:
            for d in range(2):
                self.cross(d, n - 2).wait_recv()
                self.forward(d, n - 2).start()

        for d in range(2):
            for kind, units in enumerate((*self.sets, self.mine, *self.sets, self.theirs)):
                self.every(units, self.sent.at[kind, d])
                if kind > 2:
                    self.every(units, self.got.at[kind - 3, d])
        if self.vec is not None:
            lax.fori_loop(0, n - 1, lambda k, _: (self.vec_hop(k).wait_send(), 0)[1], 0)
        self.stored().wait()


class Chain:
    def __init__(self, first, second):
        self.first, self.second, self.n = first, second, first.n
        second.follows = True
        self.arrays = first.arrays + second.arrays
        self.out_shapes = first.out_shapes + second.out_shapes
        self.scratch = first.scratch + second.scratch

    def bind(self, ins, outs, scratch):
        a, b, c = len(self.first.arrays), len(self.first.out_shapes), len(self.first.scratch)
        self.first.bind(ins[:a], outs[:b], scratch[:c])
        self.second.bind(ins[a:], outs[b:], scratch[c:])

    def step(self, t):
        self.first.step(t)
        pl.when(t == self.n)(lambda: self.first.finish(self.n + 1))
        self.second.step(t - (self.n - 2))

    def finish(self, ticks):
        self.second.finish(ticks - (self.n - 2))


class Scatter:
    def __init__(self, n, sources, alone, vec=None, start=1, every=1):
        self.n, self.arrays = n, list(sources) + ([] if vec is None else [vec])
        self.vec, self.start, self.every = vec, start, every
        self.counts = [1 if s.ndim == 2 else s.shape[s.ndim - 3] for s in sources]
        self.kinds = [s.ndim for s in sources]
        units = self.units = sum(self.counts)
        self.ne, self.ns = alone, units - 2 * alone
        first = sources[0].shape
        rows = self.rows = first[-2] if len(first) == 4 else first[-2] // n
        width = self.width = sources[0].shape[-1]
        half, self.quarter = rows // 2, rows // 4
        self.out_shapes = [jax.ShapeDtypeStruct((units, rows, width), bf16)]
        dma = pltpu.SemaphoreType.DMA
        self.scratch = [
            pltpu.VMEM((units, n * half, width), bf16),
            pltpu.VMEM((units, n * half, width), bf16),
            pltpu.VMEM((alone, n * half, width), bf16),
            pltpu.VMEM((2, n - 1, alone, half // 2, width), bf16),
            pltpu.VMEM((2, n - 1, self.ns, half // 2, width), bf16),
            pltpu.VMEM((self.ns, half, width), bf16),
            pltpu.VMEM((alone, half, width), bf16),
            dma((2, n)), dma((2,)), dma((2, n)), dma((2,)), dma((2, n)),
            dma((2,)), dma((2, n - 1)), dma((2,)), dma((2, n - 1)),
            dma((2,)), dma((2,)), dma((3,)), dma((3,)), dma((3,)),
        ]
        if vec is not None:
            self.out_shapes.append(jax.ShapeDtypeStruct((8, rows), f32))
            self.scratch += [
                pltpu.VMEM((n, 8, rows), f32), pltpu.VMEM((n - 1, 8, rows), f32), pltpu.VMEM((4, 8, rows), f32),
                pltpu.VMEM((8, rows), f32), dma((2,)), dma((n - 1,)), dma((n - 1,)), dma((3,)), dma((3,)),
            ]

    def bind(self, ins, outs, scratch):
        self.ins, self.out = ins, outs[0]
        (self.near, self.beside, self.over, slots_e, slots_s, self.swap_s, self.swap_e, self.local, self.cs, self.cr,
         self.xs, self.xr, *ring_sems, self.ss, self.sr, self.os, self.orr, self.done) = scratch[:21]
        self.slots, self.ring_sems = (slots_e, slots_s), (ring_sems[:2], ring_sems[2:])
        if self.vec is not None:
            self.vec_in, self.vec_out, self.ins = ins[-1], outs[1], ins[:-1]
            (self.v_near, self.v_ring, self.v_all, self.v_sum, self.v_local, self.v_rs, self.v_rr,
             self.v_ss, self.v_sr) = scratch[21:]
        (self.x, self.c, self.shard, self.pos, self.shard_at, self.ways, self.sibling, self.across,
         self.corner) = neighbours(self.n)
        self.on_ring = self.ne + self.ns
        self.theirs = pl.ds((1 - self.x) * self.on_ring, self.ne)
        self.mine = pl.ds(self.x * self.on_ring, self.ne)
        self.shared = pl.ds(self.ne, self.ns)
        self.sets = (self.mine, self.shared)

    def owner(self, d, k):
        return self.shard_at(self.pos - self.ways[d][1] * (1 + k))

    def span(self, d, k):
        return block_of(self.owner(d, k) * 2 + d, self.quarter)

    def region(self, ref, d, k):
        return ref.at[:, self.span(d, k), :]

    def pieces(self, d, k, core, target):
        owner = self.owner(d, k)
        u = 0
        for ref, count, kind in zip(self.ins, self.counts, self.kinds):
            rows = block_of(owner * 4 + core * 2 + d, self.quarter)
            if kind == 4:
                src = ref.at[owner, :, block_of(core * 2 + d, self.quarter), :]
            else:
                src = ref.at[rows, :] if kind == 2 else ref.at[:, rows, :]
            units = u if kind == 2 else pl.ds(u, count)
            yield src, target.at[units, self.span(d, k), :]
            u += count

    def crossing(self, d, k):
        rows = self.span(d, k)
        return remote(
            self.near.at[self.theirs, rows, :], self.over.at[:, rows, :], self.xs.at[d], self.xr.at[d, k], self.across
        )

    def hop(self, e, d, k):
        src = self.near.at[self.sets[e], self.span(d, k), :]
        sent, got = self.ring_sems[e]
        return remote(src, self.slots[e].at[d, k], sent.at[d], got.at[d, k], self.ways[d][0])

    def vec_hop(self, k):
        return remote(self.v_near.at[self.owner(0, k)], self.v_ring.at[k], self.v_rs.at[k], self.v_rr.at[k], self.ways[0][0])

    def begin(self):
        n = self.n

        def loads(k, _):
            for d in range(2):
                for src, dst in self.pieces(d, k, self.c, self.near):
                    pltpu.make_async_copy(src, dst, self.local.at[d, k]).start()
            return 0

        lax.fori_loop(0, n, loads, 0)
        if self.vec is not None:
            for s in range(n):
                pltpu.make_async_copy(
                    self.vec_in.at[:, pl.ds(s * self.rows, self.rows)], self.v_near.at[s], self.v_local.at[0]
                ).start()
        greet((self.ways[0][0], self.ways[1][0], self.sibling, self.across) + (() if self.vec is None else (self.corner,)))

        def sends(k, _):
            for d in range(2):
                for src, dst in self.pieces(d, k, 1 - self.c, self.beside):
                    remote(src, dst, self.cs.at[d], self.cr.at[d, k], self.sibling).start()
            return 0

        lax.fori_loop(0, n, sends, 0)
        if self.vec is not None:
            pltpu.make_async_copy(self.v_near, self.v_near, self.v_local.at[0]).wait()

    def arrived(self, ref, ssem, rsem, d, k):
        here = self.region(ref, d, k)
        return remote(here, here, ssem.at[d], rsem.at[d, k], self.sibling)

    def pair(self, k):
        for d in range(2):
            rows = self.span(d, k)
            here = self.region(self.near, d, k)
            pltpu.make_async_copy(here, here, self.local.at[d, k]).wait()
            self.arrived(self.beside, self.cs, self.cr, d, k).wait_recv()

            def add(u, _):
                self.near[u, rows, :] = self.near[u, rows, :] + self.beside[u, rows, :]
                return 0

            lax.fori_loop(0, self.units, add, 0)
            self.crossing(d, k).start()

    def combine(self, k, later):
        for e in (1, 0):
            for d in range(2):
                rows = self.span(d, k)
                if later:
                    self.hop(e, d, k - 1).wait_recv()
                if e == 0:
                    self.crossing(d, k).wait_recv()

                def add_shared(i, _):
                    u = self.ne + i
                    self.near[u, rows, :] = self.near[u, rows, :] + self.slots[1][d, k - 1, i]
                    return 0

                def add_mine(i, _):
                    u = self.x * self.on_ring + i
                    value = self.near[u, rows, :].astype(f32) + self.over[i, rows, :].astype(f32)
                    if later:
                        value = value + self.slots[0][d, k - 1, i].astype(f32)
                    self.near[u, rows, :] = value.astype(bf16)
                    return 0

                if e == 0:
                    lax.fori_loop(0, self.ne, add_mine, 0)
                elif later:
                    lax.fori_loop(0, self.ns, add_shared, 0)

                @pl.when(k < self.n - 1)
                def _():
                    self.hop(e, d, k).start()

        if self.vec is not None:
            if later:
                self.vec_hop(k - 1).wait_recv()
                self.v_near[self.owner(0, k)] = self.v_near[self.owner(0, k)] + self.v_ring[k - 1]

            @pl.when(k < self.n - 1)
            def _():
                self.vec_hop(k).start()

    def step(self, t):
        n = self.n
        pl.when(t == 0)(self.begin)
        since = t - self.start
        if self.every > 1:
            k, on = (since + n * self.every) // self.every - n, lax.rem(since + n * self.every, self.every) == 0
        else:
            k, on = since, since >= 0

        @pl.when(since == 0)
        def _():
            self.pair(0)
            self.pair(1)
            self.combine(0, False)

        @pl.when(on & (k > 0) & (k < n))
        def _():
            self.combine(k, True)

        @pl.when(on & (k >= 0) & (k + 2 < n))
        def _():
            self.pair(k + 2)

        pl.when(since == (n - 1) * self.every)(self.exchange)
        pl.when(since == (n - 1) * self.every + max(2, self.every))(self.join)

    def swap(self, e):
        src = self.near.at[self.sets[e], block_of(self.shard, self.rows // 2), :]
        return remote(src, (self.swap_e, self.swap_s)[e], self.ss.at[e], self.sr.at[e], self.across)

    def result(self, j, away):
        half = block_of(self.c, self.rows // 2)
        src = (self.near.at[self.mine, block_of(self.shard, self.rows // 2), :], self.swap_s, self.swap_e)[j]
        dst = self.out.at[(self.mine, self.shared, self.theirs)[j], half, :]
        if away:
            return remote(src, dst, self.os.at[j], self.orr.at[j], self.sibling)
        return pltpu.make_async_copy(src, dst, self.done.at[j])

    def shares(self):
        sums, rep = self.v_near.at[self.shard], self.x * 2 + self.c
        return [
            remote(sums, self.v_all.at[rep], self.v_ss.at[j], self.v_sr.at[j], who)
            for j, who in enumerate((self.sibling, self.across, self.corner))
        ]

    def put(self, j):
        self.result(j, True).start()
        self.result(j, False).start()

    def exchange(self):
        self.swap(1).start()
        self.swap(0).start()
        self.put(0)
        if self.vec is not None:
            for copy in self.shares():
                copy.start()
            self.v_all[self.x * 2 + self.c] = self.v_near[self.shard]

    def join(self):
        at = block_of(self.shard, self.rows // 2)
        self.swap(1).wait_recv()

        def add(i, _):
            self.swap_s[i] = self.swap_s[i] + self.near[self.ne + i, at, :]
            return 0

        lax.fori_loop(0, self.ns, add, 0)
        self.put(1)
        self.swap(0).wait_recv()
        self.put(2)

    def finish(self, ticks):
        n = self.n
        last = self.start + (n - 1) * self.every
        assert ticks > last - self.every
        if ticks <= last:
            self.combine(n - 1, True)
            self.exchange()
        if ticks <= last + max(2, self.every):
            self.join()
        if self.vec is not None:
            for copy in self.shares():
                copy.wait()
            self.v_sum[...] = (self.v_all[0] + self.v_all[1]) + (self.v_all[2] + self.v_all[3])
            load(self.v_sum, self.vec_out, self.v_local.at[1]).wait()
        for j in range(3):
            self.result(j, False).wait()
            self.result(j, True).wait()
        for e in range(2):
            self.swap(e).wait_send()

        span = pl.ds(0, n * self.quarter)
        for d in range(2):
            totals = [(self.beside.at[:, span, :], self.cs.at[d]), (self.over.at[:, span, :], self.xs.at[d])]
            totals += [(self.slots[e].at[d], self.ring_sems[e][0].at[d]) for e in range(2)]
            for whole, sem in totals:
                pltpu.make_async_copy(whole, whole, sem).wait()
        if self.vec is not None:
            lax.fori_loop(0, n - 1, lambda k, _: (self.vec_hop(k).wait_send(), 0)[1], 0)


def hosted(
    kernel, steps, args, in_specs, out_shapes, out_specs, scratch, name, carry=None, collective_id=None, done_by=None, ticks=1, vmem=58,
    late=(),
):
    args, in_specs = list(args), list(in_specs)
    stores = []
    for at, _, lead in late:
        in_specs[at] = HBM
        stores.append(pltpu.VMEM(args[at].shape if lead is None else (lead,) + args[at].shape[1:], args[at].dtype))
    scratch = list(scratch) + stores + ([pltpu.SemaphoreType.DMA((len(late),))] if late else [])
    counts = [len(args), len(out_shapes), len(scratch)]
    extra = [0, 0, 0]
    params = dict(vmem_limit_bytes=vmem * MIB)
    if carry is not None:
        extra = [len(carry.arrays), len(carry.out_shapes), len(carry.scratch)]
        params.update(collective_id=collective_id, has_side_effects=True)

    def whole(*refs):
        main, other, first = [], [], 0
        for count, more in zip(counts, extra):
            main += refs[first : first + count]
            other.append(refs[first + count : first + count + more])
            first += count + more
        i = pl.program_id(0)
        copies = []
        if late:
            *main, late_sems = main
            kept = main[len(main) - len(late) :]
            main = main[: len(main) - len(late)]
            for m, (at, _, lead) in enumerate(late):
                src = main[at] if lead is None else main[at].at[pl.ds(0, lead)]
                copies.append(pltpu.make_async_copy(src, kept[m], late_sems.at[m]))
                main[at] = kept[m]

        def tick(j):
            if carry is not None:
                carry.step(i * ticks + j)
            if j == 0 and late:
                pl.when(i == 0)(lambda: [copy.start() for copy in copies] and None)
                for copy, (_, step, _) in zip(copies, late):
                    pl.when(i == step)(copy.wait)

        if carry is not None:
            carry.bind(*other)
        if ticks == 1:
            tick(0)
            if done_by is not None:
                pl.when(i == done_by)(lambda: carry.finish(done_by + 1))
            if kernel is not None:
                kernel(*main)
        else:
            kernel(tick, *main)
        if carry is not None and done_by is None:
            pl.when(i == steps - 1)(lambda: carry.finish(steps * ticks))

    return pl.pallas_call(
        whole,
        grid=(steps,),
        out_shape=list(out_shapes) + (carry.out_shapes if carry else []),
        in_specs=list(in_specs) + [HBM] * extra[0],
        out_specs=list(out_specs) + [HBM] * extra[1],
        scratch_shapes=list(scratch) + (carry.scratch if carry else []),
        compiler_params=pltpu.CompilerParams(**params),
        name=name,
    )(*args, *(carry.arrays if carry else []))


def norm_forward(resid, gain, shift):
    mean = jnp.mean(resid, -1, keepdims=True)
    centred = resid - mean
    variance = jnp.mean(centred * centred, -1, keepdims=True)
    inverse = lax.rsqrt(variance + EPS)
    normed = centred * inverse
    return (normed * gain + shift, normed, inverse)


def norm_backward(grad_out, normed, inverse, gain):
    grad_gain = jnp.sum(grad_out * normed, 0, keepdims=True)
    grad_shift = jnp.sum(grad_out, 0, keepdims=True)
    grad_normed = grad_out * gain
    centre_term = jnp.mean(grad_normed, -1, keepdims=True)
    slope_term = jnp.mean(grad_normed * normed, -1, keepdims=True)
    return (inverse * (grad_normed - centre_term - normed * slope_term), grad_gain, grad_shift)


def fixed(a):
    zeros = (0,) * a.ndim
    return pl.BlockSpec(a.shape, lambda i: zeros, pipeline_mode=pl.Buffered(1))


def slices(rows, count):
    size = rows // count
    return [slice(j * size, (j + 1) * size) for j in range(count)]


def first_lanes(shape):
    return lax.broadcasted_iota(jnp.int32, shape, len(shape) - 1) < HD


def region_bias(starts_ref, region, size, transposed):
    first = region * size
    one = first + lax.broadcasted_iota(jnp.int32, (size, size), 0)
    two = first + lax.broadcasted_iota(jnp.int32, (size, size), 1)
    q_at, k_at = (two, one) if transposed else (one, two)
    start = starts_ref[0, region]
    q_in = (q_at >= start) & (q_at < start + PIC)
    k_in = (k_at >= start) & (k_at < start + PIC)
    return jnp.where((k_at <= q_at) | (q_in & k_in), 0.0, NEGATIVE)


def self_forward_kernel(regions, lead, scale, carry, starts_ref, x_ref, *refs):
    refs = list(refs)
    w_ref = refs.pop(0) if carry is None else carry.first.full
    q_ref, k_ref, v_ref, o_ref, lse_ref, bias_ref, w_buf, sems = refs
    rows, size = x_ref.shape[0], x_ref.shape[0] // regions
    i = pl.program_id(0)
    j = i - lead
    pairs = pl.num_programs(0) - lead

    @pl.when(i == 0)
    def _():
        for r in range(regions):
            bias_ref[r] = region_bias(starts_ref, r, size, False)

    def fetch(pair, slot):
        return pltpu.make_async_copy(w_ref.at[:, :, block_of(pair, 2 * HD)], w_buf.at[slot], sems.at[slot])

    @pl.when(j == 0)
    def _():
        fetch(0, 0).start()

    @pl.when(j >= 0)
    def _():
        slot = lax.rem(i - lead + 2, 2)

        @pl.when(j + 1 < pairs)
        def _():
            fetch(j + 1, 1 - slot).start()

        fetch(j, slot).wait()
        made = dot(x_ref[...], jnp.concatenate([w_buf[slot, u] for u in range(3)], 1))
        q_ref[...] = (made[:, : 2 * HD] * scale).astype(bf16)
        k_ref[...] = made[:, 2 * HD : 4 * HD].astype(bf16)
        v_ref[...] = made[:, 4 * HD :].astype(bf16)
        low = first_lanes((1, 2 * HD))
        outs, lses = [[], []], [[], []]
        for h in range(2):
            keys = jnp.where(low if h == 0 else ~low, k_ref[...], jnp.zeros((), bf16))
            for r in range(regions):
                span = slice(r * size, (r + 1) * size)
                q = q_ref[span, :]
                scores = []
                if r:
                    scores.append((dot(q, keys[: r * size], 1, 1), v_ref[: r * size, :]))
                scores.append((dot(q, keys[span], 1, 1) + bias_ref[r], v_ref[span, :]))
                top = functools.reduce(jnp.maximum, [jnp.max(s, -1, keepdims=True) for s, _ in scores])
                total, mixed = 0.0, 0.0
                for s, v in scores:
                    e = jnp.exp(s - top)
                    total = total + jnp.sum(e, -1, keepdims=True)
                    mixed = mixed + dot(e.astype(bf16), v)
                outs[h].append(mixed / total)
                lses[h].append(top + jnp.log(total))
        for r in range(regions):
            span = slice(r * size, (r + 1) * size)
            o_ref[span, :] = jnp.where(low, outs[0][r], outs[1][r]).astype(bf16)
            turned = jnp.where(low, lses[0][r], lses[1][r]).T
            lse_ref[0, 0:1, span] = turned[0:1]
            lse_ref[0, 1:2, span] = turned[HD : HD + 1]


def self_forward(states, weights, starts, scale, carry, collective_id):
    rows, width = states.shape
    regions = starts.shape[1]
    size = rows // regions
    pairs = width // (2 * HD)
    lead = 0 if carry is None else carry.n
    args, specs = [starts, states], [pl.BlockSpec(memory_space=pltpu.SMEM), fixed(states)]
    if carry is None:
        args.append(weights)
        specs.append(HBM)
    column = pl.BlockSpec((rows, 2 * HD), lambda i: (0, jnp.maximum(i - lead, 0)))
    return hosted(
        functools.partial(self_forward_kernel, regions, lead, scale, carry), lead + pairs, args, specs,
        [jax.ShapeDtypeStruct((rows, width), bf16)] * 4 + [jax.ShapeDtypeStruct((pairs, 8, rows), f32)],
        [column] * 4 + [pl.BlockSpec((1, 8, rows), lambda i: (jnp.maximum(i - lead, 0), 0, 0))],
        [pltpu.VMEM((regions, size, size), f32), pltpu.VMEM((2, 3, width, 2 * HD), bf16), pltpu.SemaphoreType.DMA((2,))],
        "self_forward", carry, collective_id,
    )


def self_backward_kernel(
    regions, scale, pairs, starts_ref, q_ref, k_ref, v_ref, g_ref, o_ref, lse_ref, x_ref, w_ref, resid_ref,
    g_query_ref, g_key_ref, g_value_ref, grad_ref, bias_ref, grads,
):
    rows, width = x_ref.shape
    size = rows // regions
    i = pl.program_id(0)
    spans = slices(rows, regions)
    low = first_lanes((1, 2 * HD))

    @pl.when(i == 0)
    def _():
        for r in range(regions):
            bias_ref[r] = region_bias(starts_ref, r, size, True)

    @pl.when(i < pairs)
    def _():
        product = g_ref[...].astype(f32) * o_ref[...].astype(f32)
        chooser = lax.broadcasted_iota(jnp.int32, (8, 2 * HD), 0)
        chooser = ((chooser == 0) & first_lanes((8, 2 * HD))) | ((chooser == 1) & ~first_lanes((8, 2 * HD)))
        chooser = chooser.astype(f32).astype(bf16)
        upper = product.astype(bf16)
        lower = (product - upper.astype(f32)).astype(bf16)
        deltas = dot(chooser, upper, 1, 1) + dot(chooser, lower, 1, 1)
        gq, gk, gv = {}, {}, {}
        for h in range(2):
            pick = low if h == 0 else ~low
            zero = jnp.zeros((), bf16)
            keys = jnp.where(pick, k_ref[...], zero)
            values = jnp.where(pick, v_ref[...], zero)
            for r, span in enumerate(spans):
                q, g = q_ref[span, :], g_ref[span, :]
                lse = lse_ref[0, h : h + 1, span]
                delta = deltas[h : h + 1, span]
                for j, keyed in enumerate(spans[: r + 1]):
                    scores = dot(keys[keyed], q, 1, 1)
                    if j == r:
                        scores = scores + bias_ref[r]
                    probs = jnp.exp(scores - lse)
                    grad_probs = dot(values[keyed], g, 1, 1)
                    grad_scores = (probs * (grad_probs - delta)).astype(bf16)
                    gv[h, j] = gv.get((h, j), 0.0) + dot(probs.astype(bf16), g)
                    gk[h, j] = gk.get((h, j), 0.0) + dot(grad_scores, q)
                    gq[h, r] = gq.get((h, r), 0.0) + dot(grad_scores, k_ref[keyed, :], 0, 0)
        cols = block_of(i, 2 * HD)
        for r, span in enumerate(spans):
            grads[0, span, cols] = jnp.where(low, gq[0, r], gq[1, r]).astype(bf16) * scale
            grads[1, span, cols] = jnp.where(low, gk[0, r], gk[1, r]).astype(bf16)
            grads[2, span, cols] = jnp.where(low, gv[0, r], gv[1, r]).astype(bf16)

    for u, out in enumerate((g_query_ref, g_key_ref, g_value_ref)):

        @pl.when(i == pairs + u)
        def _():
            for span in slices(width, 4):
                out[span, :] = dot(x_ref[:, span], grads[u], 0, 0).astype(bf16)

    @pl.when(i >= pairs + 3)
    def _():
        at = block_of(i - pairs - 3, grad_ref.shape[0])
        total = resid_ref[...]
        for u in range(3):
            total = total + dot(grads[u, at, :], w_ref[u], 1, 1)
        grad_ref[...] = total


def self_backward(q, k, v, g, o, lse, starts, states, weights, resid, scale, carry, collective_id):
    rows, width = q.shape
    regions = starts.shape[1]
    size = rows // regions
    pairs, parts = width // (2 * HD), 4
    last = pairs - 1
    column = pl.BlockSpec((rows, 2 * HD), lambda i: (0, jnp.minimum(i, last)))
    some = pl.BlockSpec((rows // parts, width), lambda i: (jnp.maximum(i - pairs - 3, 0), 0))
    square = jax.ShapeDtypeStruct((width, width), bf16)
    return hosted(
        functools.partial(self_backward_kernel, regions, scale, pairs), pairs + 3 + parts,
        [starts, q, k, v, g, o, lse, states, weights, resid],
        [pl.BlockSpec(memory_space=pltpu.SMEM)] + [column] * 5
        + [pl.BlockSpec((1, 8, rows), lambda i: (jnp.minimum(i, last), 0, 0)), fixed(states), fixed(weights), some],
        [square] * 3 + [jax.ShapeDtypeStruct((rows, width), f32)], [fixed(square)] * 3 + [some],
        [pltpu.VMEM((regions, size, size), f32), pltpu.VMEM((3, rows, width), bf16)],
        "self_backward", carry, collective_id, vmem=60, late=((7, pairs, None), (8, pairs + 3, None)),
    )


def cross_forward_kernel(
    scale, tick, x_ref, mixed_in, enc_ref, w_ref, vec_ref, low_ref, n1_ref, i1_ref, q_ref, k_ref, v_ref, mixed_ref,
    lse_ref, two_ref, n2_ref, i2_ref, low_two_ref,
):
    tick(0)

    @pl.when(pl.program_id(0) == 0)
    def _():
        k_ref[...] = dot(enc_ref[...], w_ref[2]).astype(bf16)
        v_ref[...] = dot(enc_ref[...], w_ref[3]).astype(bf16)

    one, n1_ref[...], i1_ref[...] = norm_forward(
        x_ref[...].astype(f32) + dot(mixed_in[...], w_ref[0]), vec_ref[0:1, :], vec_ref[1:2, :]
    )
    low_ref[...] = one.astype(bf16)
    q_ref[...] = (dot(low_ref[...], w_ref[1]) * scale).astype(bf16)
    rows, width = x_ref.shape
    low = first_lanes((1, 2 * HD))
    lane = lax.broadcasted_iota(jnp.int32, (1, 2 * HD), 1)
    lses = jnp.zeros((rows, 2 * HD), f32)
    for pair in range(width // (2 * HD)):
        if pair == 2:
            tick(1)
        cols = slice(pair * 2 * HD, (pair + 1) * 2 * HD)
        parts = []
        for h in range(2):
            keys = jnp.where(low if h == 0 else ~low, k_ref[:, cols], jnp.zeros((), bf16))
            scores = dot(q_ref[:, cols], keys, 1, 1)
            top = jnp.max(scores, -1, keepdims=True)
            e = jnp.exp(scores - top)
            total = jnp.sum(e, -1, keepdims=True)
            parts.append(dot(e.astype(bf16), v_ref[:, cols]) / total)
            lses = jnp.where(lane == 8 * pair + h, top + jnp.log(total), lses)
        mixed_ref[:, cols] = jnp.where(low, *parts).astype(bf16)
    lse_ref[...] = lses.T[: lse_ref.shape[0]]
    two, n2_ref[...], i2_ref[...] = norm_forward(one + dot(mixed_ref[...], w_ref[4]), vec_ref[2:3, :], vec_ref[3:4, :])
    two_ref[...] = two
    low_two_ref[...] = two.astype(bf16)


def cross_forward(states, mixed, encoded, weights, vecs, scale, carry, collective_id):
    rows, width = states.shape
    steps = 4
    block = pl.BlockSpec((rows // steps, width), lambda i: (i, 0))
    thin = pl.BlockSpec((rows // steps, 1), lambda i: (i, 0))
    heads = width // HD * 4
    tall = lambda kind: jax.ShapeDtypeStruct((rows, width), kind)
    column = jax.ShapeDtypeStruct((rows, 1), f32)
    outs = [
        (tall(bf16), block), (tall(f32), block), (column, thin), (tall(bf16), block), (encoded, fixed(encoded)),
        (encoded, fixed(encoded)), (tall(bf16), block),
        (jax.ShapeDtypeStruct((heads, rows), f32), pl.BlockSpec((heads, rows // steps), lambda i: (0, i))),
        (tall(f32), block), (tall(f32), block), (column, thin), (tall(bf16), block),
    ]
    return hosted(
        functools.partial(cross_forward_kernel, scale), steps, [states, mixed, encoded, weights, vecs],
        [block, block, fixed(encoded), fixed(weights), fixed(vecs)],
        [jax.ShapeDtypeStruct(o.shape, o.dtype) for o, _ in outs], [spec for _, spec in outs], [],
        "cross_forward", carry, collective_id, ticks=2,
    )


def cross_backward_kernel(
    scale, pairs, parts, b2_ref, mixed_ref, low_ref, mixed_one_ref, q_ref, lse_ref, k_ref, v_ref, w_ref, vec_ref, g2_ref,
    n1_ref, i1_ref, w_out_ref, enc_ref, g_out_ref, g_query_ref, g_self_out_ref, g_key_ref, g_value_ref, g1_ref, gm_ref,
    sums_ref, g_enc_ref, g_mixed, gq_all, b1_all, gk_all, gv_all,
):
    i = pl.program_id(0)
    rows, width = b2_ref.shape

    @pl.when(i == 0)
    def _():
        for span in slices(rows, 4):
            g_mixed[span, :] = dot(b2_ref[span, :], w_out_ref[0], 1, 1).astype(bf16)
        sums_ref[...] = jnp.zeros_like(sums_ref)

    j = i - 1

    @pl.when((j >= 0) & (j < pairs))
    def _():
        cols = block_of(j, 2 * HD)
        low = first_lanes((1, 2 * HD))
        chooser = lax.broadcasted_iota(jnp.int32, (8, 2 * HD), 0)
        chooser = ((chooser == 0) & first_lanes((8, 2 * HD))) | ((chooser == 1) & ~first_lanes((8, 2 * HD)))
        chooser = chooser.astype(f32).astype(bf16)
        gks, gvs = [0.0, 0.0], [0.0, 0.0]
        for span in slices(rows, 2):
            g, q = g_mixed[span, cols], q_ref[span, :]
            product = g.astype(f32) * mixed_ref[span, cols].astype(f32)
            upper = product.astype(bf16)
            lower = (product - upper.astype(f32)).astype(bf16)
            deltas = dot(chooser, upper, 1, 1) + dot(chooser, lower, 1, 1)
            gqs = []
            for h in range(2):
                pick = low if h == 0 else ~low
                keys = jnp.where(pick, k_ref[...], jnp.zeros((), bf16))
                values = jnp.where(pick, v_ref[...], jnp.zeros((), bf16))
                probs = jnp.exp(dot(keys, q, 1, 1) - lse_ref[h : h + 1, span])
                grad_scores = (probs * (dot(values, g, 1, 1) - deltas[h : h + 1, :])).astype(bf16)
                gvs[h] = gvs[h] + dot(probs.astype(bf16), g)
                gks[h] = gks[h] + dot(grad_scores, q)
                gqs.append(dot(grad_scores, k_ref[...], 0, 0))
            gq_all[span, cols] = jnp.where(low, *gqs).astype(bf16) * scale
        gk_all[:, cols] = jnp.where(low, *gks).astype(bf16)
        gv_all[:, cols] = jnp.where(low, *gvs).astype(bf16)

    m = j - pairs

    @pl.when((m >= 0) & (m < parts))
    def _():
        at = block_of(m, rows // parts)
        grad_one = g2_ref[...] + dot(gq_all[at, :], w_ref[1], 1, 1)
        grad, g_gain, g_shift = norm_backward(grad_one, n1_ref[...], i1_ref[...], vec_ref[0:1, :])
        sums_ref[0:1, :] += g_gain
        sums_ref[1:2, :] += g_shift
        g1_ref[...] = grad
        b1_all[at, :] = grad.astype(bf16)
        gm_ref[...] = dot(b1_all[at, :], w_ref[0], 1, 1).astype(bf16)

    for u, (left, right, out) in enumerate(
        ((mixed_ref, b2_ref, g_out_ref), (low_ref, gq_all, g_query_ref), (mixed_one_ref, b1_all, g_self_out_ref))
    ):

        @pl.when(m == parts + u)
        def _():
            for span in slices(width, 4):
                out[span, :] = dot(left[:, span], right[...], 0, 0).astype(bf16)

    @pl.when(m == parts + 3)
    def _():
        for span in slices(width, 2):
            g_key_ref[span, :] = dot(enc_ref[:, span], gk_all[...], 0, 0).astype(bf16)
            g_value_ref[span, :] = dot(enc_ref[:, span], gv_all[...], 0, 0).astype(bf16)
        g_enc_ref[...] = dot(gk_all[...], w_ref[2], 1, 1) + dot(gv_all[...], w_ref[3], 1, 1)


def cross_backward(
    branch, mixed, low, mixed_one, grad, normed, inverse, q, lse, k, v, weights, vecs, encoded, scale, carry, collective_id
):
    rows, width = q.shape
    pairs, parts = width // (2 * HD), 4
    column = lambda a: pl.BlockSpec((a.shape[0], 2 * HD), lambda i: (0, jnp.clip(i - 1, 0, pairs - 1)))
    some = lambda cols: pl.BlockSpec((rows // parts, cols), lambda i: (jnp.clip(i - 1 - pairs, 0, parts - 1), 0))
    square = jax.ShapeDtypeStruct((width, width), bf16)
    outs = [
        *[(square, fixed(square))] * 5, (grad, some(width)), (q, some(width)), (vecs, fixed(vecs)),
        (jax.ShapeDtypeStruct(k.shape, f32), fixed(k)),
    ]
    args = [branch, mixed, low, mixed_one, q, lse, k, v, weights, vecs, grad, normed, inverse, weights, encoded]
    out_weight = pl.BlockSpec((1, width, width), lambda i: (4, 0, 0), pipeline_mode=pl.Buffered(1))
    lse_spec = pl.BlockSpec((8, rows), lambda i: (jnp.clip(i - 1, 0, pairs - 1), 0))
    return hosted(
        functools.partial(cross_backward_kernel, scale, pairs, parts), 1 + pairs + parts + 4, args,
        [fixed(a) for a in args[:4]] + [column(q), lse_spec, column(k), column(v), fixed(weights), fixed(vecs)]
        + [some(width), some(width), some(1), out_weight, HBM],
        [jax.ShapeDtypeStruct(o.shape, o.dtype) for o, _ in outs], [spec for _, spec in outs],
        [pltpu.VMEM((rows, width), bf16)] * 3 + [pltpu.VMEM(k.shape, bf16)] * 2, "cross_backward", carry, collective_id, vmem=62,
        late=((2, 1 + pairs, None), (3, 1 + pairs, None), (8, 1 + pairs, 4), (14, 1 + pairs, None)),
    )


def ffn_forward_kernel(blocks, carry, low_ref, two_ref, cot_ref, vec_ref, w1_ref, *refs):
    refs = list(refs)
    w2_ref = refs.pop(0) if carry is None else carry.full
    final_ref, branch_ref, grad_ref, slope_ref, g_contract_ref, sums_ref, acts, acc, w2_buf, sems = refs
    i = pl.program_id(0)
    spans = slices(low_ref.shape[0], 4)

    @pl.when(i < blocks)
    def _():
        for span in spans:
            pre = dot(low_ref[span, :], w1_ref[0])
            phi = 0.5 * (1.0 + lax.erf(pre * INV_ROOT_TWO))
            acts[i, span, :] = (pre * phi).astype(bf16)
            slope_ref[span, :] = (phi + pre * jnp.exp(-0.5 * pre * pre) * INV_ROOT_TWO_PI).astype(bf16)

    j = i - blocks

    def fetch(block, slot):
        return pltpu.make_async_copy(w2_ref.at[block], w2_buf.at[slot], sems.at[slot])

    @pl.when(j == 0)
    def _():
        fetch(0, 0).start()
        acc[...] = two_ref[...]

    @pl.when((j >= 0) & (j < blocks))
    def _():
        slot = lax.rem(j + blocks * 2, 2)

        @pl.when(j + 1 < blocks)
        def _():
            fetch(j + 1, 1 - slot).start()

        fetch(j, slot).wait()
        w2 = w2_buf[slot].reshape(-1, w2_buf.shape[-1])
        for span in spans:
            acc[span, :] += dot(acts[j, span, :], w2)

    @pl.when(j == blocks - 1)
    def _():
        gain, shift = vec_ref[4:5, :], vec_ref[5:6, :]
        sums = [0.0, 0.0]
        for span in slices(low_ref.shape[0], 8):
            final, normed, inverse = norm_forward(acc[span, :], gain, shift)
            final_ref[span, :] = final.astype(bf16)
            grad, *parts = norm_backward(cot_ref[span, :].astype(f32), normed, inverse, gain)
            grad_ref[span, :] = grad
            branch_ref[span, :] = grad.astype(bf16)
            sums = [a + b for a, b in zip(sums, parts)]
        sums_ref[...] = jnp.zeros_like(sums_ref)
        sums_ref[0:1, :] = sums[0]
        sums_ref[1:2, :] = sums[1]

    @pl.when(j >= blocks)
    def _():
        made = dot(acts[j - blocks], branch_ref[...], 0, 0).astype(bf16)
        g_contract_ref[0] = made.reshape(g_contract_ref.shape[1:])


def ffn_forward(low, two, cotangent, vecs, w1, w2, carry, collective_id):
    rows, width = low.shape
    if carry is not None:
        blocks, size = carry.n, carry.units * carry.rows
    else:
        blocks, size = w2.shape[0], w2.shape[1] * w2.shape[2]
    per = width // size
    last = blocks - 1
    args = [low, two, cotangent, vecs, w1]
    specs = [fixed(a) for a in args[:4]]
    specs.append(pl.BlockSpec((1, width, size), lambda i: (jnp.minimum(i, last) // per, 0, lax.rem(jnp.minimum(i, last), per))))
    if carry is None:
        args.append(w2)
        specs.append(HBM)
    tall = jax.ShapeDtypeStruct((rows, blocks * size), bf16)
    part = w2.shape[1:] if carry is None else (carry.units, carry.rows, width)
    outs = [low, low, two, tall, jax.ShapeDtypeStruct((blocks,) + part, bf16), jax.ShapeDtypeStruct((8, width), f32)]
    out_specs = [fixed(a) for a in outs[:3]]
    out_specs.append(pl.BlockSpec((rows, size), lambda i: (0, jnp.minimum(i, last))))
    out_specs.append(pl.BlockSpec((1,) + part, lambda i: (jnp.maximum(i - 2 * blocks, 0), 0, 0, 0)))
    out_specs.append(fixed(outs[5]))
    return hosted(
        functools.partial(ffn_forward_kernel, blocks, carry), 3 * blocks, args, specs,
        [jax.ShapeDtypeStruct(a.shape, a.dtype) for a in outs], out_specs,
        [
            pltpu.VMEM((blocks, rows, size), bf16), pltpu.VMEM((rows, width), f32),
            pltpu.VMEM((2,) + part, bf16), pltpu.SemaphoreType.DMA((2,)),
        ],
        "ffn_forward", carry, collective_id, done_by=blocks if carry else None, vmem=60,
        late=((1, blocks, None), (2, 2 * blocks - 1, None)),
    )


def ffn_backward_kernel(
    blocks, low_ref, branch_ref, vec_ref, w1_ref, w2_ref, slope_ref, normed_ref, inverse_ref, g_ref,
    g_expand_ref, grad_ref, branch_two_ref, sums_ref, turned, acc, g_pre, sem,
):
    i = pl.program_id(0)
    rows = low_ref.shape[0]
    spans = slices(rows, 4)
    start = pltpu.make_async_copy(g_ref, acc, sem.at[0])

    @pl.when(i == 0)
    def _():
        start.start()
        turned[...] = low_ref[...].T
        sums_ref[...] = jnp.zeros_like(sums_ref)

    @pl.when(i < blocks)
    def _():
        w2 = w2_ref[0].reshape(-1, w2_ref.shape[-1])
        for span in spans:
            g_pre[span, :] = (dot(branch_ref[span, :], w2, 1, 1) * slope_ref[span, :].astype(f32)).astype(bf16)
        for span in slices(turned.shape[0], 4):
            g_expand_ref[0, span, :] = dot(turned[span, :], g_pre[...]).astype(bf16)
        pl.when(i == 0)(start.wait)
        for span in spans:
            acc[span, :] += dot(g_pre[span, :], w1_ref[0], 1, 1)

    @pl.when(i >= blocks)
    def _():
        at = block_of(i - blocks, grad_ref.shape[0])
        grad, g_gain, g_shift = norm_backward(acc[at, :], normed_ref[...], inverse_ref[...], vec_ref[2:3, :])
        grad_ref[...] = grad
        branch_two_ref[...] = grad.astype(bf16)
        sums_ref[0:1, :] += g_gain
        sums_ref[1:2, :] += g_shift


def ffn_backward(low, branch, grad, normed, inverse, vecs, w1, w2, slope, carry, collective_id):
    rows, width = low.shape
    blocks, size = w2.shape[0], w2.shape[1] * w2.shape[2]
    per, last, parts = width // size, w2.shape[0] - 1, 4
    wide = pl.BlockSpec((1, width, size), lambda i: (jnp.minimum(i, last) // per, 0, lax.rem(jnp.minimum(i, last), per)))
    deep = pl.BlockSpec((1,) + w2.shape[1:], lambda i: (jnp.minimum(i, last), 0, 0, 0))
    column = pl.BlockSpec((rows, size), lambda i: (0, jnp.minimum(i, last)))
    some = lambda cols: pl.BlockSpec((rows // parts, cols), lambda i: (jnp.maximum(i - blocks, 0), 0))
    args = [low, branch, vecs, w1, w2, slope, normed, inverse, grad]
    outs = [w1, grad, low, vecs]
    return hosted(
        functools.partial(ffn_backward_kernel, blocks), blocks + parts, args,
        [fixed(a) for a in args[:3]] + [wide, deep, column, some(width), some(1), HBM],
        [jax.ShapeDtypeStruct(a.shape, a.dtype) for a in outs], [wide, some(width), some(width), fixed(vecs)],
        [
            pltpu.VMEM((width, rows), bf16), pltpu.VMEM((rows, width), f32), pltpu.VMEM((rows, size), bf16),
            pltpu.SemaphoreType.DMA((1,)),
        ],
        "ffn_backward", carry, collective_id, vmem=60,
    )


def body(n, states, encoded, starts, cotangent, *weights):
    matrices, vectors = weights[:10], weights[10:]
    expand, contract = matrices[8], matrices[9]
    rows, width = matrices[0].shape
    blocks = contract.shape[0] // rows
    scale = HD ** (-0.5)
    small = n <= 16
    vec = jnp.zeros((16, max(rows, 128)), bf16).at[: len(vectors), :rows].set(jnp.stack(vectors))
    take = lambda shards, units, alone, **more: Gather(n, width, shards, units, alone, **more) if small else None
    if small:
        chain = Chain(take(matrices[:3], 3, 1, vec=vec), take(matrices[3:8], 5, 2))
        q_self, k_self, v_self, mixed_self, lse_self, first, vecs, second = self_forward(states, None, starts, scale, chain, 0)
    else:
        first = lax.all_gather(jnp.stack(matrices[:3]), "shard", axis=1, tiled=True)
        vecs = lax.all_gather(vec, "shard", axis=0)
        second = lax.all_gather(jnp.stack(matrices[3:8]), "shard", axis=1, tiled=True)
        q_self, k_self, v_self, mixed_self, lse_self = self_forward(states, first, starts, scale, None, None)
    vecs = vecs[:, : len(vectors), :rows].transpose(1, 0, 2).reshape(len(vectors), width).astype(f32)
    vecs = jnp.concatenate([vecs, jnp.zeros((2, width), f32)])
    (one_low, normed_one, inverse_one, q_cross, k_cross, v_cross, mixed_cross, lse_cross, hidden_two, normed_two, inverse_two,
     two_low, *third) = cross_forward(states, mixed_self, encoded, second, vecs, scale, take([expand], blocks, 1), 2)
    if not small:
        third = [lax.all_gather(expand.reshape(rows, blocks, width).transpose(1, 0, 2), "shard", axis=1, tiled=True)]
    w1 = third[0]
    w2 = None
    if not small:
        w2 = lax.all_gather(contract, "shard", axis=0, tiled=True).reshape(8, 4, -1, width)
    final, branch_three, grad_three, slope, g_contract, sums_three, *fourth = ffn_forward(
        two_low, hidden_two, cotangent, vecs, w1, w2, take([contract], blocks, 1, owner_first=True), 3
    )
    if small:
        w2 = fourth[0]

    give = lambda sources, alone, **more: Scatter(n, sources, alone, **more) if small else None
    g_expand, grad_resid_two, branch_two, sums_two, *own_contract = ffn_backward(
        two_low, branch_three, grad_three, normed_two, inverse_two, vecs, w1, w2, slope, give([g_contract], 1), 4
    )
    (g_cross_out, g_cross_query, g_self_out, g_cross_key, g_cross_value, grad_resid_one, grad_mixed, sums_one, grad_encoded,
     *own_expand) = cross_backward(
        branch_two, mixed_cross, one_low, mixed_self, grad_resid_two, normed_one, inverse_one, q_cross, lse_cross, k_cross,
        v_cross, second, vecs, encoded, scale, give([g_expand], 1, start=1, every=2), 5
    )
    g_cross = [g_cross_query, g_cross_key, g_cross_value, g_cross_out]
    g_query, g_key, g_value, grad_states, *own_middle = self_backward(
        q_self, k_self, v_self, grad_mixed, mixed_self, lse_self, starts, states, first, grad_resid_one, scale,
        give([*g_cross, g_self_out], 1), 6
    )
    g_self = [g_query, g_key, g_value]
    grads_vec = jnp.concatenate([sums_one[:2], sums_two[:2], sums_three[:2], jnp.zeros((2, width), f32)])
    if small:
        own_self, own_vec = hosted(None, n + 3, [], [], [], [], [], "scatter_last", give(g_self, 1, vec=grads_vec), 7)
        own_contract, own_expand, own_middle = own_contract[0], own_expand[0], own_middle[0]
    else:
        total = lambda g: lax.psum(lax.psum_scatter(g, "shard", scatter_dimension=1, tiled=True), "rep")
        own_self = total(jnp.stack(g_self))
        own_middle = total(jnp.stack([*g_cross, g_self_out]))
        own_expand = total(g_expand)
        own_contract = total(g_contract.reshape(1, -1, width))
        own_vec = lax.dynamic_slice_in_dim(
            lax.psum(grads_vec, ("rep", "shard")), lax.axis_index("shard") * rows, rows, 1
        )
    own_contract = own_contract.reshape(blocks * rows, width).astype(f32)
    own_expand = jnp.concatenate([own_expand[j] for j in range(blocks)], 1).astype(f32)
    attention = [own_self[0], own_self[1], own_self[2], own_middle[4]] + [own_middle[j] for j in range(4)]
    return (
        final,
        grad_states,
        grad_encoded,
        *[g.astype(f32) for g in attention],
        own_expand,
        own_contract,
        *[own_vec[i] for i in range(6)],
    )


def solution(mesh):
    many, few = P(("rep", "shard"), None), P("shard", None)
    return jax.shard_map(
        functools.partial(body, mesh.shape["shard"]),
        mesh=mesh,
        in_specs=(many,) * 4 + (few,) * 10 + (P("shard"),) * 6,
        out_specs=(many,) * 3 + (few,) * 10 + (P("shard"),) * 6,
        check_vma=False,
    )
```

```python
import functools

import jax
import jax.numpy as jnp
from jax import lax
from jax.experimental import pallas as pl
from jax.experimental.pallas import tpu as pltpu
from jax.sharding import PartitionSpec as P

HD = 64
PIC = 256
EPS = 1e-05
NEGATIVE = -1e30
INV_ROOT_TWO = 0.7071067811865476
INV_ROOT_TWO_PI = 0.3989422804014327
MESH = pl.DeviceIdType.MESH
MIB = 1 << 20
HBM = pl.BlockSpec(memory_space=pltpu.HBM)
bf16 = jnp.bfloat16
f32 = jnp.float32


def dot(a, b, ca=1, cb=0):
    return lax.dot_general(a, b, (((ca,), (cb,)), ((), ())), preferred_element_type=f32)


def place(n):
    half = n // 2

    def shard_at(pos):
        pos = lax.rem(pos + 2 * n, n)
        back = pos // half
        return (1 - back) * 2 * pos + back * (2 * (n - 1 - pos) + 1)

    s = lax.axis_index("shard")
    odd = s % 2
    pos = (1 - odd) * (s // 2) + odd * (n - 1 - s // 2)
    return pos, shard_at


def greet(partners):
    barrier = pltpu.get_barrier_semaphore()
    for who in partners:
        pl.semaphore_signal(barrier, inc=1, device_id=who, device_id_type=MESH)
    pl.semaphore_wait(barrier, len(partners))


def send(src, dst, ssem, rsem, who):
    copy = pltpu.make_async_remote_copy(
        src_ref=src, dst_ref=dst, send_sem=ssem, recv_sem=rsem, device_id=who, device_id_type=MESH
    )
    copy.start()
    return copy


def load(src, dst, sem):
    copy = pltpu.make_async_copy(src, dst, sem)
    copy.start()
    return copy


def neighbours(n):
    rep, shard = lax.axis_index("rep"), lax.axis_index("shard")
    x, c = rep // 2, rep % 2
    pos, shard_at = place(n)
    ways = (((rep, shard_at(pos + 1)), 1), ((rep, shard_at(pos - 1)), -1))
    sibling, across, corner = (x * 2 + 1 - c, shard), ((1 - x) * 2 + c, shard), ((1 - x) * 2 + 1 - c, shard)
    return x, c, shard, pos, shard_at, ways, sibling, across, corner


def remote(src, dst, ssem, rsem, who):
    return pltpu.make_async_remote_copy(
        src_ref=src, dst_ref=dst, send_sem=ssem, recv_sem=rsem, device_id=who, device_id_type=MESH
    )


def block_of(index, size):
    return pl.ds(pl.multiple_of(index * size, size), size)


class Gather:
    def __init__(self, n, width, shards, units, alone, owner_first=False, vec=None):
        self.n, self.shards, self.owner_first, self.vec, self.follows = n, shards, owner_first, vec, False
        self.units, self.ne, self.ns = units, alone, units - 2 * alone
        self.rows, self.width = sum(s.size for s in shards) // (units * width), width
        self.arrays = list(shards) + ([] if vec is None else [vec])
        shape = (n, units, self.rows, self.width) if owner_first else (units, n * self.rows, self.width)
        self.out_shapes = [jax.ShapeDtypeStruct(shape, bf16)]
        dma = pltpu.SemaphoreType.DMA
        self.scratch = [pltpu.VMEM((units, self.rows, width), bf16), dma((2,)), dma((6, 2)), dma((3, 2))]
        self.scratch += [dma((2, n - 1))] * 3
        if vec is not None:
            self.out_shapes.append(jax.ShapeDtypeStruct((n,) + vec.shape, vec.dtype))
            self.scratch += [dma((1,)), dma((n - 1,)), dma((n - 1,))]

    def bind(self, ins, outs, scratch):
        self.ins, self.full = ins, outs[0]
        self.own, self.local, self.sent, self.got, *self.came = scratch[:7]
        if self.vec is not None:
            self.vec_in, self.vecs, self.vec_sems = ins[-1], outs[1], scratch[7:]
            self.ins = ins[:-1]
        (self.x, self.c, self.shard, self.pos, self.shard_at, self.ways, self.sibling, self.across, _) = neighbours(self.n)
        on_ring = self.ne + self.ns
        self.mine = pl.ds(self.x * on_ring, self.ne)
        self.sets = (self.mine, pl.ds(self.ne, self.ns))
        self.theirs = pl.ds((1 - self.x) * on_ring, self.ne)

    def at(self, units, owner):
        if self.owner_first:
            return self.full.at[owner, units]
        return self.full.at[units, block_of(owner, self.rows), :]

    def spot(self, units, d, k):
        owner = self.shard_at(self.pos - self.ways[d][1] * k)
        quarter = self.rows // 4
        if self.owner_first:
            return self.full.at[owner, units, block_of(self.c * 2 + d, quarter), :]
        return self.full.at[units, block_of(owner * 4 + self.c * 2 + d, quarter), :]

    def moved(self, kind, units, d, k, hop, who):
        here = self.spot(units, d, k)
        came = self.came[kind].at[d, hop] if kind < 3 else self.got.at[kind - 3, d]
        return remote(here, here, self.sent.at[kind, d], came, who)

    def every(self, units, sem):
        size = self.rows // 4
        if self.owner_first:
            hops = self.full.at[pl.ds(0, self.n - 1), units, pl.ds(0, size), :]
        else:
            hops = self.full.at[units, pl.ds(0, (self.n - 1) * size), :]
        pltpu.make_async_copy(hops, hops, sem).wait()

    def first(self, e, d):
        src = self.own.at[self.sets[e], block_of(self.c * 2 + d, self.rows // 4), :]
        return remote(src, self.spot(self.sets[e], d, 0), self.sent.at[e, d], self.came[e].at[d, 0], self.ways[d][0])

    def stored(self):
        return pltpu.make_async_copy(self.own, self.at(pl.ds(0, self.units), self.shard), self.local.at[1])

    def ring(self, e, d, k):
        return self.moved(e, self.sets[e], d, k, k, self.ways[d][0])

    def side(self, e, d, k):
        return self.moved(3 + e, self.sets[e], d, k + 1, k, self.sibling)

    def cross(self, d, k):
        return self.moved(2, self.mine, d, k + 1, k, self.across)

    def forward(self, d, k):
        return self.moved(5, self.theirs, d, k + 1, k, self.sibling)

    def vec_hop(self, k):
        here = self.vecs.at[self.shard_at(self.pos - k)]
        return remote(here, here, self.vec_sems[1].at[k], self.vec_sems[2].at[k], self.ways[0][0])

    def begin(self):
        per = self.units // len(self.ins)
        for i, ref in enumerate(self.ins):
            for j in range(per):
                if ref.shape[1] > self.width:
                    part = ref.at[:, pl.ds(j * self.width, self.width)]
                else:
                    part = ref.at[pl.ds(j * self.rows, self.rows), :]
                pltpu.make_async_copy(part, self.own.at[i * per + j], self.local.at[0]).start()
        if self.vec is not None:
            pltpu.make_async_copy(self.vec_in, self.vecs.at[self.shard], self.vec_sems[0].at[0]).start()
        if not self.follows:
            greet((self.ways[0][0], self.ways[1][0], self.sibling, self.across))
        pltpu.make_async_copy(self.own, self.own, self.local.at[0]).wait()
        for e in range(2):
            for d in range(2):
                self.first(e, d).start()
        self.stored().start()
        if self.vec is not None:
            pltpu.make_async_copy(self.vec_in, self.vecs.at[self.shard], self.vec_sems[0].at[0]).wait()

    def step(self, i):
        n = self.n
        pl.when(i == 0)(self.begin)

        for e in range(2):
            for d in range(2):

                @pl.when((i > 0) & (i < n))
                def _():
                    self.ring(e, d, i - 1).wait_recv()

                    @pl.when(i < n - 1)
                    def _():
                        self.ring(e, d, i).start()

                    if e == 0:
                        self.cross(d, i - 1).start()
                    self.side(e, d, i - 1).start()

        @pl.when((i > 1) & (i <= n))
        def _():
            for d in range(2):
                self.cross(d, i - 2).wait_recv()
                self.forward(d, i - 2).start()

        if self.vec is not None:
            @pl.when((i > 0) & (i < n))
            def _():
                self.vec_hop(i - 1).wait_recv()

            @pl.when(i < n - 1)
            def _():
                self.vec_hop(i).start()

    def finish(self, steps):
        n = self.n
        if steps <= n:
            for d in range(2):
                self.cross(d, n - 2).wait_recv()
                self.forward(d, n - 2).start()

        for d in range(2):
            for kind, units in enumerate((*self.sets, self.mine, *self.sets, self.theirs)):
                self.every(units, self.sent.at[kind, d])
                if kind > 2:
                    self.every(units, self.got.at[kind - 3, d])
        if self.vec is not None:
            lax.fori_loop(0, n - 1, lambda k, _: (self.vec_hop(k).wait_send(), 0)[1], 0)
        self.stored().wait()


class Chain:
    def __init__(self, first, second):
        self.first, self.second, self.n = first, second, first.n
        second.follows = True
        self.arrays = first.arrays + second.arrays
        self.out_shapes = first.out_shapes + second.out_shapes
        self.scratch = first.scratch + second.scratch

    def bind(self, ins, outs, scratch):
        a, b, c = len(self.first.arrays), len(self.first.out_shapes), len(self.first.scratch)
        self.first.bind(ins[:a], outs[:b], scratch[:c])
        self.second.bind(ins[a:], outs[b:], scratch[c:])

    def step(self, t):
        self.first.step(t)
        pl.when(t == self.n)(lambda: self.first.finish(self.n + 1))
        self.second.step(t - (self.n - 2))

    def finish(self, ticks):
        self.second.finish(ticks - (self.n - 2))


class Scatter:
    def __init__(self, n, sources, alone, vec=None, start=1, every=1):
        self.n, self.arrays = n, list(sources) + ([] if vec is None else [vec])
        self.vec, self.start, self.every = vec, start, every
        self.counts = [1 if s.ndim == 2 else s.shape[s.ndim - 3] for s in sources]
        self.kinds = [s.ndim for s in sources]
        units = self.units = sum(self.counts)
        self.ne, self.ns = alone, units - 2 * alone
        first = sources[0].shape
        rows = self.rows = first[-2] if len(first) == 4 else first[-2] // n
        width = self.width = sources[0].shape[-1]
        half, self.quarter = rows // 2, rows // 4
        self.out_shapes = [jax.ShapeDtypeStruct((units, rows, width), bf16)]
        dma = pltpu.SemaphoreType.DMA
        self.scratch = [
            pltpu.VMEM((units, n * half, width), bf16),
            pltpu.VMEM((units, n * half, width), bf16),
            pltpu.VMEM((alone, n * half, width), bf16),
            pltpu.VMEM((2, n - 1, alone, half // 2, width), bf16),
            pltpu.VMEM((2, n - 1, self.ns, half // 2, width), bf16),
            pltpu.VMEM((self.ns, half, width), bf16),
            pltpu.VMEM((alone, half, width), bf16),
            dma((2, n)), dma((2,)), dma((2, n)), dma((2,)), dma((2, n)),
            dma((2,)), dma((2, n - 1)), dma((2,)), dma((2, n - 1)),
            dma((2,)), dma((2,)), dma((3,)), dma((3,)), dma((3,)),
        ]
        if vec is not None:
            self.out_shapes.append(jax.ShapeDtypeStruct((8, rows), f32))
            self.scratch += [
                pltpu.VMEM((n, 8, rows), f32), pltpu.VMEM((n - 1, 8, rows), f32), pltpu.VMEM((4, 8, rows), f32),
                pltpu.VMEM((8, rows), f32), dma((2,)), dma((n - 1,)), dma((n - 1,)), dma((3,)), dma((3,)),
            ]

    def bind(self, ins, outs, scratch):
        self.ins, self.out = ins, outs[0]
        (self.near, self.beside, self.over, slots_e, slots_s, self.swap_s, self.swap_e, self.local, self.cs, self.cr,
         self.xs, self.xr, *ring_sems, self.ss, self.sr, self.os, self.orr, self.done) = scratch[:21]
        self.slots, self.ring_sems = (slots_e, slots_s), (ring_sems[:2], ring_sems[2:])
        if self.vec is not None:
            self.vec_in, self.vec_out, self.ins = ins[-1], outs[1], ins[:-1]
            (self.v_near, self.v_ring, self.v_all, self.v_sum, self.v_local, self.v_rs, self.v_rr,
             self.v_ss, self.v_sr) = scratch[21:]
        (self.x, self.c, self.shard, self.pos, self.shard_at, self.ways, self.sibling, self.across,
         self.corner) = neighbours(self.n)
        self.on_ring = self.ne + self.ns
        self.theirs = pl.ds((1 - self.x) * self.on_ring, self.ne)
        self.mine = pl.ds(self.x * self.on_ring, self.ne)
        self.shared = pl.ds(self.ne, self.ns)
        self.sets = (self.mine, self.shared)

    def owner(self, d, k):
        return self.shard_at(self.pos - self.ways[d][1] * (1 + k))

    def span(self, d, k):
        return block_of(self.owner(d, k) * 2 + d, self.quarter)

    def region(self, ref, d, k):
        return ref.at[:, self.span(d, k), :]

    def pieces(self, d, k, core, target):
        owner = self.owner(d, k)
        u = 0
        for ref, count, kind in zip(self.ins, self.counts, self.kinds):
            rows = block_of(owner * 4 + core * 2 + d, self.quarter)
            if kind == 4:
                src = ref.at[owner, :, block_of(core * 2 + d, self.quarter), :]
            else:
                src = ref.at[rows, :] if kind == 2 else ref.at[:, rows, :]
            units = u if kind == 2 else pl.ds(u, count)
            yield src, target.at[units, self.span(d, k), :]
            u += count

    def crossing(self, d, k):
        rows = self.span(d, k)
        return remote(
            self.near.at[self.theirs, rows, :], self.over.at[:, rows, :], self.xs.at[d], self.xr.at[d, k], self.across
        )

    def hop(self, e, d, k):
        src = self.near.at[self.sets[e], self.span(d, k), :]
        sent, got = self.ring_sems[e]
        return remote(src, self.slots[e].at[d, k], sent.at[d], got.at[d, k], self.ways[d][0])

    def vec_hop(self, k):
        return remote(self.v_near.at[self.owner(0, k)], self.v_ring.at[k], self.v_rs.at[k], self.v_rr.at[k], self.ways[0][0])

    def begin(self):
        n = self.n

        def loads(k, _):
            for d in range(2):
                for src, dst in self.pieces(d, k, self.c, self.near):
                    pltpu.make_async_copy(src, dst, self.local.at[d, k]).start()
            return 0

        lax.fori_loop(0, n, loads, 0)
        if self.vec is not None:
            for s in range(n):
                pltpu.make_async_copy(
                    self.vec_in.at[:, pl.ds(s * self.rows, self.rows)], self.v_near.at[s], self.v_local.at[0]
                ).start()
        greet((self.ways[0][0], self.ways[1][0], self.sibling, self.across) + (() if self.vec is None else (self.corner,)))

        def sends(k, _):
            for d in range(2):
                for src, dst in self.pieces(d, k, 1 - self.c, self.beside):
                    remote(src, dst, self.cs.at[d], self.cr.at[d, k], self.sibling).start()
            return 0

        lax.fori_loop(0, n, sends, 0)
        if self.vec is not None:
            pltpu.make_async_copy(self.v_near, self.v_near, self.v_local.at[0]).wait()

    def arrived(self, ref, ssem, rsem, d, k):
        here = self.region(ref, d, k)
        return remote(here, here, ssem.at[d], rsem.at[d, k], self.sibling)

    def pair(self, k):
        for d in range(2):
            rows = self.span(d, k)
            here = self.region(self.near, d, k)
            pltpu.make_async_copy(here, here, self.local.at[d, k]).wait()
            self.arrived(self.beside, self.cs, self.cr, d, k).wait_recv()

            def add(u, _):
                self.near[u, rows, :] = self.near[u, rows, :] + self.beside[u, rows, :]
                return 0

            lax.fori_loop(0, self.units, add, 0)
            self.crossing(d, k).start()

    def combine(self, k, later):
        for e in (1, 0):
            for d in range(2):
                rows = self.span(d, k)
                if later:
                    self.hop(e, d, k - 1).wait_recv()
                if e == 0:
                    self.crossing(d, k).wait_recv()

                def add_shared(i, _):
                    u = self.ne + i
                    self.near[u, rows, :] = self.near[u, rows, :] + self.slots[1][d, k - 1, i]
                    return 0

                def add_mine(i, _):
                    u = self.x * self.on_ring + i
                    value = self.near[u, rows, :].astype(f32) + self.over[i, rows, :].astype(f32)
                    if later:
                        value = value + self.slots[0][d, k - 1, i].astype(f32)
                    self.near[u, rows, :] = value.astype(bf16)
                    return 0

                if e == 0:
                    lax.fori_loop(0, self.ne, add_mine, 0)
                elif later:
                    lax.fori_loop(0, self.ns, add_shared, 0)

                @pl.when(k < self.n - 1)
                def _():
                    self.hop(e, d, k).start()

        if self.vec is not None:
            if later:
                self.vec_hop(k - 1).wait_recv()
                self.v_near[self.owner(0, k)] = self.v_near[self.owner(0, k)] + self.v_ring[k - 1]

            @pl.when(k < self.n - 1)
            def _():
                self.vec_hop(k).start()

    def step(self, t):
        n = self.n
        pl.when(t == 0)(self.begin)
        since = t - self.start
        if self.every > 1:
            k, on = (since + n * self.every) // self.every - n, lax.rem(since + n * self.every, self.every) == 0
        else:
            k, on = since, since >= 0

        @pl.when(since == 0)
        def _():
            self.pair(0)
            self.pair(1)
            self.combine(0, False)

        @pl.when(on & (k > 0) & (k < n))
        def _():
            self.combine(k, True)

        @pl.when(on & (k >= 0) & (k + 2 < n))
        def _():
            self.pair(k + 2)

        pl.when(since == (n - 1) * self.every)(self.exchange)
        pl.when(since == (n - 1) * self.every + max(2, self.every))(self.join)

    def swap(self, e):
        src = self.near.at[self.sets[e], block_of(self.shard, self.rows // 2), :]
        return remote(src, (self.swap_e, self.swap_s)[e], self.ss.at[e], self.sr.at[e], self.across)

    def result(self, j, away):
        half = block_of(self.c, self.rows // 2)
        src = (self.near.at[self.mine, block_of(self.shard, self.rows // 2), :], self.swap_s, self.swap_e)[j]
        dst = self.out.at[(self.mine, self.shared, self.theirs)[j], half, :]
        if away:
            return remote(src, dst, self.os.at[j], self.orr.at[j], self.sibling)
        return pltpu.make_async_copy(src, dst, self.done.at[j])

    def shares(self):
        sums, rep = self.v_near.at[self.shard], self.x * 2 + self.c
        return [
            remote(sums, self.v_all.at[rep], self.v_ss.at[j], self.v_sr.at[j], who)
            for j, who in enumerate((self.sibling, self.across, self.corner))
        ]

    def put(self, j):
        self.result(j, True).start()
        self.result(j, False).start()

    def exchange(self):
        self.swap(1).start()
        self.swap(0).start()
        self.put(0)
        if self.vec is not None:
            for copy in self.shares():
                copy.start()
            self.v_all[self.x * 2 + self.c] = self.v_near[self.shard]

    def join(self):
        at = block_of(self.shard, self.rows // 2)
        self.swap(1).wait_recv()

        def add(i, _):
            self.swap_s[i] = self.swap_s[i] + self.near[self.ne + i, at, :]
            return 0

        lax.fori_loop(0, self.ns, add, 0)
        self.put(1)
        self.swap(0).wait_recv()
        self.put(2)

    def finish(self, ticks):
        n = self.n
        last = self.start + (n - 1) * self.every
        assert ticks > last - self.every
        if ticks <= last:
            self.combine(n - 1, True)
            self.exchange()
        if ticks <= last + max(2, self.every):
            self.join()
        if self.vec is not None:
            for copy in self.shares():
                copy.wait()
            self.v_sum[...] = (self.v_all[0] + self.v_all[1]) + (self.v_all[2] + self.v_all[3])
            load(self.v_sum, self.vec_out, self.v_local.at[1]).wait()
        for j in range(3):
            self.result(j, False).wait()
            self.result(j, True).wait()
        for e in range(2):
            self.swap(e).wait_send()

        span = pl.ds(0, n * self.quarter)
        for d in range(2):
            totals = [(self.beside.at[:, span, :], self.cs.at[d]), (self.over.at[:, span, :], self.xs.at[d])]
            totals += [(self.slots[e].at[d], self.ring_sems[e][0].at[d]) for e in range(2)]
            for whole, sem in totals:
                pltpu.make_async_copy(whole, whole, sem).wait()
        if self.vec is not None:
            lax.fori_loop(0, n - 1, lambda k, _: (self.vec_hop(k).wait_send(), 0)[1], 0)


def hosted(
    kernel, steps, args, in_specs, out_shapes, out_specs, scratch, name, carry=None, collective_id=None, done_by=None, ticks=1, vmem=58,
    late=(),
):
    args, in_specs = list(args), list(in_specs)
    stores = []
    for at, _, lead in late:
        in_specs[at] = HBM
        stores.append(pltpu.VMEM(args[at].shape if lead is None else (lead,) + args[at].shape[1:], args[at].dtype))
    scratch = list(scratch) + stores + ([pltpu.SemaphoreType.DMA((len(late),))] if late else [])
    counts = [len(args), len(out_shapes), len(scratch)]
    extra = [0, 0, 0]
    params = dict(vmem_limit_bytes=vmem * MIB)
    if carry is not None:
        extra = [len(carry.arrays), len(carry.out_shapes), len(carry.scratch)]
        params.update(collective_id=collective_id, has_side_effects=True)

    def whole(*refs):
        main, other, first = [], [], 0
        for count, more in zip(counts, extra):
            main += refs[first : first + count]
            other.append(refs[first + count : first + count + more])
            first += count + more
        i = pl.program_id(0)
        copies = []
        if late:
            *main, late_sems = main
            kept = main[len(main) - len(late) :]
            main = main[: len(main) - len(late)]
            for m, (at, _, lead) in enumerate(late):
                src = main[at] if lead is None else main[at].at[pl.ds(0, lead)]
                copies.append(pltpu.make_async_copy(src, kept[m], late_sems.at[m]))
                main[at] = kept[m]

        def tick(j):
            if carry is not None:
                carry.step(i * ticks + j)
            if j == 0 and late:
                pl.when(i == 0)(lambda: [copy.start() for copy in copies] and None)
                for copy, (_, step, _) in zip(copies, late):
                    pl.when(i == step)(copy.wait)

        if carry is not None:
            carry.bind(*other)
        if ticks == 1:
            tick(0)
            if done_by is not None:
                pl.when(i == done_by)(lambda: carry.finish(done_by + 1))
            if kernel is not None:
                kernel(*main)
        else:
            kernel(tick, *main)
        if carry is not None and done_by is None:
            pl.when(i == steps - 1)(lambda: carry.finish(steps * ticks))

    return pl.pallas_call(
        whole,
        grid=(steps,),
        out_shape=list(out_shapes) + (carry.out_shapes if carry else []),
        in_specs=list(in_specs) + [HBM] * extra[0],
        out_specs=list(out_specs) + [HBM] * extra[1],
        scratch_shapes=list(scratch) + (carry.scratch if carry else []),
        compiler_params=pltpu.CompilerParams(**params),
        name=name,
    )(*args, *(carry.arrays if carry else []))


def norm_forward(resid, gain, shift):
    mean = jnp.mean(resid, -1, keepdims=True)
    centred = resid - mean
    variance = jnp.mean(centred * centred, -1, keepdims=True)
    inverse = lax.rsqrt(variance + EPS)
    normed = centred * inverse
    return (normed * gain + shift, normed, inverse)


def norm_backward(grad_out, normed, inverse, gain):
    grad_gain = jnp.sum(grad_out * normed, 0, keepdims=True)
    grad_shift = jnp.sum(grad_out, 0, keepdims=True)
    grad_normed = grad_out * gain
    centre_term = jnp.mean(grad_normed, -1, keepdims=True)
    slope_term = jnp.mean(grad_normed * normed, -1, keepdims=True)
    return (inverse * (grad_normed - centre_term - normed * slope_term), grad_gain, grad_shift)


def fixed(a):
    zeros = (0,) * a.ndim
    return pl.BlockSpec(a.shape, lambda i: zeros, pipeline_mode=pl.Buffered(1))


def slices(rows, count):
    size = rows // count
    return [slice(j * size, (j + 1) * size) for j in range(count)]


def first_lanes(shape):
    return lax.broadcasted_iota(jnp.int32, shape, len(shape) - 1) < HD


def region_bias(starts_ref, region, size, transposed):
    first = region * size
    one = first + lax.broadcasted_iota(jnp.int32, (size, size), 0)
    two = first + lax.broadcasted_iota(jnp.int32, (size, size), 1)
    q_at, k_at = (two, one) if transposed else (one, two)
    start = starts_ref[0, region]
    q_in = (q_at >= start) & (q_at < start + PIC)
    k_in = (k_at >= start) & (k_at < start + PIC)
    return jnp.where((k_at <= q_at) | (q_in & k_in), 0.0, NEGATIVE)


def self_forward_kernel(regions, lead, scale, carry, starts_ref, x_ref, *refs):
    refs = list(refs)
    w_ref = refs.pop(0) if carry is None else carry.first.full
    q_ref, k_ref, v_ref, o_ref, lse_ref, bias_ref, w_buf, sems = refs
    rows, size = x_ref.shape[0], x_ref.shape[0] // regions
    i = pl.program_id(0)
    j = i - lead
    pairs = pl.num_programs(0) - lead

    @pl.when(i == 0)
    def _():
        for r in range(regions):
            bias_ref[r] = region_bias(starts_ref, r, size, False)

    def fetch(pair, slot):
        return pltpu.make_async_copy(w_ref.at[:, :, block_of(pair, 2 * HD)], w_buf.at[slot], sems.at[slot])

    @pl.when(j == 0)
    def _():
        fetch(0, 0).start()

    @pl.when(j >= 0)
    def _():
        slot = lax.rem(i - lead + 2, 2)

        @pl.when(j + 1 < pairs)
        def _():
            fetch(j + 1, 1 - slot).start()

        fetch(j, slot).wait()
        made = dot(x_ref[...], jnp.concatenate([w_buf[slot, u] for u in range(3)], 1))
        q_ref[...] = (made[:, : 2 * HD] * scale).astype(bf16)
        k_ref[...] = made[:, 2 * HD : 4 * HD].astype(bf16)
        v_ref[...] = made[:, 4 * HD :].astype(bf16)
        low = first_lanes((1, 2 * HD))
        outs, lses = [[], []], [[], []]
        for h in range(2):
            keys = jnp.where(low if h == 0 else ~low, k_ref[...], jnp.zeros((), bf16))
            for r in range(regions):
                span = slice(r * size, (r + 1) * size)
                q = q_ref[span, :]
                scores = []
                if r:
                    scores.append((dot(q, keys[: r * size], 1, 1), v_ref[: r * size, :]))
                scores.append((dot(q, keys[span], 1, 1) + bias_ref[r], v_ref[span, :]))
                top = functools.reduce(jnp.maximum, [jnp.max(s, -1, keepdims=True) for s, _ in scores])
                total, mixed = 0.0, 0.0
                for s, v in scores:
                    e = jnp.exp(s - top)
                    total = total + jnp.sum(e, -1, keepdims=True)
                    mixed = mixed + dot(e.astype(bf16), v)
                outs[h].append(mixed / total)
                lses[h].append(top + jnp.log(total))
        for r in range(regions):
            span = slice(r * size, (r + 1) * size)
            o_ref[span, :] = jnp.where(low, outs[0][r], outs[1][r]).astype(bf16)
            turned = jnp.where(low, lses[0][r], lses[1][r]).T
            lse_ref[0, 0:1, span] = turned[0:1]
            lse_ref[0, 1:2, span] = turned[HD : HD + 1]


def self_forward(states, weights, starts, scale, carry, collective_id):
    rows, width = states.shape
    regions = starts.shape[1]
    size = rows // regions
    pairs = width // (2 * HD)
    lead = 0 if carry is None else carry.n
    args, specs = [starts, states], [pl.BlockSpec(memory_space=pltpu.SMEM), fixed(states)]
    if carry is None:
        args.append(weights)
        specs.append(HBM)
    column = pl.BlockSpec((rows, 2 * HD), lambda i: (0, jnp.maximum(i - lead, 0)))
    return hosted(
        functools.partial(self_forward_kernel, regions, lead, scale, carry), lead + pairs, args, specs,
        [jax.ShapeDtypeStruct((rows, width), bf16)] * 4 + [jax.ShapeDtypeStruct((pairs, 8, rows), f32)],
        [column] * 4 + [pl.BlockSpec((1, 8, rows), lambda i: (jnp.maximum(i - lead, 0), 0, 0))],
        [pltpu.VMEM((regions, size, size), f32), pltpu.VMEM((2, 3, width, 2 * HD), bf16), pltpu.SemaphoreType.DMA((2,))],
        "self_forward", carry, collective_id,
    )


def self_backward_kernel(
    regions, scale, pairs, starts_ref, q_ref, k_ref, v_ref, g_ref, o_ref, lse_ref, x_ref, w_ref, resid_ref,
    g_query_ref, g_key_ref, g_value_ref, grad_ref, bias_ref, grads,
):
    rows, width = x_ref.shape
    size = rows // regions
    i = pl.program_id(0)
    spans = slices(rows, regions)
    low = first_lanes((1, 2 * HD))

    @pl.when(i == 0)
    def _():
        for r in range(regions):
            bias_ref[r] = region_bias(starts_ref, r, size, True)

    @pl.when(i < pairs)
    def _():
        product = g_ref[...].astype(f32) * o_ref[...].astype(f32)
        chooser = lax.broadcasted_iota(jnp.int32, (8, 2 * HD), 0)
        chooser = ((chooser == 0) & first_lanes((8, 2 * HD))) | ((chooser == 1) & ~first_lanes((8, 2 * HD)))
        chooser = chooser.astype(f32).astype(bf16)
        upper = product.astype(bf16)
        lower = (product - upper.astype(f32)).astype(bf16)
        deltas = dot(chooser, upper, 1, 1) + dot(chooser, lower, 1, 1)
        gq, gk, gv = {}, {}, {}
        for h in range(2):
            pick = low if h == 0 else ~low
            zero = jnp.zeros((), bf16)
            keys = jnp.where(pick, k_ref[...], zero)
            values = jnp.where(pick, v_ref[...], zero)
            for r, span in enumerate(spans):
                q, g = q_ref[span, :], g_ref[span, :]
                lse = lse_ref[0, h : h + 1, span]
                delta = deltas[h : h + 1, span]
                for j, keyed in enumerate(spans[: r + 1]):
                    scores = dot(keys[keyed], q, 1, 1)
                    if j == r:
                        scores = scores + bias_ref[r]
                    probs = jnp.exp(scores - lse)
                    grad_probs = dot(values[keyed], g, 1, 1)
                    grad_scores = (probs * (grad_probs - delta)).astype(bf16)
                    gv[h, j] = gv.get((h, j), 0.0) + dot(probs.astype(bf16), g)
                    gk[h, j] = gk.get((h, j), 0.0) + dot(grad_scores, q)
                    gq[h, r] = gq.get((h, r), 0.0) + dot(grad_scores, k_ref[keyed, :], 0, 0)
        cols = block_of(i, 2 * HD)
        for r, span in enumerate(spans):
            grads[0, span, cols] = jnp.where(low, gq[0, r], gq[1, r]).astype(bf16) * scale
            grads[1, span, cols] = jnp.where(low, gk[0, r], gk[1, r]).astype(bf16)
            grads[2, span, cols] = jnp.where(low, gv[0, r], gv[1, r]).astype(bf16)

    for u, out in enumerate((g_query_ref, g_key_ref, g_value_ref)):

        @pl.when(i == pairs + u)
        def _():
            for span in slices(width, 4):
                out[span, :] = dot(x_ref[:, span], grads[u], 0, 0).astype(bf16)

    @pl.when(i >= pairs + 3)
    def _():
        at = block_of(i - pairs - 3, grad_ref.shape[0])
        total = resid_ref[...]
        for u in range(3):
            total = total + dot(grads[u, at, :], w_ref[u], 1, 1)
        grad_ref[...] = total


def self_backward(q, k, v, g, o, lse, starts, states, weights, resid, scale, carry, collective_id):
    rows, width = q.shape
    regions = starts.shape[1]
    size = rows // regions
    pairs, parts = width // (2 * HD), 4
    last = pairs - 1
    column = pl.BlockSpec((rows, 2 * HD), lambda i: (0, jnp.minimum(i, last)))
    some = pl.BlockSpec((rows // parts, width), lambda i: (jnp.maximum(i - pairs - 3, 0), 0))
    square = jax.ShapeDtypeStruct((width, width), bf16)
    return hosted(
        functools.partial(self_backward_kernel, regions, scale, pairs), pairs + 3 + parts,
        [starts, q, k, v, g, o, lse, states, weights, resid],
        [pl.BlockSpec(memory_space=pltpu.SMEM)] + [column] * 5
        + [pl.BlockSpec((1, 8, rows), lambda i: (jnp.minimum(i, last), 0, 0)), fixed(states), fixed(weights), some],
        [square] * 3 + [jax.ShapeDtypeStruct((rows, width), f32)], [fixed(square)] * 3 + [some],
        [pltpu.VMEM((regions, size, size), f32), pltpu.VMEM((3, rows, width), bf16)],
        "self_backward", carry, collective_id, vmem=60, late=((7, pairs, None), (8, pairs + 3, None)),
    )


def cross_forward_kernel(
    scale, tick, x_ref, mixed_in, enc_ref, w_ref, vec_ref, low_ref, n1_ref, i1_ref, q_ref, k_ref, v_ref, mixed_ref,
    lse_ref, two_ref, n2_ref, i2_ref, low_two_ref,
):
    tick(0)

    @pl.when(pl.program_id(0) == 0)
    def _():
        k_ref[...] = dot(enc_ref[...], w_ref[2]).astype(bf16)
        v_ref[...] = dot(enc_ref[...], w_ref[3]).astype(bf16)

    one, n1_ref[...], i1_ref[...] = norm_forward(
        x_ref[...].astype(f32) + dot(mixed_in[...], w_ref[0]), vec_ref[0:1, :], vec_ref[1:2, :]
    )
    low_ref[...] = one.astype(bf16)
    q_ref[...] = (dot(low_ref[...], w_ref[1]) * scale).astype(bf16)
    rows, width = x_ref.shape
    low = first_lanes((1, 2 * HD))
    lane = lax.broadcasted_iota(jnp.int32, (1, 2 * HD), 1)
    lses = jnp.zeros((rows, 2 * HD), f32)
    for pair in range(width // (2 * HD)):
        if pair == 2:
            tick(1)
        cols = slice(pair * 2 * HD, (pair + 1) * 2 * HD)
        parts = []
        for h in range(2):
            keys = jnp.where(low if h == 0 else ~low, k_ref[:, cols], jnp.zeros((), bf16))
            scores = dot(q_ref[:, cols], keys, 1, 1)
            top = jnp.max(scores, -1, keepdims=True)
            e = jnp.exp(scores - top)
            total = jnp.sum(e, -1, keepdims=True)
            parts.append(dot(e.astype(bf16), v_ref[:, cols]) / total)
            lses = jnp.where(lane == 8 * pair + h, top + jnp.log(total), lses)
        mixed_ref[:, cols] = jnp.where(low, *parts).astype(bf16)
    lse_ref[...] = lses.T[: lse_ref.shape[0]]
    two, n2_ref[...], i2_ref[...] = norm_forward(one + dot(mixed_ref[...], w_ref[4]), vec_ref[2:3, :], vec_ref[3:4, :])
    two_ref[...] = two
    low_two_ref[...] = two.astype(bf16)


def cross_forward(states, mixed, encoded, weights, vecs, scale, carry, collective_id):
    rows, width = states.shape
    steps = 4
    block = pl.BlockSpec((rows // steps, width), lambda i: (i, 0))
    thin = pl.BlockSpec((rows // steps, 1), lambda i: (i, 0))
    heads = width // HD * 4
    tall = lambda kind: jax.ShapeDtypeStruct((rows, width), kind)
    column = jax.ShapeDtypeStruct((rows, 1), f32)
    outs = [
        (tall(bf16), block), (tall(f32), block), (column, thin), (tall(bf16), block), (encoded, fixed(encoded)),
        (encoded, fixed(encoded)), (tall(bf16), block),
        (jax.ShapeDtypeStruct((heads, rows), f32), pl.BlockSpec((heads, rows // steps), lambda i: (0, i))),
        (tall(f32), block), (tall(f32), block), (column, thin), (tall(bf16), block),
    ]
    return hosted(
        functools.partial(cross_forward_kernel, scale), steps, [states, mixed, encoded, weights, vecs],
        [block, block, fixed(encoded), fixed(weights), fixed(vecs)],
        [jax.ShapeDtypeStruct(o.shape, o.dtype) for o, _ in outs], [spec for _, spec in outs], [],
        "cross_forward", carry, collective_id, ticks=2,
    )


def cross_backward_kernel(
    scale, pairs, parts, b2_ref, mixed_ref, low_ref, mixed_one_ref, q_ref, lse_ref, k_ref, v_ref, w_ref, vec_ref, g2_ref,
    n1_ref, i1_ref, w_out_ref, enc_ref, g_out_ref, g_query_ref, g_self_out_ref, g_key_ref, g_value_ref, g1_ref, gm_ref,
    sums_ref, g_enc_ref, g_mixed, gq_all, b1_all, gk_all, gv_all,
):
    i = pl.program_id(0)
    rows, width = b2_ref.shape

    @pl.when(i == 0)
    def _():
        for span in slices(rows, 4):
            g_mixed[span, :] = dot(b2_ref[span, :], w_out_ref[0], 1, 1).astype(bf16)
        sums_ref[...] = jnp.zeros_like(sums_ref)

    j = i - 1

    @pl.when((j >= 0) & (j < pairs))
    def _():
        cols = block_of(j, 2 * HD)
        low = first_lanes((1, 2 * HD))
        chooser = lax.broadcasted_iota(jnp.int32, (8, 2 * HD), 0)
        chooser = ((chooser == 0) & first_lanes((8, 2 * HD))) | ((chooser == 1) & ~first_lanes((8, 2 * HD)))
        chooser = chooser.astype(f32).astype(bf16)
        gks, gvs = [0.0, 0.0], [0.0, 0.0]
        for span in slices(rows, 2):
            g, q = g_mixed[span, cols], q_ref[span, :]
            product = g.astype(f32) * mixed_ref[span, cols].astype(f32)
            upper = product.astype(bf16)
            lower = (product - upper.astype(f32)).astype(bf16)
            deltas = dot(chooser, upper, 1, 1) + dot(chooser, lower, 1, 1)
            gqs = []
            for h in range(2):
                pick = low if h == 0 else ~low
                keys = jnp.where(pick, k_ref[...], jnp.zeros((), bf16))
                values = jnp.where(pick, v_ref[...], jnp.zeros((), bf16))
                probs = jnp.exp(dot(keys, q, 1, 1) - lse_ref[h : h + 1, span])
                grad_scores = (probs * (dot(values, g, 1, 1) - deltas[h : h + 1, :])).astype(bf16)
                gvs[h] = gvs[h] + dot(probs.astype(bf16), g)
                gks[h] = gks[h] + dot(grad_scores, q)
                gqs.append(dot(grad_scores, k_ref[...], 0, 0))
            gq_all[span, cols] = jnp.where(low, *gqs).astype(bf16) * scale
        gk_all[:, cols] = jnp.where(low, *gks).astype(bf16)
        gv_all[:, cols] = jnp.where(low, *gvs).astype(bf16)

    m = j - pairs

    @pl.when((m >= 0) & (m < parts))
    def _():
        at = block_of(m, rows // parts)
        grad_one = g2_ref[...] + dot(gq_all[at, :], w_ref[1], 1, 1)
        grad, g_gain, g_shift = norm_backward(grad_one, n1_ref[...], i1_ref[...], vec_ref[0:1, :])
        sums_ref[0:1, :] += g_gain
        sums_ref[1:2, :] += g_shift
        g1_ref[...] = grad
        b1_all[at, :] = grad.astype(bf16)
        gm_ref[...] = dot(b1_all[at, :], w_ref[0], 1, 1).astype(bf16)

    for u, (left, right, out) in enumerate(
        ((mixed_ref, b2_ref, g_out_ref), (low_ref, gq_all, g_query_ref), (mixed_one_ref, b1_all, g_self_out_ref))
    ):

        @pl.when(m == parts + u)
        def _():
            for span in slices(width, 4):
                out[span, :] = dot(left[:, span], right[...], 0, 0).astype(bf16)

    @pl.when(m == parts + 3)
    def _():
        for span in slices(width, 2):
            g_key_ref[span, :] = dot(enc_ref[:, span], gk_all[...], 0, 0).astype(bf16)
            g_value_ref[span, :] = dot(enc_ref[:, span], gv_all[...], 0, 0).astype(bf16)
        g_enc_ref[...] = dot(gk_all[...], w_ref[2], 1, 1) + dot(gv_all[...], w_ref[3], 1, 1)


def cross_backward(
    branch, mixed, low, mixed_one, grad, normed, inverse, q, lse, k, v, weights, vecs, encoded, scale, carry, collective_id
):
    rows, width = q.shape
    pairs, parts = width // (2 * HD), 4
    column = lambda a: pl.BlockSpec((a.shape[0], 2 * HD), lambda i: (0, jnp.clip(i - 1, 0, pairs - 1)))
    some = lambda cols: pl.BlockSpec((rows // parts, cols), lambda i: (jnp.clip(i - 1 - pairs, 0, parts - 1), 0))
    square = jax.ShapeDtypeStruct((width, width), bf16)
    outs = [
        *[(square, fixed(square))] * 5, (grad, some(width)), (q, some(width)), (vecs, fixed(vecs)),
        (jax.ShapeDtypeStruct(k.shape, f32), fixed(k)),
    ]
    args = [branch, mixed, low, mixed_one, q, lse, k, v, weights, vecs, grad, normed, inverse, weights, encoded]
    out_weight = pl.BlockSpec((1, width, width), lambda i: (4, 0, 0), pipeline_mode=pl.Buffered(1))
    lse_spec = pl.BlockSpec((8, rows), lambda i: (jnp.clip(i - 1, 0, pairs - 1), 0))
    return hosted(
        functools.partial(cross_backward_kernel, scale, pairs, parts), 1 + pairs + parts + 4, args,
        [fixed(a) for a in args[:4]] + [column(q), lse_spec, column(k), column(v), fixed(weights), fixed(vecs)]
        + [some(width), some(width), some(1), out_weight, HBM],
        [jax.ShapeDtypeStruct(o.shape, o.dtype) for o, _ in outs], [spec for _, spec in outs],
        [pltpu.VMEM((rows, width), bf16)] * 3 + [pltpu.VMEM(k.shape, bf16)] * 2, "cross_backward", carry, collective_id, vmem=62,
        late=((2, 1 + pairs, None), (3, 1 + pairs, None), (8, 1 + pairs, 4), (14, 1 + pairs, None)),
    )


def ffn_forward_kernel(blocks, carry, low_ref, two_ref, cot_ref, vec_ref, w1_ref, *refs):
    refs = list(refs)
    w2_ref = refs.pop(0) if carry is None else carry.full
    final_ref, branch_ref, grad_ref, slope_ref, g_contract_ref, sums_ref, acts, acc, w2_buf, sems = refs
    i = pl.program_id(0)
    spans = slices(low_ref.shape[0], 4)

    @pl.when(i < blocks)
    def _():
        for span in spans:
            pre = dot(low_ref[span, :], w1_ref[0])
            phi = 0.5 * (1.0 + lax.erf(pre * INV_ROOT_TWO))
            acts[i, span, :] = (pre * phi).astype(bf16)
            slope_ref[span, :] = (phi + pre * jnp.exp(-0.5 * pre * pre) * INV_ROOT_TWO_PI).astype(bf16)

    j = i - blocks

    def fetch(block, slot):
        return pltpu.make_async_copy(w2_ref.at[pl.ds(block * 2, 2)], w2_buf.at[slot], sems.at[slot])

    half = blocks // 2

    @pl.when(j == 0)
    def _():
        fetch(0, 0).start()
        acc[...] = two_ref[...]

    @pl.when((j >= 0) & (j < half))
    def _():
        slot = lax.rem(j + blocks * 2, 2)

        @pl.when(j + 1 < half)
        def _():
            fetch(j + 1, 1 - slot).start()

        fetch(j, slot).wait()
        w2 = [w2_buf[slot, m].reshape(-1, w2_buf.shape[-1]) for m in range(2)]
        for span in spans:
            acc[span, :] += dot(acts[2 * j, span, :], w2[0]) + dot(acts[2 * j + 1, span, :], w2[1])

    @pl.when(j == half - 1)
    def _():
        gain, shift = vec_ref[4:5, :], vec_ref[5:6, :]
        sums = [0.0, 0.0]
        for span in slices(low_ref.shape[0], 8):
            final, normed, inverse = norm_forward(acc[span, :], gain, shift)
            final_ref[span, :] = final.astype(bf16)
            grad, *parts = norm_backward(cot_ref[span, :].astype(f32), normed, inverse, gain)
            grad_ref[span, :] = grad
            branch_ref[span, :] = grad.astype(bf16)
            sums = [a + b for a, b in zip(sums, parts)]
        sums_ref[...] = jnp.zeros_like(sums_ref)
        sums_ref[4:5, :] = sums[0]
        sums_ref[5:6, :] = sums[1]

    @pl.when(j >= half)
    def _():
        made = dot(acts[j - half], branch_ref[...], 0, 0).astype(bf16)
        g_contract_ref[0] = made.reshape(g_contract_ref.shape[1:])


def ffn_forward(low, two, cotangent, vecs, w1, w2, carry, collective_id):
    rows, width = low.shape
    if carry is not None:
        blocks, size = carry.n, carry.units * carry.rows
    else:
        blocks, size = w2.shape[0], w2.shape[1] * w2.shape[2]
    per = width // size
    last = blocks - 1
    args = [low, two, cotangent, vecs, w1]
    specs = [fixed(a) for a in args[:4]]
    specs.append(pl.BlockSpec((1, width, size), lambda i: (jnp.minimum(i, last) // per, 0, lax.rem(jnp.minimum(i, last), per))))
    if carry is None:
        args.append(w2)
        specs.append(HBM)
    tall = jax.ShapeDtypeStruct((rows, blocks * size), bf16)
    part = w2.shape[1:] if carry is None else (carry.units, carry.rows, width)
    outs = [low, low, two, tall, jax.ShapeDtypeStruct((blocks,) + part, bf16), jax.ShapeDtypeStruct((8, width), f32)]
    out_specs = [fixed(a) for a in outs[:3]]
    out_specs.append(pl.BlockSpec((rows, size), lambda i: (0, jnp.minimum(i, last))))
    out_specs.append(pl.BlockSpec((1,) + part, lambda i: (jnp.maximum(i - blocks - blocks // 2, 0), 0, 0, 0)))
    out_specs.append(fixed(outs[5]))
    return hosted(
        functools.partial(ffn_forward_kernel, blocks, carry), 2 * blocks + blocks // 2, args, specs,
        [jax.ShapeDtypeStruct(a.shape, a.dtype) for a in outs], out_specs,
        [
            pltpu.VMEM((blocks, rows, size), bf16), pltpu.VMEM((rows, width), f32),
            pltpu.VMEM((2, 2) + part, bf16), pltpu.SemaphoreType.DMA((2,)),
        ],
        "ffn_forward", carry, collective_id, done_by=blocks if carry else None, vmem=60,
        late=((1, blocks, None), (2, blocks + blocks // 2 - 1, None)),
    )


def ffn_backward_kernel(
    blocks, low_ref, branch_ref, vec_ref, w1_ref, w2_ref, slope_ref, normed_ref, inverse_ref, g_ref,
    g_expand_ref, grad_ref, branch_two_ref, sums_ref, turned, acc, g_pre, sem,
):
    i = pl.program_id(0)
    rows = low_ref.shape[0]
    spans = slices(rows, 4)
    start = pltpu.make_async_copy(g_ref, acc, sem.at[0])

    @pl.when(i == 0)
    def _():
        start.start()
        turned[...] = low_ref[...].T
        sums_ref[...] = jnp.zeros_like(sums_ref)

    @pl.when(i < blocks)
    def _():
        w2 = w2_ref[0].reshape(-1, w2_ref.shape[-1])
        for span in spans:
            g_pre[span, :] = (dot(branch_ref[span, :], w2, 1, 1) * slope_ref[span, :].astype(f32)).astype(bf16)
        for span in slices(turned.shape[0], 4):
            g_expand_ref[0, span, :] = dot(turned[span, :], g_pre[...]).astype(bf16)
        pl.when(i == 0)(start.wait)
        for span in spans:
            acc[span, :] += dot(g_pre[span, :], w1_ref[0], 1, 1)

    @pl.when(i >= blocks)
    def _():
        at = block_of(i - blocks, grad_ref.shape[0])
        grad, g_gain, g_shift = norm_backward(acc[at, :], normed_ref[...], inverse_ref[...], vec_ref[2:3, :])
        grad_ref[...] = grad
        branch_two_ref[...] = grad.astype(bf16)
        sums_ref[2:3, :] += g_gain
        sums_ref[3:4, :] += g_shift


def ffn_backward(low, branch, grad, normed, inverse, vecs, w1, w2, slope, carry, collective_id):
    rows, width = low.shape
    blocks, size = w2.shape[0], w2.shape[1] * w2.shape[2]
    per, last, parts = width // size, w2.shape[0] - 1, 4
    wide = pl.BlockSpec((1, width, size), lambda i: (jnp.minimum(i, last) // per, 0, lax.rem(jnp.minimum(i, last), per)))
    deep = pl.BlockSpec((1,) + w2.shape[1:], lambda i: (jnp.minimum(i, last), 0, 0, 0))
    column = pl.BlockSpec((rows, size), lambda i: (0, jnp.minimum(i, last)))
    some = lambda cols: pl.BlockSpec((rows // parts, cols), lambda i: (jnp.maximum(i - blocks, 0), 0))
    args = [low, branch, vecs, w1, w2, slope, normed, inverse, grad]
    outs = [w1, grad, low, vecs]
    return hosted(
        functools.partial(ffn_backward_kernel, blocks), blocks + parts, args,
        [fixed(a) for a in args[:3]] + [wide, deep, column, some(width), some(1), HBM],
        [jax.ShapeDtypeStruct(a.shape, a.dtype) for a in outs], [wide, some(width), some(width), fixed(vecs)],
        [
            pltpu.VMEM((width, rows), bf16), pltpu.VMEM((rows, width), f32), pltpu.VMEM((rows, size), bf16),
            pltpu.SemaphoreType.DMA((1,)),
        ],
        "ffn_backward", carry, collective_id, vmem=60,
    )


def body(n, states, encoded, starts, cotangent, *weights):
    matrices, vectors = weights[:10], weights[10:]
    expand, contract = matrices[8], matrices[9]
    rows, width = matrices[0].shape
    blocks = contract.shape[0] // rows
    scale = HD ** (-0.5)
    small = n <= 16
    vec = jnp.zeros((16, max(rows, 128)), bf16).at[: len(vectors), :rows].set(jnp.stack(vectors))
    take = lambda shards, units, alone, **more: Gather(n, width, shards, units, alone, **more) if small else None
    if small:
        chain = Chain(take(matrices[:3], 3, 1, vec=vec), take(matrices[3:8], 5, 2))
        q_self, k_self, v_self, mixed_self, lse_self, first, vecs, second = self_forward(states, None, starts, scale, chain, 0)
    else:
        first = lax.all_gather(jnp.stack(matrices[:3]), "shard", axis=1, tiled=True)
        vecs = lax.all_gather(vec, "shard", axis=0)
        second = lax.all_gather(jnp.stack(matrices[3:8]), "shard", axis=1, tiled=True)
        q_self, k_self, v_self, mixed_self, lse_self = self_forward(states, first, starts, scale, None, None)
    vecs = vecs[:, : len(vectors), :rows].transpose(1, 0, 2).reshape(len(vectors), width).astype(f32)
    vecs = jnp.concatenate([vecs, jnp.zeros((2, width), f32)])
    (one_low, normed_one, inverse_one, q_cross, k_cross, v_cross, mixed_cross, lse_cross, hidden_two, normed_two, inverse_two,
     two_low, *third) = cross_forward(states, mixed_self, encoded, second, vecs, scale, take([expand], blocks, 1), 2)
    if not small:
        third = [lax.all_gather(expand.reshape(rows, blocks, width).transpose(1, 0, 2), "shard", axis=1, tiled=True)]
    w1 = third[0]
    w2 = None
    if not small:
        w2 = lax.all_gather(contract, "shard", axis=0, tiled=True).reshape(8, 4, -1, width)
    final, branch_three, grad_three, slope, g_contract, sums_three, *fourth = ffn_forward(
        two_low, hidden_two, cotangent, vecs, w1, w2, take([contract], blocks, 1, owner_first=True), 3
    )
    if small:
        w2 = fourth[0]

    give = lambda sources, alone, **more: Scatter(n, sources, alone, **more) if small else None
    g_expand, grad_resid_two, branch_two, sums_two, *own_contract = ffn_backward(
        two_low, branch_three, grad_three, normed_two, inverse_two, vecs, w1, w2, slope, give([g_contract], 1), 4
    )
    (g_cross_out, g_cross_query, g_self_out, g_cross_key, g_cross_value, grad_resid_one, grad_mixed, sums_one, grad_encoded,
     *own_expand) = cross_backward(
        branch_two, mixed_cross, one_low, mixed_self, grad_resid_two, normed_one, inverse_one, q_cross, lse_cross, k_cross,
        v_cross, second, vecs, encoded, scale, give([g_expand], 1, start=1, every=2), 5
    )
    g_cross = [g_cross_query, g_cross_key, g_cross_value, g_cross_out]
    g_query, g_key, g_value, grad_states, *own_middle = self_backward(
        q_self, k_self, v_self, grad_mixed, mixed_self, lse_self, starts, states, first, grad_resid_one, scale,
        give([*g_cross, g_self_out], 1), 6
    )
    g_self = [g_query, g_key, g_value]
    grads_vec = sums_one + sums_two + sums_three
    if small:
        own_self, own_vec = hosted(None, n + 3, [], [], [], [], [], "scatter_last", give(g_self, 1, vec=grads_vec), 7)
        own_contract, own_expand, own_middle = own_contract[0], own_expand[0], own_middle[0]
    else:
        total = lambda g: lax.psum(lax.psum_scatter(g, "shard", scatter_dimension=1, tiled=True), "rep")
        own_self = total(jnp.stack(g_self))
        own_middle = total(jnp.stack([*g_cross, g_self_out]))
        own_expand = total(g_expand)
        own_contract = total(g_contract.reshape(1, -1, width))
        own_vec = lax.dynamic_slice_in_dim(
            lax.psum(grads_vec, ("rep", "shard")), lax.axis_index("shard") * rows, rows, 1
        )
    own_contract = own_contract.reshape(blocks * rows, width).astype(f32)
    own_expand = jnp.concatenate([own_expand[j] for j in range(blocks)], 1).astype(f32)
    attention = [own_self[0], own_self[1], own_self[2], own_middle[4]] + [own_middle[j] for j in range(4)]
    return (
        final,
        grad_states,
        grad_encoded,
        *[g.astype(f32) for g in attention],
        own_expand,
        own_contract,
        *[own_vec[i] for i in range(6)],
    )


def solution(mesh):
    many, few = P(("rep", "shard"), None), P("shard", None)
    return jax.shard_map(
        functools.partial(body, mesh.shape["shard"]),
        mesh=mesh,
        in_specs=(many,) * 4 + (few,) * 10 + (P("shard"),) * 6,
        out_specs=(many,) * 3 + (few,) * 10 + (P("shard"),) * 6,
        check_vma=False,
    )
```
